128 devices in a mesh: grp: 8 (over z_hi, x), ep: 8 (over y, core), tp: 2 (over z_lo).
Axes of the slice: x: 4, y: 4, z: 4 (z_hi: 2, z_lo: 2; z = z_hi * 2 + z_lo), core: 2. Of those that a mesh axis runs over, the one named last changes fastest.
Arguments:
- residual: bfloat16 [2048, 4096], P(('grp', 'ep'), 'tp'), may hold values from -400 to 400
- queries: bfloat16 [2048, 4096], P(('grp', 'ep'), 'tp'), may hold values from -8 to 8
- token_key_value: bfloat16 [2048, 2, 1024], P(('grp', 'ep'), None, 'tp'), may hold values from -4 to 4
- cache: bfloat16 [2048, 2, 192, 1024], P(('grp', 'ep'), None, None, 'tp'), may hold values from -8 to 8
- cache_length: int32 [2048], P(('grp', 'ep')), may hold values from 2 to 192, as said below
- active: int32 [2048], P(('grp', 'ep')), may hold values from 0 to 1, as said below
- routes: int32 [2048, 2], P(('grp', 'ep')), may hold values from 0 to 7, as said below
- norm_gain: bfloat16 [4096], P('tp'), may hold values from 0.099609375 to 1.8984375
- router: bfloat16 [4096, 8], P('tp'), may hold values from -0.09375 to 0.09375
- w_gate: bfloat16 [8, 4096, 8192], P('ep', ('grp', 'tp')), may hold values from -0.09375 to 0.09375
- w_up: bfloat16 [8, 4096, 8192], P('ep', ('grp', 'tp')), may hold values from -0.09375 to 0.09375
- w_down: bfloat16 [8, 4096, 8192], P('ep', ('grp', 'tp')), may hold values from -0.0625 to 0.0625
Outputs:
- delta: bfloat16 [2048, 4096], P(('grp', 'ep'), 'tp')
The draws below stay inside these ranges and needn't reach their ends.
Inputs may be any that keep to these rules, and one draw needn't show every extreme that they name: `cache_length`: every device's 32 sequences include one with 192 cached positions. The sequences that name their group's common expert first (see routes) all have active = 1. `routes`: each sequence names two different experts; among the sequences of one device no expert is named more than 16 times, and one expert, the same for every device of a grp index, is named first by exactly 16 of each such device's sequences.
All inputs are finite; a program needn't handle non-finite values.
Results may differ from the reference program's by a relative error of at most 0.012.
Values may be sent and summed in bfloat16 or wider, within the bound.
A program may use at most 192 MiB of HBM per device.

```python
import jax
import jax.numpy as jnp
from jax import lax

MODEL_WIDTH = 4096
QUERY_HEADS = 32
KEY_VALUE_HEADS = 8
HEAD_SIZE = 128
FF = 8192
LOCAL_SEQUENCES = 32
MAX_POSITIONS = 192
CAP = 16
EXPERTS = 8
GROUP_SEQS = 256
TOTAL_SEQUENCES = 2048
N_GRP = 8
N_EP = 8


def route_plan(key):
    starting_point = jax.random.fold_in(key, 7)
    block_list = TOTAL_SEQUENCES // LOCAL_SEQUENCES
    row_ids = jnp.arange(TOTAL_SEQUENCES, dtype=jnp.int32)
    block_ids = row_ids // LOCAL_SEQUENCES
    group_ids = row_ids // GROUP_SEQS
    groups = TOTAL_SEQUENCES // GROUP_SEQS
    common_expert = jax.random.randint(jax.random.fold_in(starting_point, 1), (groups,), 0, EXPERTS)[group_ids]
    order_keys = jax.random.split(jax.random.fold_in(starting_point, 2), block_list)
    placing = jax.vmap(lambda sub_key: jax.random.permutation(sub_key, LOCAL_SEQUENCES))(order_keys).reshape(TOTAL_SEQUENCES)
    offsets = jax.random.randint(jax.random.fold_in(starting_point, 3), (block_list,), 0, EXPERTS - 1)[block_ids]
    other_keys = jax.random.split(jax.random.fold_in(starting_point, 4), block_list)
    other_order = jax.vmap(lambda sub_key: jax.random.permutation(sub_key, EXPERTS - 1))(other_keys)[block_ids]

    def other_expert(entry):
        column = (entry + offsets) % (EXPERTS - 1)
        picked = jnp.take_along_axis(other_order, column[:, None], axis=1)[:, 0]
        return (common_expert + 1 + picked) % EXPERTS
    leading = placing < CAP
    later = placing - CAP
    first_pick = jnp.where(leading, common_expert, other_expert(CAP + 2 * later))
    second_pick = jnp.where(leading, other_expert(placing), other_expert(CAP + 2 * later + 1))
    coin = jax.random.randint(jax.random.fold_in(starting_point, 5), (TOTAL_SEQUENCES,), 0, 2)
    still_live = jnp.where(leading, 1, coin)
    return (jnp.stack([first_pick, second_pick], axis=1).astype(jnp.int32), still_live.astype(jnp.int32))


def draw_routes(key, part):
    return route_plan(key)[0]


def draw_active(key, part):
    return route_plan(key)[1]


def draw_cache_length(key, part):
    row_ids = jnp.arange(TOTAL_SEQUENCES, dtype=jnp.int32)
    block_list = TOTAL_SEQUENCES // LOCAL_SEQUENCES
    lengths = jax.random.randint(jax.random.fold_in(key, 11), (TOTAL_SEQUENCES,), 2, MAX_POSITIONS + 1)
    longest = jax.random.randint(jax.random.fold_in(key, 12), (block_list,), 0, LOCAL_SEQUENCES)[row_ids // LOCAL_SEQUENCES]
    return jnp.where(row_ids % LOCAL_SEQUENCES == longest, MAX_POSITIONS, lengths).astype(jnp.int32)


def draw_queries(key, part):
    result = jnp.clip(jax.random.normal(jax.random.fold_in(key, 6), (TOTAL_SEQUENCES, MODEL_WIDTH), jnp.float32), -4.0, 4.0)
    return result.astype(jnp.bfloat16)


def draw_cache(key, part):
    array_extent = (TOTAL_SEQUENCES, 2, MAX_POSITIONS, KEY_VALUE_HEADS * HEAD_SIZE)
    result = jnp.clip(jax.random.normal(jax.random.fold_in(key, 9), array_extent, jnp.float32), -4.0, 4.0)
    return result.astype(jnp.bfloat16)


def draw_residual(key, part):
    columns = jnp.arange(MODEL_WIDTH, dtype=jnp.int32).astype(jnp.float32) / MODEL_WIDTH
    column_scale = jnp.power(10.0, 0.5 * columns + 0.5 * jax.random.uniform(jax.random.fold_in(key, 62), (MODEL_WIDTH,), jnp.float32))
    row_draw = jax.random.uniform(jax.random.fold_in(key, 61), (TOTAL_SEQUENCES, 1), jnp.float32)
    row_scale = jnp.power(10.0, row_draw)
    values = jnp.clip(jax.random.normal(jax.random.fold_in(key, 65), (TOTAL_SEQUENCES, MODEL_WIDTH), jnp.float32), -4.0, 4.0)
    return (values * row_scale * column_scale[None, :]).astype(jnp.bfloat16)


def block_levels(own_key, extent, shards, smallest, top_value):
    def one(axis_at, shards_of):
        heights = jax.random.uniform(jax.random.fold_in(jax.random.fold_in(own_key, 6), axis_at), (shards_of,), jnp.float32, smallest / len(shards), top_value / len(shards))
        return jnp.repeat(jnp.exp(heights), extent[axis_at] // shards_of).reshape((-1,) + (1,) * (len(extent) - axis_at - 1))

    factor_of = one(*shards[0])
    for cut in shards[1:]:
        factor_of = factor_of * one(*cut)
    return factor_of


def gaussian(key, extent, deviation, most, cuts=(), kind=jnp.bfloat16):
    factor_of = block_levels(key, extent, cuts, -0.22, 0.18) if cuts else 1.0
    drawn = jax.random.normal(key, extent, jnp.float32) * deviation * factor_of
    return jnp.minimum(jnp.maximum(drawn, -most), most).astype(kind)


def setup_inputs(seed: int = 0) -> dict:
    keys = jax.random.split(jax.random.key(seed), 13)
    return {
        "residual": draw_residual(jax.random.fold_in(keys[12], 71), 0),
        "queries": draw_queries(jax.random.fold_in(keys[12], 71), 0),
        "token_key_value": gaussian(keys[2], (TOTAL_SEQUENCES, 2, KEY_VALUE_HEADS * HEAD_SIZE), 1.0, 4.0, ((0, 64), (2, 2))),
        "cache": draw_cache(jax.random.fold_in(keys[12], 71), 0),
        "cache_length": draw_cache_length(jax.random.fold_in(keys[12], 71), 0),
        "active": draw_active(jax.random.fold_in(keys[12], 71), 0),
        "routes": draw_routes(jax.random.fold_in(keys[12], 71), 0),
        "norm_gain": jnp.clip(1.0 + 0.18 * jax.random.normal(keys[7], (MODEL_WIDTH,), jnp.float32), 0.099609375, 1.8984375).astype(jnp.bfloat16),
        "router": gaussian(keys[8], (MODEL_WIDTH, EXPERTS), MODEL_WIDTH ** -0.5, 0.09375, ((0, 2),)),
        "w_gate": gaussian(keys[9], (EXPERTS, MODEL_WIDTH, FF), MODEL_WIDTH ** -0.5, 0.09375, ((0, 8), (1, 16))),
        "w_up": gaussian(keys[10], (EXPERTS, MODEL_WIDTH, FF), MODEL_WIDTH ** -0.5, 0.09375, ((0, 8), (1, 16))),
        "w_down": gaussian(keys[11], (EXPERTS, MODEL_WIDTH, FF), FF ** -0.5, 0.0625, ((0, 8), (1, 16))),
    }


EPSILON = 1e-05

def block_attention(inputs):
    query_matrix, incoming_pair, cache_contents, lengths = inputs
    batch_entries = query_matrix.shape[0]
    group_share = QUERY_HEADS // KEY_VALUE_HEADS
    score_scale = HEAD_SIZE ** (-0.5)
    finest_precision = lax.Precision.HIGHEST
    query_head_rows = query_matrix.astype(jnp.float32).reshape(batch_entries, KEY_VALUE_HEADS, group_share, HEAD_SIZE)
    stored_keys = cache_contents[:, 0].astype(jnp.float32).reshape(batch_entries, MAX_POSITIONS, KEY_VALUE_HEADS, HEAD_SIZE)
    stored_values = cache_contents[:, 1].astype(jnp.float32).reshape(batch_entries, MAX_POSITIONS, KEY_VALUE_HEADS, HEAD_SIZE)
    incoming_key = incoming_pair[:, 0].astype(jnp.float32).reshape(batch_entries, KEY_VALUE_HEADS, HEAD_SIZE)
    incoming_value = incoming_pair[:, 1].astype(jnp.float32).reshape(batch_entries, KEY_VALUE_HEADS, HEAD_SIZE)
    scores = jnp.einsum('bkgd,blkd->bkgl', query_head_rows, stored_keys, precision=finest_precision) * score_scale
    in_cache = jnp.arange(MAX_POSITIONS, dtype=jnp.int32)[None, None, None, :] < lengths[:, None, None, None]
    scores = jnp.where(in_cache, scores, -jnp.inf)
    self_score = jnp.einsum('hont,hot->hon', query_head_rows, incoming_key, precision=finest_precision) * score_scale
    highest = jnp.maximum(lax.optimization_barrier(jnp.max(scores, axis=-1)), self_score)
    exponent = jnp.exp(scores - highest[..., None])
    own_exp = jnp.exp(self_score - highest)
    totals = lax.optimization_barrier(jnp.sum(exponent, axis=-1)) + own_exp
    normalized = (exponent / totals[..., None]).astype(jnp.bfloat16)
    own_weight = (own_exp / totals).astype(jnp.bfloat16)
    normalized = lax.optimization_barrier(normalized).astype(jnp.float32)
    own_weight = lax.optimization_barrier(own_weight).astype(jnp.float32)
    mixture = jnp.einsum('bkgl,blkd->bkgd', normalized, stored_values, precision=finest_precision)
    mixture = mixture + own_weight[..., None] * incoming_value[:, :, None, :]
    return mixture.reshape(batch_entries, QUERY_HEADS * HEAD_SIZE).astype(jnp.bfloat16)

def reference(residual, queries, token_key_value, cache, cache_length, active, routes, norm_gain, router, w_gate, w_up, w_down):
    block_list = TOTAL_SEQUENCES // LOCAL_SEQUENCES
    attention_output = lax.map(block_attention, (queries.reshape(block_list, LOCAL_SEQUENCES, MODEL_WIDTH), token_key_value.reshape(block_list, LOCAL_SEQUENCES, 2, KEY_VALUE_HEADS * HEAD_SIZE), cache.reshape(block_list, LOCAL_SEQUENCES, 2, MAX_POSITIONS, KEY_VALUE_HEADS * HEAD_SIZE), cache_length.reshape(block_list, LOCAL_SEQUENCES))).reshape(TOTAL_SEQUENCES, MODEL_WIDTH)
    state = residual.astype(jnp.float32) + attention_output.astype(jnp.float32)
    row_scale = jnp.sqrt(lax.optimization_barrier(jnp.mean(state * state, axis=1, keepdims=True)) + EPSILON)
    scaled = state * norm_gain.astype(jnp.float32)[None, :]
    normed = (scaled / row_scale).astype(jnp.bfloat16)
    logits = jnp.dot(scaled, router.astype(jnp.float32), precision=lax.Precision.HIGHEST) / row_scale
    chosen = jnp.take_along_axis(logits, routes, axis=1)
    weight_first = jax.nn.sigmoid(chosen[:, 0] - chosen[:, 1])
    weight_second = 1.0 - weight_first
    still_live = active == 1
    bound = N_GRP * N_EP * CAP

    def one_expert(running, expert_id):
        hit_first = (routes[:, 0] == expert_id) & still_live
        hit_second = (routes[:, 1] == expert_id) & still_live
        hit_any = hit_first | hit_second
        row_index = jnp.nonzero(hit_any, size=bound, fill_value=0)[0].astype(jnp.int32)
        filled = jnp.arange(bound, dtype=jnp.int32) < jnp.sum(hit_any.astype(jnp.int32))
        chosen_rows = normed[row_index]
        gate_part = jnp.dot(chosen_rows, w_gate[expert_id], preferred_element_type=jnp.float32)
        up_part = jnp.dot(chosen_rows, w_up[expert_id], preferred_element_type=jnp.float32)
        hidden = (jax.nn.silu(gate_part) * up_part).astype(jnp.bfloat16)
        expert_out = lax.dot_general(hidden, w_down[expert_id], (((1,), (1,)), ((), ())), preferred_element_type=jnp.float32).astype(jnp.bfloat16)
        mixing = jnp.where(hit_first[row_index], weight_first[row_index], weight_second[row_index])
        mixing = jnp.where(filled, mixing, 0.0)
        return (running.at[row_index].add(expert_out.astype(jnp.float32) * mixing[:, None]), None)
    moe_sum, _ = lax.scan(one_expert, jnp.zeros((TOTAL_SEQUENCES, MODEL_WIDTH), jnp.float32), jnp.arange(EXPERTS, dtype=jnp.int32))
    delta = jnp.where(still_live[:, None], attention_output.astype(jnp.float32) + moe_sum, 0.0)
    return delta.astype(jnp.bfloat16)
```

```python
import jax
import jax.numpy as jnp
from jax import lax
from jax.experimental import pallas as pl
from jax.experimental.pallas import tpu as pltpu
from jax.sharding import PartitionSpec as P

MODEL_WIDTH = 4096
QUERY_HEADS = 32
KEY_VALUE_HEADS = 8
HEAD_SIZE = 128


EPSILON = 1e-05

SIDE = 4
ROWS = 64
DBLK = 256
DSET = SIDE * DBLK
FBLK = 2048
FT = 512
MESH_AXES = ("grp", "ep", "tp")
MESH_ID = pl.DeviceIdType.MESH


def line_permutation(step):
    pairs = []
    for grp in range(8):
        for ep in range(8):
            for tp in range(2):
                x, z = grp % 4, (grp // 4) * 2 + tp
                if ep % 2 == 0:
                    x2, z2 = (x + step) % SIDE, z
                else:
                    x2, z2 = x, (z + step) % SIDE
                pairs.append(((grp * 8 + ep) * 2 + tp, (((z2 // 2) * 4 + x2) * 8 + ep) * 2 + z2 % 2))
    return pairs


def coordinates():
    grp, ep, tp = (lax.axis_index(name) for name in MESH_AXES)
    x = lax.rem(grp, 4)
    z = lax.div(grp, 4) * 2 + tp
    core = lax.rem(ep, 2)
    return x + (z - x) * core, z + (x - z) * core, core, ep


def moe_kernel(
    x_in, w_gate, w_up, w_down, g1, g2, g3, u1, u2, u3, d1, d2, d3, y_out,
    rows, wg, wu, wd, send, fwd, got, own, hid, part, part32, part_in, y_send,
    w_sem, xs_send, xs_recv, x_local, xa_send, xa_recv, rs_send, rs_recv, ag_send, ag_recv,
    o_send, o_recv, y_ssem, y_rsem, y_local,
):
    a, b, core, ep = coordinates()

    def place(at_a, at_b):
        return at_a + (at_b - at_a) * core, at_b + (at_a - at_b) * core

    def peer(at_a, at_b):
        x, z = place(at_a, at_b)
        return (lax.div(z, 2) * 4 + x, ep, lax.rem(z, 2))

    def block(at_a, at_b):
        x, z = place(at_a, at_b)
        return pl.multiple_of((lax.div(z, 2) * 8 + x * 2 + lax.rem(z, 2)) * DBLK, DBLK)

    def shifted(value, by):
        return lax.rem(value + by + SIDE, SIDE)

    def remote(src, dst, ssem, rsem, to):
        return pltpu.make_async_remote_copy(
            src_ref=src, dst_ref=dst, send_sem=ssem, recv_sem=rsem, device_id=to, device_id_type=MESH_ID
        )

    right, left, across = shifted(b, 1), shifted(b, -1), shifted(b, 2)

    loads = []
    for which, (full, parts, dst) in enumerate(
        ((w_gate, (g1, g2, g3), wg), (w_up, (u1, u2, u3), wu), (w_down, (d1, d2, d3), wd))
    ):
        column = pl.ds(pl.multiple_of(a * FBLK, FBLK), FBLK)
        for step in range(SIDE):
            row = pl.ds(pl.multiple_of(shifted(a, -step) * DBLK, DBLK), DBLK)
            src = full.at[:, column] if step == 0 else parts[step - 1]
            copy = pltpu.make_async_copy(src, dst.at[row], w_sem.at[which, step])
            copy.start()
            loads.append(copy)

    barrier = pltpu.get_barrier_semaphore()
    for step in range(1, SIDE):
        pl.semaphore_signal(barrier, inc=1, device_id=peer(shifted(a, step), b), device_id_type=MESH_ID)
        pl.semaphore_signal(barrier, inc=1, device_id=peer(a, shifted(b, step)), device_id_type=MESH_ID)
    pl.semaphore_wait(barrier, 2 * (SIDE - 1))

    copies = []
    for step in (2, 1, 3):
        to_b = shifted(b, step)
        for k in range(SIDE):
            copy = remote(
                x_in.at[:, pl.ds(block(k, to_b), DBLK)],
                rows.at[a, b, :, pl.ds(k * DBLK, DBLK)],
                xs_send.at[step - 1, k], xs_recv.at[step - 1, k], peer(a, to_b),
            )
            copy.start()
            copies.append(copy)
    local = []
    for k in range(SIDE):
        copy = pltpu.make_async_copy(
            x_in.at[:, pl.ds(block(k, b), DBLK)], rows.at[a, b, :, pl.ds(k * DBLK, DBLK)], x_local.at[k]
        )
        copy.start()
        local.append(copy)
    for copy in local + copies:
        copy.wait()

    copies = []
    for step in (2, 1, 3):
        copy = remote(
            rows.at[a], rows.at[a], xa_send.at[step - 1], xa_recv.at[step - 1], peer(shifted(a, step), b)
        )
        copy.start()
        copies.append(copy)
    for copy in loads[: 2 * SIDE]:
        copy.wait()
    for copy in copies:
        copy.wait()

    def partial(group, half, tile):
        lhs = rows[pl.ds(2 * half, 2), group].reshape(2 * ROWS, DSET)
        cols = pl.ds(pl.multiple_of(tile * FT, FT), FT)
        ups = pl.ds(pl.multiple_of(tile * FT + FBLK, FT), FT)
        gate = jnp.dot(lhs, wg[:, cols], preferred_element_type=jnp.float32)
        up = jnp.dot(lhs, wu[:, cols], preferred_element_type=jnp.float32)
        return cols, ups, gate, up

    def fill(group, half, slot, extra=None):
        @pl.loop(0, FBLK // FT)
        def _(tile):
            cols, ups, gate, up = partial(group, half, tile)
            if extra is not None:
                gate = gate + fwd[extra, :, cols].astype(jnp.float32)
                up = up + fwd[extra, :, ups].astype(jnp.float32)
            send[slot, :, cols] = gate.astype(jnp.bfloat16)
            send[slot, :, ups] = up.astype(jnp.bfloat16)

    to_right, to_left = peer(a, right), peer(a, left)
    fill(across, 0, 0)
    over_right = remote(send.at[0], fwd.at[0], rs_send.at[0], rs_recv.at[0], to_right)
    over_right.start()
    fill(across, 1, 1)
    over_left = remote(send.at[1], fwd.at[1], rs_send.at[1], rs_recv.at[1], to_left)
    over_left.start()
    fill(right, 1, 2)
    plain_right = remote(send.at[2], got.at[1], rs_send.at[2], rs_recv.at[2], to_right)
    plain_right.start()
    fill(left, 0, 3)
    plain_left = remote(send.at[3], got.at[2], rs_send.at[3], rs_recv.at[3], to_left)
    plain_left.start()
    over_right.wait()
    fill(right, 0, 4, 0)
    sum_right = remote(send.at[4], got.at[0], rs_send.at[4], rs_recv.at[4], to_right)
    sum_right.start()
    over_left.wait()
    fill(left, 1, 5, 1)
    sum_left = remote(send.at[5], got.at[3], rs_send.at[5], rs_recv.at[5], to_left)
    sum_left.start()

    for half in range(2):

        @pl.loop(0, FBLK // FT)
        def _(tile, half=half):
            cols, ups, gate, up = partial(b, half, tile)
            own[half, :, cols] = gate
            own[half, :, ups] = up

    for copy in (plain_right, plain_left, sum_right, sum_left):
        copy.wait()

    for half in range(2):

        @pl.loop(0, FBLK // FT)
        def _(tile, half=half):
            cols = pl.ds(pl.multiple_of(tile * FT, FT), FT)
            ups = pl.ds(pl.multiple_of(tile * FT + FBLK, FT), FT)
            gate = (
                own[half, :, cols]
                + got[half, :, cols].astype(jnp.float32)
                + got[2 + half, :, cols].astype(jnp.float32)
            )
            up = (
                own[half, :, ups]
                + got[half, :, ups].astype(jnp.float32)
                + got[2 + half, :, ups].astype(jnp.float32)
            )
            value = gate / (1.0 + jnp.exp(-gate)) * up
            hid[b, half, :, cols] = value.astype(jnp.bfloat16)

    own_right = remote(hid.at[b], hid.at[b], ag_send.at[0], ag_recv.at[0], to_right)
    own_left = remote(hid.at[b], hid.at[b], ag_send.at[1], ag_recv.at[1], to_left)
    own_right.start()
    own_left.start()
    for copy in loads[2 * SIDE :]:
        copy.wait()

    o_copies = {}

    def down(order, group):
        lhs = hid[group].reshape(SIDE * ROWS, FBLK)

        @pl.loop(0, DSET // DBLK)
        def _(tile):
            cols = pl.ds(pl.multiple_of(tile * DBLK, DBLK), DBLK)
            out = lax.dot_general(
                lhs, wd[cols, :], (((1,), (1,)), ((), ())), preferred_element_type=jnp.float32
            ).reshape(SIDE, ROWS, DBLK)
            part32[order, :, :, cols] = out
            part[order, :, :, cols] = out.astype(jnp.bfloat16)

        for step in (2, 1, 3):
            to_a = shifted(a, step)
            copy = remote(
                part.at[order, to_a], part_in.at[order, step - 1],
                o_send.at[order, step - 1], o_recv.at[order, step - 1], peer(to_a, b),
            )
            copy.start()
            o_copies[order, step] = copy

    y_copies = []

    def finish(order, group):
        total = part32[order, a]
        for step in range(1, SIDE):
            o_copies[order, step].wait()
            total = total + part_in[order, step - 1].astype(jnp.float32)
        y_send[order] = total.astype(jnp.bfloat16)
        for k in range(SIDE):
            src = y_send.at[order, :, pl.ds(k * DBLK, DBLK)]
            dst = y_out.at[:, pl.ds(block(k, b), DBLK)]
            if order == 0:
                copy = pltpu.make_async_copy(src, dst, y_local.at[k])
            else:
                copy = remote(src, dst, y_ssem.at[order - 1, k], y_rsem.at[order - 1, k], peer(a, group))
            copy.start()
            y_copies.append(copy)

    down(0, b)
    own_right.wait()
    on_right = remote(hid.at[left, 0], hid.at[left, 0], ag_send.at[2], ag_recv.at[2], to_right)
    on_right.start()
    own_left.wait()
    on_left = remote(hid.at[right, 1], hid.at[right, 1], ag_send.at[3], ag_recv.at[3], to_left)
    on_left.start()
    down(1, left)
    down(3, right)
    finish(0, b)
    on_right.wait()
    on_left.wait()
    down(2, across)
    finish(1, left)
    finish(3, right)
    finish(2, across)
    for copy in y_copies:
        copy.wait()


def expert_layer(x_in, w_gate, w_up, w_down, moved):
    bf16, f32 = jnp.bfloat16, jnp.float32
    dma = pltpu.SemaphoreType.DMA
    scratch = [
        pltpu.VMEM((SIDE, SIDE, ROWS, DSET), bf16),
        pltpu.VMEM((DSET, FBLK), bf16),
        pltpu.VMEM((DSET, FBLK), bf16),
        pltpu.VMEM((DSET, FBLK), bf16),
        pltpu.VMEM((6, 2 * ROWS, 2 * FBLK), bf16),
        pltpu.VMEM((2, 2 * ROWS, 2 * FBLK), bf16),
        pltpu.VMEM((4, 2 * ROWS, 2 * FBLK), bf16),
        pltpu.VMEM((2, 2 * ROWS, 2 * FBLK), f32),
        pltpu.VMEM((SIDE, 2, 2 * ROWS, FBLK), bf16),
        pltpu.VMEM((SIDE, SIDE, ROWS, DSET), bf16),
        pltpu.VMEM((SIDE, SIDE, ROWS, DSET), f32),
        pltpu.VMEM((SIDE, SIDE - 1, ROWS, DSET), bf16),
        pltpu.VMEM((SIDE, ROWS, DSET), bf16),
        dma((3, SIDE)),
        dma((3, SIDE)), dma((3, SIDE)), dma((SIDE,)),
        dma((3,)), dma((3,)),
        dma((6,)), dma((6,)),
        dma((4,)), dma((4,)),
        dma((SIDE, 3)), dma((SIDE, 3)),
        dma((3, SIDE)), dma((3, SIDE)), dma((SIDE,)),
    ]
    anywhere = pl.BlockSpec(memory_space=pl.ANY)
    return pl.pallas_call(
        moe_kernel,
        out_shape=jax.ShapeDtypeStruct((ROWS, MODEL_WIDTH), bf16),
        in_specs=[anywhere] * 13,
        out_specs=anywhere,
        scratch_shapes=scratch,
        compiler_params=pltpu.CompilerParams(
            collective_id=0, has_side_effects=True, vmem_limit_bytes=60 * 1024 * 1024
        ),
        cost_estimate=pl.CostEstimate(flops=13 * 10**9, bytes_accessed=14 * 10**6, transcendentals=10**6),
        name="expert_layer",
    )(x_in, w_gate, w_up, w_down, *moved)


def attend_local(queries, token_key_value, cache, cache_length):
    seq_count = queries.shape[0]
    positions = cache.shape[2]
    heads_kv = cache.shape[3] // HEAD_SIZE
    group_share = QUERY_HEADS // KEY_VALUE_HEADS
    score_scale = HEAD_SIZE ** (-0.5)
    query_head_rows = queries.reshape(seq_count, heads_kv, group_share, HEAD_SIZE)
    stored_keys = cache[:, 0].reshape(seq_count, positions, heads_kv, HEAD_SIZE)
    stored_values = cache[:, 1].reshape(seq_count, positions, heads_kv, HEAD_SIZE)
    incoming_key = token_key_value[:, 0].reshape(seq_count, heads_kv, HEAD_SIZE)
    incoming_value = token_key_value[:, 1].reshape(seq_count, heads_kv, HEAD_SIZE)
    scores = (
        jnp.einsum(
            "skgd,slkd->skgl", query_head_rows, stored_keys, preferred_element_type=jnp.float32
        )
        * score_scale
    )
    in_cache = (
        jnp.arange(positions, dtype=jnp.int32)[None, None, None, :]
        < cache_length[:, None, None, None]
    )
    scores = jnp.where(in_cache, scores, -jnp.inf)
    self_score = (
        jnp.einsum(
            "skgd,skd->skg", query_head_rows, incoming_key, preferred_element_type=jnp.float32
        )
        * score_scale
    )
    highest = jnp.maximum(jnp.max(scores, axis=-1), self_score)
    exponent = jnp.exp(scores - highest[..., None])
    own_exp = jnp.exp(self_score - highest)
    totals = jnp.sum(exponent, axis=-1) + own_exp
    normalized = (exponent / totals[..., None]).astype(jnp.bfloat16)
    own_weight = (own_exp / totals).astype(jnp.bfloat16)
    mixture = jnp.einsum(
        "skgl,slkd->skgd", normalized, stored_values, preferred_element_type=jnp.float32
    )
    mixture = (
        mixture
        + own_weight.astype(jnp.float32)[..., None]
        * incoming_value.astype(jnp.float32)[:, :, None, :]
    )
    return mixture.reshape(seq_count, heads_kv * group_share * HEAD_SIZE).astype(jnp.bfloat16)


def per_device(
    residual,
    queries,
    token_key_value,
    cache,
    cache_length,
    active,
    routes,
    norm_gain,
    router,
    w_gate,
    w_up,
    w_down,
):
    tp_count = lax.axis_size("tp")
    tp_rank = lax.axis_index("tp")
    w_gate, w_up, w_down = w_gate[0], w_up[0], w_down[0]
    line_rank = coordinates()[0]
    moved = []
    for weight in (w_gate, w_up, w_down):
        for step in range(1, SIDE):
            column = lax.rem(line_rank + step, SIDE) * FBLK
            piece = lax.dynamic_slice(weight, (0, column), (DBLK, FBLK))
            moved.append(lax.ppermute(piece, MESH_AXES, line_permutation(step)))
    attention_output = attend_local(queries, token_key_value, cache, cache_length)
    state = residual.astype(jnp.float32) + attention_output.astype(jnp.float32)
    scaled = state * norm_gain.astype(jnp.float32)[None, :]
    squares, raw_logits = lax.psum(
        (
            jnp.sum(state * state, axis=1),
            jnp.dot(scaled, router.astype(jnp.float32), precision=lax.Precision.HIGHEST),
        ),
        "tp",
    )
    row_scale = jnp.sqrt(squares / MODEL_WIDTH + EPSILON)[:, None]
    logits = raw_logits / row_scale
    normed = lax.all_gather((scaled / row_scale).astype(jnp.bfloat16), "tp", axis=1, tiled=True)
    chosen = jnp.take_along_axis(logits, routes, axis=1)
    weight_first = jax.nn.sigmoid(chosen[:, 0] - chosen[:, 1])
    weight_second = 1.0 - weight_first
    seq_count = residual.shape[0]
    expert_count = router.shape[1]
    half_cap = seq_count // 2 // tp_count
    slot_total = half_cap * expert_count
    still_live = active == 1
    flat_expert = routes.reshape(-1)
    flat_live = jnp.repeat(still_live, 2)
    onehot = (
        (flat_expert[:, None] == jnp.arange(expert_count, dtype=jnp.int32)[None, :])
        & flat_live[:, None]
    ).astype(jnp.int32)
    before = jnp.cumsum(onehot, axis=0) - onehot
    rank_order = jnp.sum(before * onehot, axis=1)
    owner_half = rank_order // half_cap
    slot_index = rank_order % half_cap * expert_count + flat_expert
    on_this_half = flat_live & (owner_half == tp_rank)
    selector = (
        (
            (slot_index[:, None] == jnp.arange(slot_total, dtype=jnp.int32)[None, :])
            & on_this_half[:, None]
        )
        .astype(jnp.bfloat16)
        .reshape(seq_count, 2, slot_total)
    )
    senders = selector[:, 0] + selector[:, 1]
    outgoing = lax.dot_general(
        senders, normed, (((0,), (0,)), ((), ())), preferred_element_type=jnp.float32
    )
    outgoing = outgoing.astype(jnp.bfloat16).reshape(half_cap, expert_count, normed.shape[1])
    arrived = lax.all_to_all(outgoing, "ep", split_axis=1, concat_axis=0, tiled=True)
    results = expert_layer(arrived.reshape(ROWS, MODEL_WIDTH), w_gate, w_up, w_down, moved)
    results = results.reshape(ROWS, 1, MODEL_WIDTH)
    returned = lax.all_to_all(results, "ep", split_axis=0, concat_axis=1, tiled=True).reshape(
        slot_total, normed.shape[1]
    )
    pick_first = jnp.dot(selector[:, 0], returned, preferred_element_type=jnp.float32)
    pick_second = jnp.dot(selector[:, 1], returned, preferred_element_type=jnp.float32)
    combined = weight_first[:, None] * pick_first + weight_second[:, None] * pick_second
    moe_sum = lax.psum_scatter(
        combined.astype(jnp.bfloat16), "tp", scatter_dimension=1, tiled=True
    ).astype(jnp.float32)
    delta = jnp.where(still_live[:, None], attention_output.astype(jnp.float32) + moe_sum, 0.0)
    return delta.astype(jnp.bfloat16)


def solution(mesh):
    in_specs = (
        P(("grp", "ep"), "tp"),
        P(("grp", "ep"), "tp"),
        P(("grp", "ep"), None, "tp"),
        P(("grp", "ep"), None, None, "tp"),
        P(("grp", "ep")),
        P(("grp", "ep")),
        P(("grp", "ep"), None),
        P("tp"),
        P("tp", None),
        P("ep", ("grp", "tp"), None),
        P("ep", ("grp", "tp"), None),
        P("ep", ("grp", "tp"), None),
    )
    out_specs = P(("grp", "ep"), "tp")
    return jax.shard_map(
        per_device, mesh=mesh, in_specs=in_specs, out_specs=out_specs, check_vma=False
    )
```

```python
import functools

import jax
import jax.numpy as jnp
from jax import lax
from jax.experimental import pallas as pl
from jax.experimental.pallas import tpu as pltpu
from jax.sharding import PartitionSpec as P

MODEL_WIDTH = 4096
QUERY_HEADS = 32
KEY_VALUE_HEADS = 8
HEAD_SIZE = 128


EPSILON = 1e-05

SIDE = 4
DEVICES = 128
CAP = 16
PIECES = 64
ALL_ROWS = PIECES * CAP
DBLK = 256
DSET = SIDE * DBLK
FBLK = 2048
FT = 512
MESH_AXES = ("grp", "ep", "tp")
MESH_ID = pl.DeviceIdType.MESH


def line_permutation(step):
    pairs = []
    for grp in range(8):
        for ep in range(8):
            for tp in range(2):
                x, z = grp % 4, (grp // 4) * 2 + tp
                if ep % 2 == 0:
                    x2, z2 = (x + step) % SIDE, z
                else:
                    x2, z2 = x, (z + step) % SIDE
                pairs.append(((grp * 8 + ep) * 2 + tp, (((z2 // 2) * 4 + x2) * 8 + ep) * 2 + z2 % 2))
    return pairs


def coordinates():
    grp, ep, tp = (lax.axis_index(name) for name in MESH_AXES)
    x = lax.rem(grp, 4)
    z = lax.div(grp, 4) * 2 + tp
    core = lax.rem(ep, 2)
    return x + (z - x) * core, z + (x - z) * core, core, ep


def moe_kernel(
    keep, x_in, w_gate, w_up, w_down, g1, g2, g3, u1, u2, u3, d1, d2, d3, *refs
):
    if keep < ALL_ROWS:
        at_row, at_column, *refs = refs
    (
        y_out, landed, rows, wg, wu, wd, send, fwd, got, own, hid, part, part32, part_in, total, y_send,
        w_sem, x_send, x_recv, xa_send, xa_recv, rs_send, rs_recv, ag_send, ag_recv,
        o_send, o_recv, y_ssem, y_rsem, *spare,
    ) = refs
    quarter, eighth = keep // SIDE, keep // (2 * SIDE)
    a, b, core, ep = coordinates()
    grp, tp = lax.axis_index("grp"), lax.axis_index("tp")
    z_hi = lax.div(grp, 4)
    own_block = lax.rem(grp, 4) * 2 + tp
    itself = (grp * 8 + ep) * 2 + tp

    def peer(at_a, at_b):
        x = at_a + (at_b - at_a) * core
        z = at_b + (at_a - at_b) * core
        return (lax.div(z, 2) * 4 + x, ep, lax.rem(z, 2))

    def shifted(value, by):
        return lax.rem(value + by + SIDE, SIDE)

    def remote(src, dst, ssem, rsem, to):
        return pltpu.make_async_remote_copy(
            src_ref=src, dst_ref=dst, send_sem=ssem, recv_sem=rsem, device_id=to, device_id_type=MESH_ID
        )

    right, left, across = shifted(b, 1), shifted(b, -1), shifted(b, 2)

    loads = []
    for which, (full, parts, dst) in enumerate(
        ((w_gate, (g1, g2, g3), wg), (w_up, (u1, u2, u3), wu), (w_down, (d1, d2, d3), wd))
    ):
        column = pl.ds(pl.multiple_of(a * FBLK, FBLK), FBLK)
        for step in range(SIDE):
            row = pl.ds(pl.multiple_of(shifted(a, -step) * DBLK, DBLK), DBLK)
            src = full.at[:, column] if step == 0 else parts[step - 1]
            copy = pltpu.make_async_copy(src, dst.at[row], w_sem.at[which, step])
            copy.start()
            loads.append(copy)

    barrier = pltpu.get_barrier_semaphore()

    @pl.loop(1, DEVICES)
    def _(step):
        at = lax.rem(itself + step, DEVICES)
        to = (lax.div(at, 16), lax.rem(lax.div(at, 2), 8), lax.rem(at, 2))
        pl.semaphore_signal(barrier, inc=1, device_id=to, device_id_type=MESH_ID)

    pl.semaphore_wait(barrier, DEVICES - 1)

    def deliver(move, src_of, dst_of, to_of, sends, recvs):
        @pl.loop(0, PIECES)
        def _(step):
            to = to_of(step)
            far = (to[0] * 8 + to[1]) * 2 + to[2] != itself

            @pl.when(far)
            def _():
                remote(src_of(step), dst_of(step), sends.at[0], recvs.at[0], to).start()

            @pl.when(jnp.logical_not(far))
            def _():
                pltpu.make_async_copy(src_of(step), dst_of(step), recvs.at[0]).start()
                pltpu.make_async_copy(src_of(step), spare[move], sends.at[0]).start()

    def expert_of(step):
        return lax.rem(ep + lax.div(step, 8), 8)

    def block_of(step):
        return lax.rem(own_block + step, 8)

    deliver(
        0,
        lambda step: x_in.at[expert_of(step), :, pl.ds(pl.multiple_of(block_of(step) * DBLK, DBLK), DBLK)],
        lambda step: landed.at[grp * 8 + ep],
        lambda step: (tp * 4 + lax.div(block_of(step), 2), expert_of(step), lax.rem(block_of(step), 2)),
        x_send, x_recv,
    )
    pltpu.make_async_copy(x_in, x_in, x_send.at[0]).wait()
    pltpu.make_async_copy(landed, landed, x_recv.at[0]).wait()
    if keep < ALL_ROWS:
        place = lax.broadcasted_iota(jnp.int32, (keep, ALL_ROWS), 0)
        pick = (place == at_row[...]).astype(jnp.bfloat16)
        packed = jnp.dot(pick, landed[...].reshape(ALL_ROWS, DBLK), preferred_element_type=jnp.float32)
        rows[a] = packed.astype(jnp.bfloat16)
    else:
        rows[a] = landed[...].reshape(ALL_ROWS, DBLK)

    copies = []
    for step in (2, 1, 3):
        copy = remote(
            rows.at[a], rows.at[a], xa_send.at[step - 1], xa_recv.at[step - 1], peer(shifted(a, step), b)
        )
        copy.start()
        copies.append(copy)
    for copy in loads[: 2 * SIDE]:
        copy.wait()
    for copy in copies:
        copy.wait()

    def partial(group, half, tile):
        first = pl.multiple_of(group * quarter + half * eighth, 16)
        lhs = jnp.concatenate([rows[k, pl.ds(first, eighth), :] for k in range(SIDE)], axis=1)
        cols = pl.ds(pl.multiple_of(tile * FT, FT), FT)
        ups = pl.ds(pl.multiple_of(tile * FT + FBLK, FT), FT)
        gate = jnp.dot(lhs, wg[:, cols], preferred_element_type=jnp.float32)
        up = jnp.dot(lhs, wu[:, cols], preferred_element_type=jnp.float32)
        return cols, ups, gate, up

    def fill(group, half, slot, extra=None):
        @pl.loop(0, FBLK // FT)
        def _(tile):
            cols, ups, gate, up = partial(group, half, tile)
            if extra is not None:
                gate = gate + fwd[extra, :, cols].astype(jnp.float32)
                up = up + fwd[extra, :, ups].astype(jnp.float32)
            send[slot, :, cols] = gate.astype(jnp.bfloat16)
            send[slot, :, ups] = up.astype(jnp.bfloat16)

    to_right, to_left = peer(a, right), peer(a, left)
    fill(across, 0, 0)
    over_right = remote(send.at[0], fwd.at[0], rs_send.at[0], rs_recv.at[0], to_right)
    over_right.start()
    fill(across, 1, 1)
    over_left = remote(send.at[1], fwd.at[1], rs_send.at[1], rs_recv.at[1], to_left)
    over_left.start()
    fill(right, 1, 2)
    plain_right = remote(send.at[2], got.at[1], rs_send.at[2], rs_recv.at[2], to_right)
    plain_right.start()
    fill(left, 0, 3)
    plain_left = remote(send.at[3], got.at[2], rs_send.at[3], rs_recv.at[3], to_left)
    plain_left.start()
    over_right.wait()
    fill(right, 0, 4, 0)
    sum_right = remote(send.at[4], got.at[0], rs_send.at[4], rs_recv.at[4], to_right)
    sum_right.start()
    over_left.wait()
    fill(left, 1, 5, 1)
    sum_left = remote(send.at[5], got.at[3], rs_send.at[5], rs_recv.at[5], to_left)
    sum_left.start()

    for half in range(2):

        @pl.loop(0, FBLK // FT)
        def _(tile, half=half):
            cols, ups, gate, up = partial(b, half, tile)
            own[half, :, cols] = gate
            own[half, :, ups] = up

    for copy in (plain_right, plain_left, sum_right, sum_left):
        copy.wait()

    for half in range(2):

        @pl.loop(0, FBLK // FT)
        def _(tile, half=half):
            cols = pl.ds(pl.multiple_of(tile * FT, FT), FT)
            ups = pl.ds(pl.multiple_of(tile * FT + FBLK, FT), FT)
            gate = (
                own[half, :, cols]
                + got[half, :, cols].astype(jnp.float32)
                + got[2 + half, :, cols].astype(jnp.float32)
            )
            up = (
                own[half, :, ups]
                + got[half, :, ups].astype(jnp.float32)
                + got[2 + half, :, ups].astype(jnp.float32)
            )
            value = gate / (1.0 + jnp.exp(-gate)) * up
            hid[b, half, :, cols] = value.astype(jnp.bfloat16)

    own_right = remote(hid.at[b], hid.at[b], ag_send.at[0], ag_recv.at[0], to_right)
    own_left = remote(hid.at[b], hid.at[b], ag_send.at[1], ag_recv.at[1], to_left)
    own_right.start()
    own_left.start()
    for copy in loads[2 * SIDE :]:
        copy.wait()

    o_copies = {}

    def down(order, group):
        lhs = hid[group].reshape(quarter, FBLK)

        def block(step):
            cols = pl.ds(pl.multiple_of(lax.rem(a + step, SIDE) * DBLK, DBLK), DBLK)
            return lax.dot_general(lhs, wd[cols, :], (((1,), (1,)), ((), ())), preferred_element_type=jnp.float32)

        @pl.loop(1, SIDE)
        def _(step):
            part[order, step - 1] = block(step).astype(jnp.bfloat16)

        for step in (2, 1, 3):
            copy = remote(
                part.at[order, step - 1], part_in.at[order, step - 1],
                o_send.at[order, step - 1], o_recv.at[order, step - 1], peer(shifted(a, step), b),
            )
            copy.start()
            o_copies[order, step] = copy
        part32[order] = block(0)

    def finish(order, group):
        value = part32[order]
        for step in range(1, SIDE):
            o_copies[order, step].wait()
            value = value + part_in[order, step - 1].astype(jnp.float32)
        total[pl.ds(pl.multiple_of(group * quarter, 16), quarter), :] = value.astype(jnp.bfloat16)

    down(0, b)
    own_right.wait()
    on_right = remote(hid.at[left, 0], hid.at[left, 0], ag_send.at[2], ag_recv.at[2], to_right)
    on_right.start()
    own_left.wait()
    on_left = remote(hid.at[right, 1], hid.at[right, 1], ag_send.at[3], ag_recv.at[3], to_left)
    on_left.start()
    down(1, left)
    down(3, right)
    finish(0, b)
    on_right.wait()
    on_left.wait()
    down(2, across)
    finish(1, left)
    finish(3, right)
    finish(2, across)

    if keep < ALL_ROWS:
        place = lax.broadcasted_iota(jnp.int32, (ALL_ROWS, keep), 1)
        pick = (place == at_column[...]).astype(jnp.bfloat16)
        spread = jnp.dot(pick, total[...], preferred_element_type=jnp.float32)
        y_send[...] = spread.astype(jnp.bfloat16).reshape(PIECES, CAP, DBLK)
    else:
        y_send[...] = total[...].reshape(PIECES, CAP, DBLK)

    def source_of(step):
        return lax.rem(grp * 8 + ep + step, PIECES)

    deliver(
        1,
        lambda step: y_send.at[source_of(step)],
        lambda step: y_out.at[ep, :, pl.ds(pl.multiple_of(own_block * DBLK, DBLK), DBLK)],
        lambda step: (lax.div(source_of(step), 8), lax.rem(source_of(step), 8), z_hi),
        y_ssem, y_rsem,
    )
    pltpu.make_async_copy(y_send, y_send, y_ssem.at[0]).wait()
    pltpu.make_async_copy(y_out, y_out, y_rsem.at[0]).wait()


def expert_layer(keep, x_in, w_gate, w_up, w_down, moved, places=()):
    bf16, f32 = jnp.bfloat16, jnp.float32
    dma = pltpu.SemaphoreType.DMA
    quarter, eighth = keep // SIDE, keep // (2 * SIDE)
    scratch = [
        pltpu.VMEM((PIECES, CAP, DBLK), bf16),
        pltpu.VMEM((SIDE, keep, DBLK), bf16),
        pltpu.VMEM((DSET, FBLK), bf16),
        pltpu.VMEM((DSET, FBLK), bf16),
        pltpu.VMEM((DSET, FBLK), bf16),
        pltpu.VMEM((6, eighth, 2 * FBLK), bf16),
        pltpu.VMEM((2, eighth, 2 * FBLK), bf16),
        pltpu.VMEM((4, eighth, 2 * FBLK), bf16),
        pltpu.VMEM((2, eighth, 2 * FBLK), f32),
        pltpu.VMEM((SIDE, 2, eighth, FBLK), bf16),
        pltpu.VMEM((SIDE, SIDE - 1, quarter, DBLK), bf16),
        pltpu.VMEM((SIDE, quarter, DBLK), f32),
        pltpu.VMEM((SIDE, SIDE - 1, quarter, DBLK), bf16),
        pltpu.VMEM((keep, DBLK), bf16),
        pltpu.VMEM((PIECES, CAP, DBLK), bf16),
        dma((3, SIDE)),
        dma((1,)), dma((1,)),
        dma((3,)), dma((3,)),
        dma((6,)), dma((6,)),
        dma((4,)), dma((4,)),
        dma((SIDE, 3)), dma((SIDE, 3)),
        dma((1,)), dma((1,)),
        pltpu.VMEM((CAP, DBLK), bf16),
        pltpu.VMEM((CAP, DBLK), bf16),
    ]
    anywhere = pl.BlockSpec(memory_space=pl.ANY)
    return pl.pallas_call(
        functools.partial(moe_kernel, keep),
        out_shape=jax.ShapeDtypeStruct(x_in.shape, bf16),
        in_specs=[anywhere] * 13 + [pl.BlockSpec(memory_space=pltpu.VMEM)] * len(places),
        out_specs=anywhere,
        scratch_shapes=scratch,
        compiler_params=pltpu.CompilerParams(
            collective_id=keep // 128, has_side_effects=True, vmem_limit_bytes=60 * 1024 * 1024
        ),
        cost_estimate=pl.CostEstimate(
            flops=13 * 10**6 * keep, bytes_accessed=14 * 10**6, transcendentals=10**6
        ),
        name="expert_layer",
    )(x_in, w_gate, w_up, w_down, *moved, *places)


def attend_local(queries, token_key_value, cache, cache_length):
    seq_count = queries.shape[0]
    positions = cache.shape[2]
    heads_kv = cache.shape[3] // HEAD_SIZE
    group_share = QUERY_HEADS // KEY_VALUE_HEADS
    score_scale = HEAD_SIZE ** (-0.5)
    query_head_rows = queries.reshape(seq_count, heads_kv, group_share, HEAD_SIZE)
    stored_keys = cache[:, 0].reshape(seq_count, positions, heads_kv, HEAD_SIZE)
    stored_values = cache[:, 1].reshape(seq_count, positions, heads_kv, HEAD_SIZE)
    incoming_key = token_key_value[:, 0].reshape(seq_count, heads_kv, HEAD_SIZE)
    incoming_value = token_key_value[:, 1].reshape(seq_count, heads_kv, HEAD_SIZE)
    scores = (
        jnp.einsum(
            "skgd,slkd->skgl", query_head_rows, stored_keys, preferred_element_type=jnp.float32
        )
        * score_scale
    )
    in_cache = (
        jnp.arange(positions, dtype=jnp.int32)[None, None, None, :]
        < cache_length[:, None, None, None]
    )
    scores = jnp.where(in_cache, scores, -jnp.inf)
    self_score = (
        jnp.einsum(
            "skgd,skd->skg", query_head_rows, incoming_key, preferred_element_type=jnp.float32
        )
        * score_scale
    )
    highest = jnp.maximum(jnp.max(scores, axis=-1), self_score)
    exponent = jnp.exp(scores - highest[..., None])
    own_exp = jnp.exp(self_score - highest)
    totals = jnp.sum(exponent, axis=-1) + own_exp
    normalized = (exponent / totals[..., None]).astype(jnp.bfloat16)
    own_weight = (own_exp / totals).astype(jnp.bfloat16)
    mixture = jnp.einsum(
        "skgl,slkd->skgd", normalized, stored_values, preferred_element_type=jnp.float32
    )
    mixture = (
        mixture
        + own_weight.astype(jnp.float32)[..., None]
        * incoming_value.astype(jnp.float32)[:, :, None, :]
    )
    return mixture.reshape(seq_count, heads_kv * group_share * HEAD_SIZE).astype(jnp.bfloat16)


def per_device(
    residual,
    queries,
    token_key_value,
    cache,
    cache_length,
    active,
    routes,
    norm_gain,
    router,
    w_gate,
    w_up,
    w_down,
):
    w_gate, w_up, w_down = w_gate[0], w_up[0], w_down[0]
    line_rank = coordinates()[0]
    moved = []
    for weight in (w_gate, w_up, w_down):
        for step in range(1, SIDE):
            column = lax.rem(line_rank + step, SIDE) * FBLK
            piece = lax.dynamic_slice(weight, (0, column), (DBLK, FBLK))
            moved.append(lax.ppermute(piece, MESH_AXES, line_permutation(step)))
    attention_output = attend_local(queries, token_key_value, cache, cache_length)
    state = residual.astype(jnp.float32) + attention_output.astype(jnp.float32)
    scaled = state * norm_gain.astype(jnp.float32)[None, :]
    squares, raw_logits = lax.psum(
        (
            jnp.sum(state * state, axis=1),
            jnp.dot(scaled, router.astype(jnp.float32), precision=lax.Precision.HIGHEST),
        ),
        "tp",
    )
    row_scale = jnp.sqrt(squares / MODEL_WIDTH + EPSILON)[:, None]
    logits = raw_logits / row_scale
    normed = (scaled / row_scale).astype(jnp.bfloat16)
    chosen = jnp.take_along_axis(logits, routes, axis=1)
    weight_first = jax.nn.sigmoid(chosen[:, 0] - chosen[:, 1])
    weight_second = 1.0 - weight_first
    seq_count = residual.shape[0]
    expert_count = router.shape[1]
    slot_total = CAP * expert_count
    still_live = active == 1
    flat_expert = routes.reshape(-1)
    flat_live = jnp.repeat(still_live, 2)
    onehot = (
        (flat_expert[:, None] == jnp.arange(expert_count, dtype=jnp.int32)[None, :])
        & flat_live[:, None]
    ).astype(jnp.int32)
    before = jnp.cumsum(onehot, axis=0) - onehot
    rank_order = jnp.sum(before * onehot, axis=1)
    slot_index = flat_expert * CAP + rank_order
    selector = (
        (
            (slot_index[:, None] == jnp.arange(slot_total, dtype=jnp.int32)[None, :])
            & flat_live[:, None]
        )
        .astype(jnp.bfloat16)
        .reshape(seq_count, 2, slot_total)
    )
    senders = selector[:, 0] + selector[:, 1]
    outgoing = lax.dot_general(
        senders, normed, (((0,), (0,)), ((), ())), preferred_element_type=jnp.float32
    )
    outgoing = outgoing.astype(jnp.bfloat16).reshape(expert_count, CAP, normed.shape[1])
    returned = expert_layer(ALL_ROWS, outgoing, w_gate, w_up, w_down, moved)
    returned = returned.reshape(slot_total, normed.shape[1])
    pick_first = jnp.dot(selector[:, 0], returned, preferred_element_type=jnp.float32)
    pick_second = jnp.dot(selector[:, 1], returned, preferred_element_type=jnp.float32)
    moe_sum = weight_first[:, None] * pick_first + weight_second[:, None] * pick_second
    delta = jnp.where(still_live[:, None], attention_output.astype(jnp.float32) + moe_sum, 0.0)
    return delta.astype(jnp.bfloat16)


def solution(mesh):
    in_specs = (
        P(("grp", "ep"), "tp"),
        P(("grp", "ep"), "tp"),
        P(("grp", "ep"), None, "tp"),
        P(("grp", "ep"), None, None, "tp"),
        P(("grp", "ep")),
        P(("grp", "ep")),
        P(("grp", "ep"), None),
        P("tp"),
        P("tp", None),
        P("ep", ("grp", "tp"), None),
        P("ep", ("grp", "tp"), None),
        P("ep", ("grp", "tp"), None),
    )
    out_specs = P(("grp", "ep"), "tp")
    return jax.shard_map(
        per_device, mesh=mesh, in_specs=in_specs, out_specs=out_specs, check_vma=False
    )
```

```python
import functools

import jax
import jax.numpy as jnp
from jax import lax
from jax.experimental import pallas as pl
from jax.experimental.pallas import tpu as pltpu
from jax.sharding import PartitionSpec as P

MODEL_WIDTH = 4096
QUERY_HEADS = 32
KEY_VALUE_HEADS = 8
HEAD_SIZE = 128


EPSILON = 1e-05

SIDE = 4
DEVICES = 128
CAP = 16
PIECES = 64
ALL_ROWS = PIECES * CAP
CHUNK = 128
SIZES = (512, 640, ALL_ROWS)
DBLK = 256
DSET = SIDE * DBLK
FBLK = 2048
FT = 512
MESH_AXES = ("grp", "ep", "tp")
MESH_ID = pl.DeviceIdType.MESH


def line_permutation(step):
    pairs = []
    for grp in range(8):
        for ep in range(8):
            for tp in range(2):
                x, z = grp % 4, (grp // 4) * 2 + tp
                if ep % 2 == 0:
                    x2, z2 = (x + step) % SIDE, z
                else:
                    x2, z2 = x, (z + step) % SIDE
                pairs.append(((grp * 8 + ep) * 2 + tp, (((z2 // 2) * 4 + x2) * 8 + ep) * 2 + z2 % 2))
    return pairs


def coordinates():
    grp, ep, tp = (lax.axis_index(name) for name in MESH_AXES)
    x = lax.rem(grp, 4)
    z = lax.div(grp, 4) * 2 + tp
    core = lax.rem(ep, 2)
    return x + (z - x) * core, z + (x - z) * core, core, ep


def moe_kernel(
    keep, x_in, w_gate, w_up, w_down, g1, g2, g3, u1, u2, u3, d1, d2, d3, *refs
):
    if keep < ALL_ROWS:
        at_row, at_column, *refs = refs
    (
        y_out, landed, rows, wg, wu, wd, send, fwd, got, own, hid, part, part32, part_in, total, y_send,
        w_sem, x_send, x_recv, xa_send, xa_recv, rs_send, rs_recv, ag_send, ag_recv,
        o_send, o_recv, y_ssem, y_rsem, *spare,
    ) = refs
    quarter, eighth = keep // SIDE, keep // (2 * SIDE)
    a, b, core, ep = coordinates()
    grp, tp = lax.axis_index("grp"), lax.axis_index("tp")
    z_hi = lax.div(grp, 4)
    own_block = lax.rem(grp, 4) * 2 + tp
    itself = (grp * 8 + ep) * 2 + tp

    def peer(at_a, at_b):
        x = at_a + (at_b - at_a) * core
        z = at_b + (at_a - at_b) * core
        return (lax.div(z, 2) * 4 + x, ep, lax.rem(z, 2))

    def shifted(value, by):
        return lax.rem(value + by + SIDE, SIDE)

    def remote(src, dst, ssem, rsem, to):
        return pltpu.make_async_remote_copy(
            src_ref=src, dst_ref=dst, send_sem=ssem, recv_sem=rsem, device_id=to, device_id_type=MESH_ID
        )

    right, left, across = shifted(b, 1), shifted(b, -1), shifted(b, 2)

    loads = []
    for which, (full, parts, dst) in enumerate(
        ((w_gate, (g1, g2, g3), wg), (w_up, (u1, u2, u3), wu), (w_down, (d1, d2, d3), wd))
    ):
        column = pl.ds(pl.multiple_of(a * FBLK, FBLK), FBLK)
        for step in range(SIDE):
            row = pl.ds(pl.multiple_of(shifted(a, -step) * DBLK, DBLK), DBLK)
            src = full.at[:, column] if step == 0 else parts[step - 1]
            copy = pltpu.make_async_copy(src, dst.at[row], w_sem.at[which, step])
            copy.start()
            loads.append(copy)

    barrier = pltpu.get_barrier_semaphore()

    @pl.loop(1, DEVICES)
    def _(step):
        at = lax.rem(itself + step, DEVICES)
        to = (lax.div(at, 16), lax.rem(lax.div(at, 2), 8), lax.rem(at, 2))
        pl.semaphore_signal(barrier, inc=1, device_id=to, device_id_type=MESH_ID)

    pl.semaphore_wait(barrier, DEVICES - 1)

    def deliver(move, src_of, dst_of, to_of, sends, recvs):
        @pl.loop(0, PIECES)
        def _(step):
            to = to_of(step)
            far = (to[0] * 8 + to[1]) * 2 + to[2] != itself

            @pl.when(far)
            def _():
                remote(src_of(step), dst_of(step), sends.at[0], recvs.at[0], to).start()

            @pl.when(jnp.logical_not(far))
            def _():
                pltpu.make_async_copy(src_of(step), dst_of(step), recvs.at[0]).start()
                pltpu.make_async_copy(src_of(step), spare[move], sends.at[0]).start()

    def expert_of(step):
        return lax.rem(ep + lax.div(step, 8), 8)

    def block_of(step):
        return lax.rem(own_block + step, 8)

    deliver(
        0,
        lambda step: x_in.at[expert_of(step), :, pl.ds(pl.multiple_of(block_of(step) * DBLK, DBLK), DBLK)],
        lambda step: landed.at[grp * 8 + ep],
        lambda step: (tp * 4 + lax.div(block_of(step), 2), expert_of(step), lax.rem(block_of(step), 2)),
        x_send, x_recv,
    )
    pltpu.make_async_copy(x_in, x_in, x_send.at[0]).wait()
    pltpu.make_async_copy(landed, landed, x_recv.at[0]).wait()
    if keep < ALL_ROWS:
        @pl.loop(0, keep // CHUNK)
        def _(chunk):
            first = pl.multiple_of(chunk * CHUNK, CHUNK)
            place = lax.broadcasted_iota(jnp.int32, (CHUNK, ALL_ROWS), 0) + first
            pick = jnp.where(place == at_row[...], 1.0, 0.0).astype(jnp.bfloat16)
            packed = jnp.dot(pick, landed[...].reshape(ALL_ROWS, DBLK), preferred_element_type=jnp.float32)
            rows[a, pl.ds(first, CHUNK), :] = packed.astype(jnp.bfloat16)
    else:
        rows[a] = landed[...].reshape(ALL_ROWS, DBLK)

    copies = []
    for step in (2, 1, 3):
        copy = remote(
            rows.at[a], rows.at[a], xa_send.at[step - 1], xa_recv.at[step - 1], peer(shifted(a, step), b)
        )
        copy.start()
        copies.append(copy)
    for copy in loads[: 2 * SIDE]:
        copy.wait()
    for copy in copies:
        copy.wait()

    def partial(group, half, tile):
        first = pl.multiple_of(group * quarter + half * eighth, 16)
        lhs = jnp.concatenate([rows[k, pl.ds(first, eighth), :] for k in range(SIDE)], axis=1)
        cols = pl.ds(pl.multiple_of(tile * FT, FT), FT)
        ups = pl.ds(pl.multiple_of(tile * FT + FBLK, FT), FT)
        gate = jnp.dot(lhs, wg[:, cols], preferred_element_type=jnp.float32)
        up = jnp.dot(lhs, wu[:, cols], preferred_element_type=jnp.float32)
        return cols, ups, gate, up

    def fill(group, half, slot, extra=None):
        @pl.loop(0, FBLK // FT)
        def _(tile):
            cols, ups, gate, up = partial(group, half, tile)
            if extra is not None:
                gate = gate + fwd[extra, :, cols].astype(jnp.float32)
                up = up + fwd[extra, :, ups].astype(jnp.float32)
            send[slot, :, cols] = gate.astype(jnp.bfloat16)
            send[slot, :, ups] = up.astype(jnp.bfloat16)

    to_right, to_left = peer(a, right), peer(a, left)
    fill(across, 0, 0)
    over_right = remote(send.at[0], fwd.at[0], rs_send.at[0], rs_recv.at[0], to_right)
    over_right.start()
    fill(across, 1, 1)
    over_left = remote(send.at[1], fwd.at[1], rs_send.at[1], rs_recv.at[1], to_left)
    over_left.start()
    fill(right, 1, 2)
    plain_right = remote(send.at[2], got.at[1], rs_send.at[2], rs_recv.at[2], to_right)
    plain_right.start()
    fill(left, 0, 3)
    plain_left = remote(send.at[3], got.at[2], rs_send.at[3], rs_recv.at[3], to_left)
    plain_left.start()
    over_right.wait()
    fill(right, 0, 4, 0)
    sum_right = remote(send.at[4], got.at[0], rs_send.at[4], rs_recv.at[4], to_right)
    sum_right.start()
    over_left.wait()
    fill(left, 1, 5, 1)
    sum_left = remote(send.at[5], got.at[3], rs_send.at[5], rs_recv.at[5], to_left)
    sum_left.start()

    for half in range(2):

        @pl.loop(0, FBLK // FT)
        def _(tile, half=half):
            cols, ups, gate, up = partial(b, half, tile)
            own[half, :, cols] = gate
            own[half, :, ups] = up

    for copy in (plain_right, plain_left, sum_right, sum_left):
        copy.wait()

    for half in range(2):

        @pl.loop(0, FBLK // FT)
        def _(tile, half=half):
            cols = pl.ds(pl.multiple_of(tile * FT, FT), FT)
            ups = pl.ds(pl.multiple_of(tile * FT + FBLK, FT), FT)
            gate = (
                own[half, :, cols]
                + got[half, :, cols].astype(jnp.float32)
                + got[2 + half, :, cols].astype(jnp.float32)
            )
            up = (
                own[half, :, ups]
                + got[half, :, ups].astype(jnp.float32)
                + got[2 + half, :, ups].astype(jnp.float32)
            )
            value = gate / (1.0 + jnp.exp(-gate)) * up
            hid[b, half, :, cols] = value.astype(jnp.bfloat16)

    own_right = remote(hid.at[b], hid.at[b], ag_send.at[0], ag_recv.at[0], to_right)
    own_left = remote(hid.at[b], hid.at[b], ag_send.at[1], ag_recv.at[1], to_left)
    own_right.start()
    own_left.start()
    for copy in loads[2 * SIDE :]:
        copy.wait()

    o_copies = {}

    def down(order, group):
        lhs = hid[group].reshape(quarter, FBLK)

        def block(step):
            cols = pl.ds(pl.multiple_of(lax.rem(a + step, SIDE) * DBLK, DBLK), DBLK)
            return lax.dot_general(lhs, wd[cols, :], (((1,), (1,)), ((), ())), preferred_element_type=jnp.float32)

        @pl.loop(1, SIDE)
        def _(step):
            part[order, step - 1] = block(step).astype(jnp.bfloat16)

        for step in (2, 1, 3):
            copy = remote(
                part.at[order, step - 1], part_in.at[order, step - 1],
                o_send.at[order, step - 1], o_recv.at[order, step - 1], peer(shifted(a, step), b),
            )
            copy.start()
            o_copies[order, step] = copy
        part32[order] = block(0)

    def finish(order, group):
        value = part32[order]
        for step in range(1, SIDE):
            o_copies[order, step].wait()
            value = value + part_in[order, step - 1].astype(jnp.float32)
        total[pl.ds(pl.multiple_of(group * quarter, 16), quarter), :] = value.astype(jnp.bfloat16)

    down(0, b)
    own_right.wait()
    on_right = remote(hid.at[left, 0], hid.at[left, 0], ag_send.at[2], ag_recv.at[2], to_right)
    on_right.start()
    own_left.wait()
    on_left = remote(hid.at[right, 1], hid.at[right, 1], ag_send.at[3], ag_recv.at[3], to_left)
    on_left.start()
    down(1, left)
    down(3, right)
    finish(0, b)
    on_right.wait()
    on_left.wait()
    down(2, across)
    finish(1, left)
    finish(3, right)
    finish(2, across)

    if keep < ALL_ROWS:
        @pl.loop(0, ALL_ROWS // CHUNK)
        def _(chunk):
            place = lax.broadcasted_iota(jnp.int32, (CHUNK, keep), 1)
            at = at_column[pl.ds(pl.multiple_of(chunk * CHUNK, CHUNK), CHUNK), :]
            pick = jnp.where(place == at, 1.0, 0.0).astype(jnp.bfloat16)
            spread = jnp.dot(pick, total[...], preferred_element_type=jnp.float32)
            first = pl.multiple_of(chunk * (CHUNK // CAP), CHUNK // CAP)
            y_send[pl.ds(first, CHUNK // CAP)] = spread.astype(jnp.bfloat16).reshape(CHUNK // CAP, CAP, DBLK)
    else:
        y_send[...] = total[...].reshape(PIECES, CAP, DBLK)

    def source_of(step):
        return lax.rem(grp * 8 + ep + step, PIECES)

    deliver(
        1,
        lambda step: y_send.at[source_of(step)],
        lambda step: y_out.at[ep, :, pl.ds(pl.multiple_of(own_block * DBLK, DBLK), DBLK)],
        lambda step: (lax.div(source_of(step), 8), lax.rem(source_of(step), 8), z_hi),
        y_ssem, y_rsem,
    )
    pltpu.make_async_copy(y_send, y_send, y_ssem.at[0]).wait()
    pltpu.make_async_copy(y_out, y_out, y_rsem.at[0]).wait()


def expert_layer(keep, x_in, w_gate, w_up, w_down, moved, places=()):
    bf16, f32 = jnp.bfloat16, jnp.float32
    dma = pltpu.SemaphoreType.DMA
    quarter, eighth = keep // SIDE, keep // (2 * SIDE)
    scratch = [
        pltpu.VMEM((PIECES, CAP, DBLK), bf16),
        pltpu.VMEM((SIDE, keep, DBLK), bf16),
        pltpu.VMEM((DSET, FBLK), bf16),
        pltpu.VMEM((DSET, FBLK), bf16),
        pltpu.VMEM((DSET, FBLK), bf16),
        pltpu.VMEM((6, eighth, 2 * FBLK), bf16),
        pltpu.VMEM((2, eighth, 2 * FBLK), bf16),
        pltpu.VMEM((4, eighth, 2 * FBLK), bf16),
        pltpu.VMEM((2, eighth, 2 * FBLK), f32),
        pltpu.VMEM((SIDE, 2, eighth, FBLK), bf16),
        pltpu.VMEM((SIDE, SIDE - 1, quarter, DBLK), bf16),
        pltpu.VMEM((SIDE, quarter, DBLK), f32),
        pltpu.VMEM((SIDE, SIDE - 1, quarter, DBLK), bf16),
        pltpu.VMEM((keep, DBLK), bf16),
        pltpu.VMEM((PIECES, CAP, DBLK), bf16),
        dma((3, SIDE)),
        dma((1,)), dma((1,)),
        dma((3,)), dma((3,)),
        dma((6,)), dma((6,)),
        dma((4,)), dma((4,)),
        dma((SIDE, 3)), dma((SIDE, 3)),
        dma((1,)), dma((1,)),
        pltpu.VMEM((CAP, DBLK), bf16),
        pltpu.VMEM((CAP, DBLK), bf16),
    ]
    anywhere = pl.BlockSpec(memory_space=pl.ANY)
    return pl.pallas_call(
        functools.partial(moe_kernel, keep),
        out_shape=jax.ShapeDtypeStruct(x_in.shape, bf16),
        in_specs=[anywhere] * 13 + [pl.BlockSpec(memory_space=pltpu.VMEM)] * len(places),
        out_specs=anywhere,
        scratch_shapes=scratch,
        compiler_params=pltpu.CompilerParams(
            collective_id=keep // 128, has_side_effects=True, vmem_limit_bytes=60 * 1024 * 1024
        ),
        cost_estimate=pl.CostEstimate(
            flops=13 * 10**6 * keep, bytes_accessed=14 * 10**6, transcendentals=10**6
        ),
        name="expert_layer",
    )(x_in, w_gate, w_up, w_down, *moved, *places)


def attend_local(queries, token_key_value, cache, cache_length):
    seq_count = queries.shape[0]
    positions = cache.shape[2]
    heads_kv = cache.shape[3] // HEAD_SIZE
    group_share = QUERY_HEADS // KEY_VALUE_HEADS
    score_scale = HEAD_SIZE ** (-0.5)
    query_head_rows = queries.reshape(seq_count, heads_kv, group_share, HEAD_SIZE)
    stored_keys = cache[:, 0].reshape(seq_count, positions, heads_kv, HEAD_SIZE)
    stored_values = cache[:, 1].reshape(seq_count, positions, heads_kv, HEAD_SIZE)
    incoming_key = token_key_value[:, 0].reshape(seq_count, heads_kv, HEAD_SIZE)
    incoming_value = token_key_value[:, 1].reshape(seq_count, heads_kv, HEAD_SIZE)
    scores = (
        jnp.einsum(
            "skgd,slkd->skgl", query_head_rows, stored_keys, preferred_element_type=jnp.float32
        )
        * score_scale
    )
    in_cache = (
        jnp.arange(positions, dtype=jnp.int32)[None, None, None, :]
        < cache_length[:, None, None, None]
    )
    scores = jnp.where(in_cache, scores, -jnp.inf)
    self_score = (
        jnp.einsum(
            "skgd,skd->skg", query_head_rows, incoming_key, preferred_element_type=jnp.float32
        )
        * score_scale
    )
    highest = jnp.maximum(jnp.max(scores, axis=-1), self_score)
    exponent = jnp.exp(scores - highest[..., None])
    own_exp = jnp.exp(self_score - highest)
    totals = jnp.sum(exponent, axis=-1) + own_exp
    normalized = (exponent / totals[..., None]).astype(jnp.bfloat16)
    own_weight = (own_exp / totals).astype(jnp.bfloat16)
    mixture = jnp.einsum(
        "skgl,slkd->skgd", normalized, stored_values, preferred_element_type=jnp.float32
    )
    mixture = (
        mixture
        + own_weight.astype(jnp.float32)[..., None]
        * incoming_value.astype(jnp.float32)[:, :, None, :]
    )
    return mixture.reshape(seq_count, heads_kv * group_share * HEAD_SIZE).astype(jnp.bfloat16)


def per_device(
    residual,
    queries,
    token_key_value,
    cache,
    cache_length,
    active,
    routes,
    norm_gain,
    router,
    w_gate,
    w_up,
    w_down,
):
    w_gate, w_up, w_down = w_gate[0], w_up[0], w_down[0]
    line_rank = coordinates()[0]
    moved = []
    for weight in (w_gate, w_up, w_down):
        for step in range(1, SIDE):
            column = lax.rem(line_rank + step, SIDE) * FBLK
            piece = lax.dynamic_slice(weight, (0, column), (DBLK, FBLK))
            moved.append(lax.ppermute(piece, MESH_AXES, line_permutation(step)))
    attention_output = attend_local(queries, token_key_value, cache, cache_length)
    state = residual.astype(jnp.float32) + attention_output.astype(jnp.float32)
    scaled = state * norm_gain.astype(jnp.float32)[None, :]
    squares, raw_logits = lax.psum(
        (
            jnp.sum(state * state, axis=1),
            jnp.dot(scaled, router.astype(jnp.float32), precision=lax.Precision.HIGHEST),
        ),
        "tp",
    )
    row_scale = jnp.sqrt(squares / MODEL_WIDTH + EPSILON)[:, None]
    logits = raw_logits / row_scale
    normed = (scaled / row_scale).astype(jnp.bfloat16)
    chosen = jnp.take_along_axis(logits, routes, axis=1)
    weight_first = jax.nn.sigmoid(chosen[:, 0] - chosen[:, 1])
    weight_second = 1.0 - weight_first
    seq_count = residual.shape[0]
    expert_count = router.shape[1]
    slot_total = CAP * expert_count
    still_live = active == 1
    flat_expert = routes.reshape(-1)
    flat_live = jnp.repeat(still_live, 2)
    onehot = (
        (flat_expert[:, None] == jnp.arange(expert_count, dtype=jnp.int32)[None, :])
        & flat_live[:, None]
    ).astype(jnp.int32)
    before = jnp.cumsum(onehot, axis=0) - onehot
    rank_order = jnp.sum(before * onehot, axis=1)
    slot_index = flat_expert * CAP + rank_order
    selector = (
        (
            (slot_index[:, None] == jnp.arange(slot_total, dtype=jnp.int32)[None, :])
            & flat_live[:, None]
        )
        .astype(jnp.bfloat16)
        .reshape(seq_count, 2, slot_total)
    )
    senders = selector[:, 0] + selector[:, 1]
    outgoing = lax.dot_general(
        senders, normed, (((0,), (0,)), ((), ())), preferred_element_type=jnp.float32
    )
    outgoing = outgoing.astype(jnp.bfloat16).reshape(expert_count, CAP, normed.shape[1])
    source = lax.axis_index("grp") * 8 + lax.axis_index("ep")
    mine = jnp.arange(PIECES, dtype=jnp.int32)[:, None] == source
    counts = jnp.where(mine, jnp.sum(onehot, axis=0).astype(jnp.float32)[None, :] * 0.5, 0.0)
    counts = lax.psum(counts, MESH_AXES).astype(jnp.int32)
    largest = jnp.max(jnp.sum(counts, axis=0))
    here = jnp.sum(jnp.where(jnp.arange(expert_count) == lax.axis_index("ep"), counts, 0), axis=1)
    index = jnp.arange(PIECES, dtype=jnp.int32)
    start = jnp.sum(jnp.where(index[:, None] > index[None, :], here[None, :], 0), axis=1)
    spot = jnp.arange(CAP, dtype=jnp.int32)[None, :]
    places = jnp.where(spot < here[:, None], start[:, None] + spot, -1)
    views = lax.optimization_barrier((places.reshape(1, ALL_ROWS), places.reshape(ALL_ROWS, 1)))
    branches = [
        functools.partial(lambda keep, views, *args: expert_layer(keep, *args, views[: 2 * (keep < ALL_ROWS)]), keep)
        for keep in SIZES
    ]
    choice = sum((largest > keep).astype(jnp.int32) for keep in SIZES[:-1])
    returned = lax.switch(choice, branches, views, outgoing, w_gate, w_up, w_down, moved)
    returned = returned.reshape(slot_total, normed.shape[1])
    pick_first = jnp.dot(selector[:, 0], returned, preferred_element_type=jnp.float32)
    pick_second = jnp.dot(selector[:, 1], returned, preferred_element_type=jnp.float32)
    moe_sum = weight_first[:, None] * pick_first + weight_second[:, None] * pick_second
    delta = jnp.where(still_live[:, None], attention_output.astype(jnp.float32) + moe_sum, 0.0)
    return delta.astype(jnp.bfloat16)


def solution(mesh):
    in_specs = (
        P(("grp", "ep"), "tp"),
        P(("grp", "ep"), "tp"),
        P(("grp", "ep"), None, "tp"),
        P(("grp", "ep"), None, None, "tp"),
        P(("grp", "ep")),
        P(("grp", "ep")),
        P(("grp", "ep"), None),
        P("tp"),
        P("tp", None),
        P("ep", ("grp", "tp"), None),
        P("ep", ("grp", "tp"), None),
        P("ep", ("grp", "tp"), None),
    )
    out_specs = P(("grp", "ep"), "tp")
    return jax.shard_map(
        per_device, mesh=mesh, in_specs=in_specs, out_specs=out_specs, check_vma=False
    )
```

```python
import functools

import jax
import jax.numpy as jnp
from jax import lax
from jax.experimental import pallas as pl
from jax.experimental.pallas import tpu as pltpu
from jax.sharding import PartitionSpec as P

MODEL_WIDTH = 4096
QUERY_HEADS = 32
KEY_VALUE_HEADS = 8
HEAD_SIZE = 128


EPSILON = 1e-05

SIDE = 4
DEVICES = 128
CAP = 16
PIECES = 64
ALL_ROWS = PIECES * CAP
CHUNK = 128
SEQS = 4
SIZES = (512, 576, 704, ALL_ROWS)
DBLK = 256
DSET = SIDE * DBLK
FBLK = 2048
FT = 512
MESH_AXES = ("grp", "ep", "tp")
MESH_ID = pl.DeviceIdType.MESH


def line_permutation(step):
    pairs = []
    for grp in range(8):
        for ep in range(8):
            for tp in range(2):
                x, z = grp % 4, (grp // 4) * 2 + tp
                if ep % 2 == 0:
                    x2, z2 = (x + step) % SIDE, z
                else:
                    x2, z2 = x, (z + step) % SIDE
                pairs.append(((grp * 8 + ep) * 2 + tp, (((z2 // 2) * 4 + x2) * 8 + ep) * 2 + z2 % 2))
    return pairs


def coordinates():
    grp, ep, tp = (lax.axis_index(name) for name in MESH_AXES)
    x = lax.rem(grp, 4)
    z = lax.div(grp, 4) * 2 + tp
    core = lax.rem(ep, 2)
    return x + (z - x) * core, z + (x - z) * core, core, ep


def parts_of(keep):
    quarter = keep // SIDE
    upper = (quarter + 31) // 32 * 16
    return quarter, upper, quarter - upper


def count_kernel(mine, counts, spare, send_sem, recv_sem):
    grp, ep, tp = (lax.axis_index(name) for name in MESH_AXES)
    source = grp * 8 + ep

    def device(step):
        at = lax.rem(source + step, PIECES)
        return (lax.div(at, 8), lax.rem(at, 8), tp)

    barrier = pltpu.get_barrier_semaphore()

    @pl.loop(1, PIECES)
    def _(step):
        pl.semaphore_signal(barrier, inc=1, device_id=device(step), device_id_type=MESH_ID)

    pl.semaphore_wait(barrier, PIECES - 1)

    @pl.loop(1, PIECES)
    def _(step):
        pltpu.make_async_remote_copy(
            src_ref=mine, dst_ref=counts.at[source], send_sem=send_sem.at[0], recv_sem=recv_sem.at[0],
            device_id=device(step), device_id_type=MESH_ID,
        ).start()

    pltpu.make_async_copy(mine, counts.at[source], recv_sem.at[0]).start()
    pltpu.make_async_copy(mine, spare, send_sem.at[0]).start()
    pltpu.make_async_copy(counts, counts, send_sem.at[0]).wait()
    pltpu.make_async_copy(counts, counts, recv_sem.at[0]).wait()


def exchange_counts(mine):
    in_vmem = pl.BlockSpec(memory_space=pltpu.VMEM)
    dma = pltpu.SemaphoreType.DMA
    return pl.pallas_call(
        count_kernel,
        out_shape=jax.ShapeDtypeStruct((PIECES, 1, 128), jnp.float32),
        in_specs=[in_vmem],
        out_specs=in_vmem,
        scratch_shapes=[pltpu.VMEM((1, 128), jnp.float32), dma((1,)), dma((1,))],
        compiler_params=pltpu.CompilerParams(collective_id=1, has_side_effects=True),
        name="exchange_counts",
    )(mine)


def moe_kernel(
    keep, x_in, w_gate, w_up, w_down, g1, g2, g3, u1, u2, u3, *refs
):
    if keep < ALL_ROWS:
        at_row, at_column, *refs = refs
    (
        y_out, landed, rows, wg, wu, wd, send, fwd, got, raw, own, hid, part, part32, part_in, total, y_send,
        w_sem, x_send, x_recv, xa_send, xa_recv, rs_send, rs_recv, ag_send, ag_recv,
        o_send, o_recv, y_ssem, y_rsem, d_send, d_recv, *spare,
    ) = refs
    quarter, upper, lower = parts_of(keep)
    a, b, core, ep = coordinates()
    grp, tp = lax.axis_index("grp"), lax.axis_index("tp")
    z_hi = lax.div(grp, 4)
    own_block = lax.rem(grp, 4) * 2 + tp
    itself = (grp * 8 + ep) * 2 + tp

    def peer(at_a, at_b):
        x = at_a + (at_b - at_a) * core
        z = at_b + (at_a - at_b) * core
        return (lax.div(z, 2) * 4 + x, ep, lax.rem(z, 2))

    def shifted(value, by):
        return lax.rem(value + by + SIDE, SIDE)

    def remote(src, dst, ssem, rsem, to):
        return pltpu.make_async_remote_copy(
            src_ref=src, dst_ref=dst, send_sem=ssem, recv_sem=rsem, device_id=to, device_id_type=MESH_ID
        )

    right, left, across = shifted(b, 1), shifted(b, -1), shifted(b, 2)

    loads = []
    for which, (full, parts, dst) in enumerate(
        ((w_gate, (g1, g2, g3), wg), (w_up, (u1, u2, u3), wu), (w_down, (), wd))
    ):
        column = pl.ds(pl.multiple_of(a * FBLK, FBLK), FBLK)
        for step in range(len(parts) + 1):
            row = pl.ds(pl.multiple_of(shifted(a, -step) * DBLK, DBLK), DBLK)
            src = full.at[:, column] if step == 0 else parts[step - 1]
            copy = pltpu.make_async_copy(src, dst.at[row], w_sem.at[which, step])
            copy.start()
            loads.append(copy)

    barrier = pltpu.get_barrier_semaphore()

    @pl.loop(1, DEVICES)
    def _(step):
        at = lax.rem(itself + step, DEVICES)
        to = (lax.div(at, 16), lax.rem(lax.div(at, 2), 8), lax.rem(at, 2))
        pl.semaphore_signal(barrier, inc=1, device_id=to, device_id_type=MESH_ID)

    pl.semaphore_wait(barrier, DEVICES - 1)

    def deliver(move, src_of, dst_of, to_of, sends, recvs):
        @pl.loop(0, PIECES)
        def _(step):
            to = to_of(step)
            far = (to[0] * 8 + to[1]) * 2 + to[2] != itself

            @pl.when(far)
            def _():
                remote(src_of(step), dst_of(step), sends.at[0], recvs.at[0], to).start()

            @pl.when(jnp.logical_not(far))
            def _():
                pltpu.make_async_copy(src_of(step), dst_of(step), recvs.at[0]).start()
                pltpu.make_async_copy(src_of(step), spare[move], sends.at[0]).start()

    def expert_of(step):
        return lax.rem(ep + lax.div(step, 8), 8)

    def block_of(step):
        return lax.rem(own_block + step, 8)

    deliver(
        0,
        lambda step: x_in.at[expert_of(step), :, pl.ds(pl.multiple_of(block_of(step) * DBLK, DBLK), DBLK)],
        lambda step: landed.at[grp * 8 + ep],
        lambda step: (tp * 4 + lax.div(block_of(step), 2), expert_of(step), lax.rem(block_of(step), 2)),
        x_send, x_recv,
    )

    def send_down(which, step):
        at = shifted(a, step)
        begin, count = ((0, 128), (0, 128), (128, 128), (128, 128), (0, 256))[which]
        copy = remote(
            w_down.at[pl.ds(begin, count), pl.ds(pl.multiple_of(at * FBLK, FBLK), FBLK)],
            wd.at[pl.ds(pl.multiple_of(a * DBLK + begin, 128), count)],
            d_send.at[which], d_recv.at[which], peer(at, b),
        )
        copy.start()
        loads.append(copy)

    for which, step in ((0, 1), (1, 3)):
        send_down(which, step)
    pltpu.make_async_copy(x_in, x_in, x_send.at[0]).wait()
    pltpu.make_async_copy(landed, landed, x_recv.at[0]).wait()
    if keep < ALL_ROWS:
        @pl.loop(0, SIDE)
        def _(chunk):
            first = pl.multiple_of(chunk * quarter, 16)
            place = lax.broadcasted_iota(jnp.int32, (quarter, ALL_ROWS), 0) + first
            pick = jnp.where(place == at_row[...], 1.0, 0.0).astype(jnp.bfloat16)
            packed = jnp.dot(pick, landed[...].reshape(ALL_ROWS, DBLK), preferred_element_type=jnp.float32)
            rows[a, pl.ds(first, quarter), :] = packed.astype(jnp.bfloat16)
    else:
        rows[a] = landed[...].reshape(ALL_ROWS, DBLK)

    copies = []
    for step in (2, 1, 3):
        copy = remote(
            rows.at[a], rows.at[a], xa_send.at[step - 1], xa_recv.at[step - 1], peer(shifted(a, step), b)
        )
        copy.start()
        copies.append(copy)
    for which, step in ((2, 1), (3, 3), (4, 2)):
        send_down(which, step)
    for copy in loads[: 2 * SIDE]:
        copy.wait()
    for copy in copies:
        copy.wait()

    def product(group, store):
        first = pl.multiple_of(group * quarter, 16)

        @pl.loop(0, FBLK // FT)
        def _(tile):
            lhs = jnp.concatenate([rows[k, pl.ds(first, quarter), :] for k in range(SIDE)], axis=1)
            for part_index, weight in enumerate((wg, wu)):
                cols = pl.ds(pl.multiple_of(tile * FT, FT), FT)
                to = pl.ds(pl.multiple_of(tile * FT + part_index * FBLK, FT), FT)
                value = jnp.dot(lhs, weight[:, cols], preferred_element_type=jnp.float32)
                store(to, value[:upper], value[upper:])

    def store_across(to, top, bottom):
        send[0, :, to] = top.astype(jnp.bfloat16)
        send[1, :lower, to] = bottom.astype(jnp.bfloat16)

    def store_right(to, top, bottom):
        raw[0, :, to] = top
        send[2, :lower, to] = bottom.astype(jnp.bfloat16)

    def store_left(to, top, bottom):
        send[3, :, to] = top.astype(jnp.bfloat16)
        raw[1, :lower, to] = bottom

    def store_own(to, top, bottom):
        own[:upper, to] = top
        own[upper:, to] = bottom

    def add_arrived(slot, which, count):
        @pl.loop(0, 2 * FBLK // FT)
        def _(tile):
            to = pl.ds(pl.multiple_of(tile * FT, FT), FT)
            value = raw[which, :count, to] + fwd[which, :count, to].astype(jnp.float32)
            send[slot, :count, to] = value.astype(jnp.bfloat16)

    def pass_on(slot, count, dst, to):
        copy = remote(send.at[slot, pl.ds(0, count)], dst.at[pl.ds(0, count)], rs_send.at[slot], rs_recv.at[slot], to)
        copy.start()
        return copy

    to_right, to_left = peer(a, right), peer(a, left)
    product(across, store_across)
    over_right = pass_on(0, upper, fwd.at[0], to_right)
    over_left = pass_on(1, lower, fwd.at[1], to_left)
    product(right, store_right)
    plain_right = pass_on(2, lower, got.at[1], to_right)
    product(left, store_left)
    plain_left = pass_on(3, upper, got.at[2], to_left)
    product(b, store_own)
    over_right.wait()
    add_arrived(4, 0, upper)
    sum_right = pass_on(4, upper, got.at[0], to_right)
    over_left.wait()
    add_arrived(5, 1, lower)
    sum_left = pass_on(5, lower, got.at[3], to_left)

    for copy in (plain_right, plain_left, sum_right, sum_left):
        copy.wait()

    @pl.loop(0, FBLK // FT)
    def _(tile):
        cols = pl.ds(pl.multiple_of(tile * FT, FT), FT)
        ups = pl.ds(pl.multiple_of(tile * FT + FBLK, FT), FT)
        for half, (begin, count) in enumerate(((0, upper), (upper, lower))):

            def whole(which):
                return (
                    own[begin : begin + count, which]
                    + got[half, :count, which].astype(jnp.float32)
                    + got[2 + half, :count, which].astype(jnp.float32)
                )

            gate, up = whole(cols), whole(ups)
            hid[b, begin : begin + count, cols] = (gate / (1.0 + jnp.exp(-gate)) * up).astype(jnp.bfloat16)

    own_right = remote(hid.at[b], hid.at[b], ag_send.at[0], ag_recv.at[0], to_right)
    own_left = remote(hid.at[b], hid.at[b], ag_send.at[1], ag_recv.at[1], to_left)
    own_right.start()
    own_left.start()
    for copy in loads[2 * SIDE :]:
        copy.wait()

    o_copies = {}

    def down(order, group):
        lhs = hid[group]

        def block(step):
            cols = pl.ds(pl.multiple_of(lax.rem(a + step, SIDE) * DBLK, DBLK), DBLK)
            return lax.dot_general(lhs, wd[cols, :], (((1,), (1,)), ((), ())), preferred_element_type=jnp.float32)

        @pl.loop(1, SIDE)
        def _(step):
            part[order, step - 1] = block(step).astype(jnp.bfloat16)

        for step in (2, 1, 3):
            copy = remote(
                part.at[order, step - 1], part_in.at[order, step - 1],
                o_send.at[order, step - 1], o_recv.at[order, step - 1], peer(shifted(a, step), b),
            )
            copy.start()
            o_copies[order, step] = copy
        part32[order] = block(0)

    def finish(order, group):
        value = part32[order]
        for step in range(1, SIDE):
            o_copies[order, step].wait()
            value = value + part_in[order, step - 1].astype(jnp.float32)
        total[pl.ds(pl.multiple_of(group * quarter, 16), quarter), :] = value.astype(jnp.bfloat16)

    down(0, b)
    own_right.wait()
    top, bottom = pl.ds(0, upper), pl.ds(upper, lower)
    on_right = remote(hid.at[left, top], hid.at[left, top], ag_send.at[2], ag_recv.at[2], to_right)
    on_right.start()
    own_left.wait()
    on_left = remote(hid.at[right, bottom], hid.at[right, bottom], ag_send.at[3], ag_recv.at[3], to_left)
    on_left.start()
    down(1, left)
    down(3, right)
    finish(0, b)
    on_right.wait()
    on_left.wait()
    down(2, across)
    finish(1, left)
    finish(3, right)
    finish(2, across)

    if keep < ALL_ROWS:
        @pl.loop(0, ALL_ROWS // CHUNK)
        def _(chunk):
            place = lax.broadcasted_iota(jnp.int32, (CHUNK, keep), 1)
            at = at_column[pl.ds(pl.multiple_of(chunk * CHUNK, CHUNK), CHUNK), :]
            pick = jnp.where(place == at, 1.0, 0.0).astype(jnp.bfloat16)
            spread = jnp.dot(pick, total[...], preferred_element_type=jnp.float32)
            first = pl.multiple_of(chunk * (CHUNK // CAP), CHUNK // CAP)
            y_send[pl.ds(first, CHUNK // CAP)] = spread.astype(jnp.bfloat16).reshape(CHUNK // CAP, CAP, DBLK)
    else:
        y_send[...] = total[...].reshape(PIECES, CAP, DBLK)

    def source_of(step):
        return lax.rem(grp * 8 + ep + step, PIECES)

    deliver(
        1,
        lambda step: y_send.at[source_of(step)],
        lambda step: y_out.at[ep, :, pl.ds(pl.multiple_of(own_block * DBLK, DBLK), DBLK)],
        lambda step: (lax.div(source_of(step), 8), lax.rem(source_of(step), 8), z_hi),
        y_ssem, y_rsem,
    )
    pltpu.make_async_copy(y_send, y_send, y_ssem.at[0]).wait()
    pltpu.make_async_copy(y_out, y_out, y_rsem.at[0]).wait()


def expert_layer(keep, x_in, w_gate, w_up, w_down, moved, places=()):
    bf16, f32 = jnp.bfloat16, jnp.float32
    dma = pltpu.SemaphoreType.DMA
    quarter, upper, _ = parts_of(keep)
    scratch = [
        pltpu.VMEM((PIECES, CAP, DBLK), bf16),
        pltpu.VMEM((SIDE, keep, DBLK), bf16),
        pltpu.VMEM((DSET, FBLK), bf16),
        pltpu.VMEM((DSET, FBLK), bf16),
        pltpu.VMEM((DSET, FBLK), bf16),
        pltpu.VMEM((6, upper, 2 * FBLK), bf16),
        pltpu.VMEM((2, upper, 2 * FBLK), bf16),
        pltpu.VMEM((4, upper, 2 * FBLK), bf16),
        pltpu.VMEM((2, upper, 2 * FBLK), f32),
        pltpu.VMEM((quarter, 2 * FBLK), f32),
        pltpu.VMEM((SIDE, quarter, FBLK), bf16),
        pltpu.VMEM((SIDE, SIDE - 1, quarter, DBLK), bf16),
        pltpu.VMEM((SIDE, quarter, DBLK), f32),
        pltpu.VMEM((SIDE, SIDE - 1, quarter, DBLK), bf16),
        pltpu.VMEM((keep, DBLK), bf16),
        pltpu.VMEM((PIECES, CAP, DBLK), bf16),
        dma((3, SIDE)),
        dma((1,)), dma((1,)),
        dma((3,)), dma((3,)),
        dma((6,)), dma((6,)),
        dma((4,)), dma((4,)),
        dma((SIDE, 3)), dma((SIDE, 3)),
        dma((1,)), dma((1,)),
        dma((5,)), dma((5,)),
        pltpu.VMEM((CAP, DBLK), bf16),
        pltpu.VMEM((CAP, DBLK), bf16),
    ]
    anywhere = pl.BlockSpec(memory_space=pl.ANY)
    return pl.pallas_call(
        functools.partial(moe_kernel, keep),
        out_shape=jax.ShapeDtypeStruct(x_in.shape, bf16),
        in_specs=[anywhere] * 10 + [pl.BlockSpec(memory_space=pltpu.VMEM)] * len(places),
        out_specs=anywhere,
        scratch_shapes=scratch,
        compiler_params=pltpu.CompilerParams(
            collective_id=keep // 64, has_side_effects=True, vmem_limit_bytes=60 * 1024 * 1024
        ),
        cost_estimate=pl.CostEstimate(
            flops=13 * 10**6 * keep, bytes_accessed=14 * 10**6, transcendentals=10**6
        ),
        name="expert_layer",
    )(x_in, w_gate, w_up, w_down, *moved, *places)


def attend_kernel(lengths, queries, token_key_value, cache, attended):
    step = pl.program_id(0)
    share = QUERY_HEADS // KEY_VALUE_HEADS
    heads = queries.shape[1]
    width = cache.shape[3]
    score_scale = HEAD_SIZE ** (-0.5)
    head = lax.broadcasted_iota(jnp.int32, (heads, width), 0)
    column = lax.broadcasted_iota(jnp.int32, (heads, width), 1)
    matches = lax.div(head, share) == lax.div(column, HEAD_SIZE)
    position = lax.broadcasted_iota(jnp.int32, (heads, cache.shape[2]), 1)

    def own_part(wide):
        wide = jnp.where(matches, wide, 0.0)
        return sum(wide[:, k * HEAD_SIZE : (k + 1) * HEAD_SIZE] for k in range(width // HEAD_SIZE))

    for i in range(SEQS):
        query = queries[i].astype(jnp.float32)
        query = jnp.where(matches, jnp.concatenate([query] * (width // HEAD_SIZE), axis=1), 0.0)
        new = token_key_value[i].astype(jnp.float32)
        scores = lax.dot_general(
            query.astype(jnp.bfloat16), cache[i, 0], (((1,), (1,)), ((), ())), preferred_element_type=jnp.float32
        )
        scores = jnp.where(position < lengths[step * SEQS + i], scores * score_scale, -jnp.inf)
        self_score = jnp.sum(query * new[0:1, :], axis=1, keepdims=True) * score_scale
        highest = jnp.maximum(jnp.max(scores, axis=1, keepdims=True), self_score)
        exponent = jnp.exp(scores - highest)
        own_exp = jnp.exp(self_score - highest)
        totals = jnp.sum(exponent, axis=1, keepdims=True) + own_exp
        normalized = (exponent / totals).astype(jnp.bfloat16)
        own_weight = (own_exp / totals).astype(jnp.bfloat16).astype(jnp.float32)
        mixture = jnp.dot(normalized, cache[i, 1], preferred_element_type=jnp.float32)
        mixture = own_part(mixture) + own_weight * own_part(jnp.broadcast_to(new[1:2, :], (heads, width)))
        attended[i] = mixture.astype(jnp.bfloat16)


def attend_local(queries, token_key_value, cache, cache_length):
    seq_count, _, positions, width = cache.shape
    heads = queries.shape[1] // HEAD_SIZE
    attended = pl.pallas_call(
        attend_kernel,
        out_shape=jax.ShapeDtypeStruct((seq_count, heads, HEAD_SIZE), jnp.bfloat16),
        grid_spec=pltpu.PrefetchScalarGridSpec(
            num_scalar_prefetch=1,
            grid=(seq_count // SEQS,),
            in_specs=[
                pl.BlockSpec((SEQS, heads, HEAD_SIZE), lambda i, _: (i, 0, 0)),
                pl.BlockSpec((SEQS, 2, width), lambda i, _: (i, 0, 0)),
                pl.BlockSpec((SEQS, 2, positions, width), lambda i, _: (i, 0, 0, 0)),
            ],
            out_specs=pl.BlockSpec((SEQS, heads, HEAD_SIZE), lambda i, _: (i, 0, 0)),
        ),
        cost_estimate=pl.CostEstimate(
            flops=4 * seq_count * heads * positions * width,
            bytes_accessed=2 * cache.size,
            transcendentals=seq_count * heads * positions,
        ),
        name="attention",
    )(cache_length, queries.reshape(seq_count, heads, HEAD_SIZE), token_key_value, cache)
    return attended.reshape(seq_count, heads * HEAD_SIZE)


def per_device(
    residual,
    queries,
    token_key_value,
    cache,
    cache_length,
    active,
    routes,
    norm_gain,
    router,
    w_gate,
    w_up,
    w_down,
):
    seq_count = residual.shape[0]
    expert_count = router.shape[1]
    slot_total = CAP * expert_count
    still_live = active == 1
    flat_expert = routes.reshape(-1)
    flat_live = jnp.repeat(still_live, 2)
    onehot = (
        (flat_expert[:, None] == jnp.arange(expert_count, dtype=jnp.int32)[None, :])
        & flat_live[:, None]
    ).astype(jnp.int32)
    before = jnp.cumsum(onehot, axis=0) - onehot
    rank_order = jnp.sum(before * onehot, axis=1)
    slot_index = flat_expert * CAP + rank_order
    mine = jnp.pad(jnp.sum(onehot, axis=0).astype(jnp.float32), (0, 128 - expert_count))
    counts = exchange_counts(mine.reshape(1, 128)).reshape(PIECES, 128)[:, :expert_count].astype(jnp.int32)
    largest = jnp.max(jnp.sum(counts, axis=0))
    here = jnp.sum(jnp.where(jnp.arange(expert_count) == lax.axis_index("ep"), counts, 0), axis=1)
    index = jnp.arange(PIECES, dtype=jnp.int32)
    start = jnp.sum(jnp.where(index[:, None] > index[None, :], here[None, :], 0), axis=1)
    spot = jnp.arange(CAP, dtype=jnp.int32)[None, :]
    places = jnp.where(spot < here[:, None], start[:, None] + spot, -1)
    views = lax.optimization_barrier((places.reshape(1, ALL_ROWS), places.reshape(ALL_ROWS, 1)))
    w_gate, w_up, w_down = w_gate[0], w_up[0], w_down[0]
    line_rank = coordinates()[0]
    moved = []
    after_counts = jnp.minimum(largest, 0)
    for weight in (w_gate, w_up):
        for step in range(1, SIDE):
            column = lax.rem(line_rank + step, SIDE) * FBLK + after_counts
            piece = lax.dynamic_slice(weight, (0, column), (DBLK, FBLK))
            moved.append(lax.ppermute(piece, MESH_AXES, line_permutation(step)))
    attention_output = attend_local(queries, token_key_value, cache, cache_length)
    state = residual.astype(jnp.float32) + attention_output.astype(jnp.float32)
    scaled = state * norm_gain.astype(jnp.float32)[None, :]
    squares, raw_logits = lax.psum(
        (
            jnp.sum(state * state, axis=1),
            jnp.dot(scaled, router.astype(jnp.float32), precision=lax.Precision.HIGHEST),
        ),
        "tp",
    )
    row_scale = jnp.sqrt(squares / MODEL_WIDTH + EPSILON)[:, None]
    logits = raw_logits / row_scale
    normed = (scaled / row_scale).astype(jnp.bfloat16)
    chosen = jnp.take_along_axis(logits, routes, axis=1)
    weight_first = jax.nn.sigmoid(chosen[:, 0] - chosen[:, 1])
    weight_second = 1.0 - weight_first
    selector = (
        (
            (slot_index[:, None] == jnp.arange(slot_total, dtype=jnp.int32)[None, :])
            & flat_live[:, None]
        )
        .astype(jnp.bfloat16)
        .reshape(seq_count, 2, slot_total)
    )
    senders = selector[:, 0] + selector[:, 1]
    outgoing = lax.dot_general(
        senders, normed, (((0,), (0,)), ((), ())), preferred_element_type=jnp.float32
    )
    outgoing = outgoing.astype(jnp.bfloat16).reshape(expert_count, CAP, normed.shape[1])
    branches = [
        functools.partial(lambda keep, views, *args: expert_layer(keep, *args, views[: 2 * (keep < ALL_ROWS)]), keep)
        for keep in SIZES
    ]
    choice = sum((largest > keep).astype(jnp.int32) for keep in SIZES[:-1])
    returned = lax.switch(choice, branches, views, outgoing, w_gate, w_up, w_down, moved)
    returned = returned.reshape(slot_total, normed.shape[1])
    pick_first = jnp.dot(selector[:, 0], returned, preferred_element_type=jnp.float32)
    pick_second = jnp.dot(selector[:, 1], returned, preferred_element_type=jnp.float32)
    moe_sum = weight_first[:, None] * pick_first + weight_second[:, None] * pick_second
    delta = jnp.where(still_live[:, None], attention_output.astype(jnp.float32) + moe_sum, 0.0)
    return delta.astype(jnp.bfloat16)


def solution(mesh):
    in_specs = (
        P(("grp", "ep"), "tp"),
        P(("grp", "ep"), "tp"),
        P(("grp", "ep"), None, "tp"),
        P(("grp", "ep"), None, None, "tp"),
        P(("grp", "ep")),
        P(("grp", "ep")),
        P(("grp", "ep"), None),
        P("tp"),
        P("tp", None),
        P("ep", ("grp", "tp"), None),
        P("ep", ("grp", "tp"), None),
        P("ep", ("grp", "tp"), None),
    )
    out_specs = P(("grp", "ep"), "tp")
    return jax.shard_map(
        per_device, mesh=mesh, in_specs=in_specs, out_specs=out_specs, check_vma=False
    )
```

```python
import functools

import jax
import jax.numpy as jnp
from jax import lax
from jax.experimental import pallas as pl
from jax.experimental.pallas import tpu as pltpu
from jax.sharding import PartitionSpec as P

MODEL_WIDTH = 4096
QUERY_HEADS = 32
KEY_VALUE_HEADS = 8
HEAD_SIZE = 128


EPSILON = 1e-05

SIDE = 4
DEVICES = 128
CAP = 16
PIECES = 64
ALL_ROWS = PIECES * CAP
CHUNK = 128
SEQS = 4
SIZES = (512, 576, 704, ALL_ROWS)
DBLK = 256
DSET = SIDE * DBLK
FBLK = 2048
FT = 512
MESH_AXES = ("grp", "ep", "tp")
MESH_ID = pl.DeviceIdType.MESH


def line_permutation(step):
    pairs = []
    for grp in range(8):
        for ep in range(8):
            for tp in range(2):
                x, z = grp % 4, (grp // 4) * 2 + tp
                if ep % 2 == 0:
                    x2, z2 = (x + step) % SIDE, z
                else:
                    x2, z2 = x, (z + step) % SIDE
                pairs.append(((grp * 8 + ep) * 2 + tp, (((z2 // 2) * 4 + x2) * 8 + ep) * 2 + z2 % 2))
    return pairs


def coordinates():
    grp, ep, tp = (lax.axis_index(name) for name in MESH_AXES)
    x = lax.rem(grp, 4)
    z = lax.div(grp, 4) * 2 + tp
    core = lax.rem(ep, 2)
    return x + (z - x) * core, z + (x - z) * core, core, ep


def parts_of(keep):
    quarter = keep // SIDE
    upper = (quarter + 31) // 32 * 16
    return quarter, upper, quarter - upper


def greet_all():
    itself = own_id()
    barrier = pltpu.get_barrier_semaphore()

    @pl.loop(1, DEVICES)
    def _(step):
        at = lax.rem(itself + step, DEVICES)
        to = (lax.div(at, 16), lax.rem(lax.div(at, 2), 8), lax.rem(at, 2))
        pl.semaphore_signal(barrier, inc=1, device_id=to, device_id_type=MESH_ID)

    return lambda: pl.semaphore_wait(barrier, DEVICES - 1)


def own_id():
    grp, ep, tp = (lax.axis_index(name) for name in MESH_AXES)
    return (grp * 8 + ep) * 2 + tp


def remote(src, dst, ssem, rsem, to):
    return pltpu.make_async_remote_copy(
        src_ref=src, dst_ref=dst, send_sem=ssem, recv_sem=rsem, device_id=to, device_id_type=MESH_ID
    )


def deliver(src_of, dst_of, to_of, sends, recvs, spare):
    itself = own_id()

    @pl.loop(0, PIECES)
    def _(step):
        to = to_of(step)
        far = (to[0] * 8 + to[1]) * 2 + to[2] != itself

        @pl.when(far)
        def _():
            remote(src_of(step), dst_of(step), sends.at[0], recvs.at[0], to).start()

        @pl.when(jnp.logical_not(far))
        def _():
            pltpu.make_async_copy(src_of(step), dst_of(step), recvs.at[0]).start()
            pltpu.make_async_copy(src_of(step), spare, sends.at[0]).start()


def dispatch_kernel(
    x_in, mine, landed, at_row, at_column, totals, counts, x_send, x_recv, c_send, c_recv, spare, c_spare
):
    grp, ep, tp = (lax.axis_index(name) for name in MESH_AXES)
    source = grp * 8 + ep
    own_block = lax.rem(grp, 4) * 2 + tp
    greet_all()()

    def counts_to(step):
        at = lax.rem(source + step, PIECES)
        return (lax.div(at, 8), lax.rem(at, 8), tp)

    deliver(lambda step: mine, lambda step: counts.at[source], counts_to, c_send, c_recv, c_spare)

    def expert_of(step):
        return lax.rem(ep + lax.div(step, 8), 8)

    def block_of(step):
        return lax.rem(own_block + step, 8)

    deliver(
        lambda step: x_in.at[expert_of(step), :, pl.ds(pl.multiple_of(block_of(step) * DBLK, DBLK), DBLK)],
        lambda step: landed.at[source],
        lambda step: (tp * 4 + lax.div(block_of(step), 2), expert_of(step), lax.rem(block_of(step), 2)),
        x_send, x_recv, spare,
    )
    pltpu.make_async_copy(counts, counts, c_send.at[0]).wait()
    pltpu.make_async_copy(counts, counts, c_recv.at[0]).wait()

    table = counts[...].reshape(PIECES, 128)
    totals[...] = jnp.sum(table, axis=0, keepdims=True)
    lane = lax.broadcasted_iota(jnp.int32, (PIECES, 128), 1)
    here = jnp.sum(jnp.where(lane == ep, table, 0.0), axis=1, keepdims=True)
    up = lax.broadcasted_iota(jnp.int32, (PIECES, PIECES), 0)
    along = lax.broadcasted_iota(jnp.int32, (PIECES, PIECES), 1)
    here_row = jnp.sum(jnp.where(up == along, here, 0.0), axis=0, keepdims=True)
    start = jnp.sum(jnp.where(along < up, here_row, 0.0), axis=1, keepdims=True)
    start_row = jnp.sum(jnp.where(up < along, here, 0.0), axis=0, keepdims=True)

    spot = lax.broadcasted_iota(jnp.int32, (PIECES, ALL_ROWS), 1)
    inside = lax.div(spot, CAP) == lax.broadcasted_iota(jnp.int32, (PIECES, ALL_ROWS), 0)
    place = lax.rem(spot, CAP).astype(jnp.float32)
    value = jnp.where(inside & (place < here), start + place + 1.0, 0.0)
    at_row[...] = jnp.sum(value, axis=0, keepdims=True).astype(jnp.int32) - 1

    spot = lax.broadcasted_iota(jnp.int32, (ALL_ROWS, PIECES), 0)
    inside = lax.div(spot, CAP) == lax.broadcasted_iota(jnp.int32, (ALL_ROWS, PIECES), 1)
    place = lax.rem(spot, CAP).astype(jnp.float32)
    value = jnp.where(inside & (place < here_row), start_row + place + 1.0, 0.0)
    at_column[...] = jnp.sum(value, axis=1, keepdims=True).astype(jnp.int32) - 1

    pltpu.make_async_copy(x_in, x_in, x_send.at[0]).wait()
    pltpu.make_async_copy(landed, landed, x_recv.at[0]).wait()


def dispatch(x_in, mine):
    in_vmem = pl.BlockSpec(memory_space=pltpu.VMEM)
    dma = pltpu.SemaphoreType.DMA
    return pl.pallas_call(
        dispatch_kernel,
        out_shape=(
            jax.ShapeDtypeStruct((PIECES, CAP, DBLK), jnp.bfloat16),
            jax.ShapeDtypeStruct((1, ALL_ROWS), jnp.int32),
            jax.ShapeDtypeStruct((ALL_ROWS, 1), jnp.int32),
            jax.ShapeDtypeStruct((1, 128), jnp.float32),
        ),
        in_specs=[pl.BlockSpec(memory_space=pl.ANY), in_vmem],
        out_specs=(in_vmem,) * 4,
        scratch_shapes=[
            pltpu.VMEM((PIECES, 1, 128), jnp.float32),
            dma((1,)), dma((1,)), dma((1,)), dma((1,)),
            pltpu.VMEM((CAP, DBLK), jnp.bfloat16),
            pltpu.VMEM((1, 128), jnp.float32),
        ],
        compiler_params=pltpu.CompilerParams(collective_id=1, has_side_effects=True),
        name="dispatch",
    )(x_in, mine)


def moe_kernel(
    keep, landed, w_gate, w_up, w_down, g1, g2, g3, u1, u2, u3, *refs
):
    if keep < ALL_ROWS:
        at_row, at_column, *refs = refs
    (
        y_out, rows, wg, wu, wd, send, fwd, got, raw, own, hid, part, part32, part_in, total, y_send,
        w_sem, xa_send, xa_recv, rs_send, rs_recv, ag_send, ag_recv,
        o_send, o_recv, y_ssem, y_rsem, d_send, d_recv, spare,
    ) = refs
    quarter, upper, lower = parts_of(keep)
    a, b, core, ep = coordinates()
    grp, tp = lax.axis_index("grp"), lax.axis_index("tp")
    z_hi = lax.div(grp, 4)
    own_block = lax.rem(grp, 4) * 2 + tp

    def peer(at_a, at_b):
        x = at_a + (at_b - at_a) * core
        z = at_b + (at_a - at_b) * core
        return (lax.div(z, 2) * 4 + x, ep, lax.rem(z, 2))

    def shifted(value, by):
        return lax.rem(value + by + SIDE, SIDE)

    right, left, across = shifted(b, 1), shifted(b, -1), shifted(b, 2)

    loads = []
    for which, (full, parts, dst) in enumerate(
        ((w_gate, (g1, g2, g3), wg), (w_up, (u1, u2, u3), wu), (w_down, (), wd))
    ):
        column = pl.ds(pl.multiple_of(a * FBLK, FBLK), FBLK)
        for step in range(len(parts) + 1):
            row = pl.ds(pl.multiple_of(shifted(a, -step) * DBLK, DBLK), DBLK)
            src = full.at[:, column] if step == 0 else parts[step - 1]
            copy = pltpu.make_async_copy(src, dst.at[row], w_sem.at[which, step])
            copy.start()
            loads.append(copy)

    wait_for_all = greet_all()

    def send_down(which, step):
        at = shifted(a, step)
        copy = remote(
            w_down.at[:, pl.ds(pl.multiple_of(at * FBLK, FBLK), FBLK)],
            wd.at[pl.ds(pl.multiple_of(a * DBLK, DBLK), DBLK)],
            d_send.at[which], d_recv.at[which], peer(at, b),
        )
        copy.start()
        loads.append(copy)

    if keep < ALL_ROWS:
        @pl.loop(0, SIDE)
        def _(chunk):
            first = pl.multiple_of(chunk * quarter, 16)
            place = lax.broadcasted_iota(jnp.int32, (quarter, ALL_ROWS), 0) + first
            pick = jnp.where(place == at_row[...], 1.0, 0.0).astype(jnp.bfloat16)
            packed = jnp.dot(pick, landed[...].reshape(ALL_ROWS, DBLK), preferred_element_type=jnp.float32)
            rows[a, pl.ds(first, quarter), :] = packed.astype(jnp.bfloat16)
    else:
        rows[a] = landed[...].reshape(ALL_ROWS, DBLK)

    wait_for_all()

    copies = []
    for step in (2, 1, 3):
        copy = remote(
            rows.at[a], rows.at[a], xa_send.at[step - 1], xa_recv.at[step - 1], peer(shifted(a, step), b)
        )
        copy.start()
        copies.append(copy)
    for which, step in ((0, 1), (1, 3), (2, 2)):
        send_down(which, step)
    for copy in loads[: 2 * SIDE]:
        copy.wait()
    for copy in copies:
        copy.wait()

    def product(group, store):
        first = pl.multiple_of(group * quarter, 16)

        @pl.loop(0, FBLK // FT)
        def _(tile):
            lhs = jnp.concatenate([rows[k, pl.ds(first, quarter), :] for k in range(SIDE)], axis=1)
            for part_index, weight in enumerate((wg, wu)):
                cols = pl.ds(pl.multiple_of(tile * FT, FT), FT)
                to = pl.ds(pl.multiple_of(tile * FT + part_index * FBLK, FT), FT)
                value = jnp.dot(lhs, weight[:, cols], preferred_element_type=jnp.float32)
                store(to, value[:upper], value[upper:])

    def store_across(to, top, bottom):
        send[0, :, to] = top.astype(jnp.bfloat16)
        send[1, :lower, to] = bottom.astype(jnp.bfloat16)

    def store_right(to, top, bottom):
        raw[0, :, to] = top
        send[2, :lower, to] = bottom.astype(jnp.bfloat16)

    def store_left(to, top, bottom):
        send[3, :, to] = top.astype(jnp.bfloat16)
        raw[1, :lower, to] = bottom

    def store_own(to, top, bottom):
        own[:upper, to] = top
        own[upper:, to] = bottom

    def add_arrived(slot, which, count):
        @pl.loop(0, 2 * FBLK // FT)
        def _(tile):
            to = pl.ds(pl.multiple_of(tile * FT, FT), FT)
            value = raw[which, :count, to] + fwd[which, :count, to].astype(jnp.float32)
            send[slot, :count, to] = value.astype(jnp.bfloat16)

    def pass_on(slot, count, dst, to):
        copy = remote(send.at[slot, pl.ds(0, count)], dst.at[pl.ds(0, count)], rs_send.at[slot], rs_recv.at[slot], to)
        copy.start()
        return copy

    to_right, to_left = peer(a, right), peer(a, left)
    product(across, store_across)
    over_right = pass_on(0, upper, fwd.at[0], to_right)
    over_left = pass_on(1, lower, fwd.at[1], to_left)
    product(right, store_right)
    plain_right = pass_on(2, lower, got.at[1], to_right)
    product(left, store_left)
    plain_left = pass_on(3, upper, got.at[2], to_left)
    product(b, store_own)
    over_right.wait()
    add_arrived(4, 0, upper)
    sum_right = pass_on(4, upper, got.at[0], to_right)
    over_left.wait()
    add_arrived(5, 1, lower)
    sum_left = pass_on(5, lower, got.at[3], to_left)

    for copy in (plain_right, plain_left, sum_right, sum_left):
        copy.wait()

    @pl.loop(0, FBLK // FT)
    def _(tile):
        cols = pl.ds(pl.multiple_of(tile * FT, FT), FT)
        ups = pl.ds(pl.multiple_of(tile * FT + FBLK, FT), FT)
        for half, (begin, count) in enumerate(((0, upper), (upper, lower))):

            def whole(which):
                return (
                    own[begin : begin + count, which]
                    + got[half, :count, which].astype(jnp.float32)
                    + got[2 + half, :count, which].astype(jnp.float32)
                )

            gate, up = whole(cols), whole(ups)
            hid[b, begin : begin + count, cols] = (gate / (1.0 + jnp.exp(-gate)) * up).astype(jnp.bfloat16)

    own_right = remote(hid.at[b], hid.at[b], ag_send.at[0], ag_recv.at[0], to_right)
    own_left = remote(hid.at[b], hid.at[b], ag_send.at[1], ag_recv.at[1], to_left)
    own_right.start()
    own_left.start()
    for copy in loads[2 * SIDE :]:
        copy.wait()

    o_copies = {}

    def down(order, group):
        lhs = hid[group]

        def block(step):
            cols = pl.ds(pl.multiple_of(lax.rem(a + step, SIDE) * DBLK, DBLK), DBLK)
            return lax.dot_general(lhs, wd[cols, :], (((1,), (1,)), ((), ())), preferred_element_type=jnp.float32)

        @pl.loop(1, SIDE)
        def _(step):
            part[order, step - 1] = block(step).astype(jnp.bfloat16)

        for step in (2, 1, 3):
            copy = remote(
                part.at[order, step - 1], part_in.at[order, step - 1],
                o_send.at[order, step - 1], o_recv.at[order, step - 1], peer(shifted(a, step), b),
            )
            copy.start()
            o_copies[order, step] = copy
        part32[order] = block(0)

    def finish(order, group):
        value = part32[order]
        for step in range(1, SIDE):
            o_copies[order, step].wait()
            value = value + part_in[order, step - 1].astype(jnp.float32)
        total[pl.ds(pl.multiple_of(group * quarter, 16), quarter), :] = value.astype(jnp.bfloat16)

    down(0, b)
    own_right.wait()
    top, bottom = pl.ds(0, upper), pl.ds(upper, lower)
    on_right = remote(hid.at[left, top], hid.at[left, top], ag_send.at[2], ag_recv.at[2], to_right)
    on_right.start()
    own_left.wait()
    on_left = remote(hid.at[right, bottom], hid.at[right, bottom], ag_send.at[3], ag_recv.at[3], to_left)
    on_left.start()
    down(1, left)
    down(3, right)
    finish(0, b)
    on_right.wait()
    on_left.wait()
    down(2, across)
    finish(1, left)
    finish(3, right)
    finish(2, across)

    if keep < ALL_ROWS:
        @pl.loop(0, ALL_ROWS // CHUNK)
        def _(chunk):
            place = lax.broadcasted_iota(jnp.int32, (CHUNK, keep), 1)
            at = at_column[pl.ds(pl.multiple_of(chunk * CHUNK, CHUNK), CHUNK), :]
            pick = jnp.where(place == at, 1.0, 0.0).astype(jnp.bfloat16)
            spread = jnp.dot(pick, total[...], preferred_element_type=jnp.float32)
            first = pl.multiple_of(chunk * (CHUNK // CAP), CHUNK // CAP)
            y_send[pl.ds(first, CHUNK // CAP)] = spread.astype(jnp.bfloat16).reshape(CHUNK // CAP, CAP, DBLK)
    else:
        y_send[...] = total[...].reshape(PIECES, CAP, DBLK)

    def source_of(step):
        return lax.rem(grp * 8 + ep + step, PIECES)

    deliver(
        lambda step: y_send.at[source_of(step)],
        lambda step: y_out.at[ep, :, pl.ds(pl.multiple_of(own_block * DBLK, DBLK), DBLK)],
        lambda step: (lax.div(source_of(step), 8), lax.rem(source_of(step), 8), z_hi),
        y_ssem, y_rsem, spare,
    )
    pltpu.make_async_copy(y_send, y_send, y_ssem.at[0]).wait()
    pltpu.make_async_copy(y_out, y_out, y_rsem.at[0]).wait()


def expert_layer(keep, landed, w_gate, w_up, w_down, moved, places=()):
    bf16, f32 = jnp.bfloat16, jnp.float32
    dma = pltpu.SemaphoreType.DMA
    quarter, upper, _ = parts_of(keep)
    scratch = [
        pltpu.VMEM((SIDE, keep, DBLK), bf16),
        pltpu.VMEM((DSET, FBLK), bf16),
        pltpu.VMEM((DSET, FBLK), bf16),
        pltpu.VMEM((DSET, FBLK), bf16),
        pltpu.VMEM((6, upper, 2 * FBLK), bf16),
        pltpu.VMEM((2, upper, 2 * FBLK), bf16),
        pltpu.VMEM((4, upper, 2 * FBLK), bf16),
        pltpu.VMEM((2, upper, 2 * FBLK), f32),
        pltpu.VMEM((quarter, 2 * FBLK), f32),
        pltpu.VMEM((SIDE, quarter, FBLK), bf16),
        pltpu.VMEM((SIDE, SIDE - 1, quarter, DBLK), bf16),
        pltpu.VMEM((SIDE, quarter, DBLK), f32),
        pltpu.VMEM((SIDE, SIDE - 1, quarter, DBLK), bf16),
        pltpu.VMEM((keep, DBLK), bf16),
        pltpu.VMEM((PIECES, CAP, DBLK), bf16),
        dma((3, SIDE)),
        dma((3,)), dma((3,)),
        dma((6,)), dma((6,)),
        dma((4,)), dma((4,)),
        dma((SIDE, 3)), dma((SIDE, 3)),
        dma((1,)), dma((1,)),
        dma((3,)), dma((3,)),
        pltpu.VMEM((CAP, DBLK), bf16),
    ]
    anywhere, in_vmem = pl.BlockSpec(memory_space=pl.ANY), pl.BlockSpec(memory_space=pltpu.VMEM)
    return pl.pallas_call(
        functools.partial(moe_kernel, keep),
        out_shape=jax.ShapeDtypeStruct((8, CAP, 8 * DBLK), bf16),
        in_specs=[in_vmem] + [anywhere] * 9 + [in_vmem] * len(places),
        out_specs=anywhere,
        scratch_shapes=scratch,
        compiler_params=pltpu.CompilerParams(
            collective_id=keep // 64, has_side_effects=True, vmem_limit_bytes=60 * 1024 * 1024
        ),
        cost_estimate=pl.CostEstimate(
            flops=13 * 10**6 * keep, bytes_accessed=14 * 10**6, transcendentals=10**6
        ),
        name="expert_layer",
    )(landed, w_gate, w_up, w_down, *moved, *places)


def attend_kernel(lengths, queries, token_key_value, cache, attended):
    step = pl.program_id(0)
    share = QUERY_HEADS // KEY_VALUE_HEADS
    heads = queries.shape[1]
    width = cache.shape[3]
    score_scale = HEAD_SIZE ** (-0.5)
    head = lax.broadcasted_iota(jnp.int32, (heads, width), 0)
    column = lax.broadcasted_iota(jnp.int32, (heads, width), 1)
    matches = lax.div(head, share) == lax.div(column, HEAD_SIZE)
    position = lax.broadcasted_iota(jnp.int32, (heads, cache.shape[2]), 1)

    def own_part(wide):
        wide = jnp.where(matches, wide, 0.0)
        return sum(wide[:, k * HEAD_SIZE : (k + 1) * HEAD_SIZE] for k in range(width // HEAD_SIZE))

    for i in range(SEQS):
        query = queries[i].astype(jnp.float32)
        query = jnp.where(matches, jnp.concatenate([query] * (width // HEAD_SIZE), axis=1), 0.0)
        new = token_key_value[i].astype(jnp.float32)
        scores = lax.dot_general(
            query.astype(jnp.bfloat16), cache[i, 0], (((1,), (1,)), ((), ())), preferred_element_type=jnp.float32
        )
        scores = jnp.where(position < lengths[step * SEQS + i], scores * score_scale, -jnp.inf)
        self_score = jnp.sum(query * new[0:1, :], axis=1, keepdims=True) * score_scale
        highest = jnp.maximum(jnp.max(scores, axis=1, keepdims=True), self_score)
        exponent = jnp.exp(scores - highest)
        own_exp = jnp.exp(self_score - highest)
        totals = jnp.sum(exponent, axis=1, keepdims=True) + own_exp
        normalized = (exponent / totals).astype(jnp.bfloat16)
        own_weight = (own_exp / totals).astype(jnp.bfloat16).astype(jnp.float32)
        mixture = jnp.dot(normalized, cache[i, 1], preferred_element_type=jnp.float32)
        mixture = own_part(mixture) + own_weight * own_part(jnp.broadcast_to(new[1:2, :], (heads, width)))
        attended[i] = mixture.astype(jnp.bfloat16)


def attend_local(queries, token_key_value, cache, cache_length):
    seq_count, _, positions, width = cache.shape
    heads = queries.shape[1] // HEAD_SIZE
    attended = pl.pallas_call(
        attend_kernel,
        out_shape=jax.ShapeDtypeStruct((seq_count, heads, HEAD_SIZE), jnp.bfloat16),
        grid_spec=pltpu.PrefetchScalarGridSpec(
            num_scalar_prefetch=1,
            grid=(seq_count // SEQS,),
            in_specs=[
                pl.BlockSpec((SEQS, heads, HEAD_SIZE), lambda i, _: (i, 0, 0)),
                pl.BlockSpec((SEQS, 2, width), lambda i, _: (i, 0, 0)),
                pl.BlockSpec((SEQS, 2, positions, width), lambda i, _: (i, 0, 0, 0)),
            ],
            out_specs=pl.BlockSpec((SEQS, heads, HEAD_SIZE), lambda i, _: (i, 0, 0)),
        ),
        cost_estimate=pl.CostEstimate(
            flops=4 * seq_count * heads * positions * width,
            bytes_accessed=2 * cache.size,
            transcendentals=seq_count * heads * positions,
        ),
        name="attention",
    )(cache_length, queries.reshape(seq_count, heads, HEAD_SIZE), token_key_value, cache)
    return attended.reshape(seq_count, heads * HEAD_SIZE)


def per_device(
    residual,
    queries,
    token_key_value,
    cache,
    cache_length,
    active,
    routes,
    norm_gain,
    router,
    w_gate,
    w_up,
    w_down,
):
    seq_count = residual.shape[0]
    expert_count = router.shape[1]
    slot_total = CAP * expert_count
    still_live = active == 1
    flat_expert = routes.reshape(-1)
    flat_live = jnp.repeat(still_live, 2)
    onehot = (
        (flat_expert[:, None] == jnp.arange(expert_count, dtype=jnp.int32)[None, :])
        & flat_live[:, None]
    ).astype(jnp.int32)
    before = jnp.cumsum(onehot, axis=0) - onehot
    rank_order = jnp.sum(before * onehot, axis=1)
    slot_index = flat_expert * CAP + rank_order
    mine = jnp.pad(jnp.sum(onehot, axis=0).astype(jnp.float32), (0, 128 - expert_count)).reshape(1, 128)
    w_gate, w_up, w_down = w_gate[0], w_up[0], w_down[0]
    line_rank = coordinates()[0]
    moved = []
    for weight in (w_gate, w_up):
        for step in range(1, SIDE):
            column = lax.rem(line_rank + step, SIDE) * FBLK
            piece = lax.dynamic_slice(weight, (0, column), (DBLK, FBLK))
            moved.append(lax.ppermute(piece, MESH_AXES, line_permutation(step)))
    attention_output = attend_local(queries, token_key_value, cache, cache_length)
    state = residual.astype(jnp.float32) + attention_output.astype(jnp.float32)
    scaled = state * norm_gain.astype(jnp.float32)[None, :]
    squares, raw_logits = lax.psum(
        (
            jnp.sum(state * state, axis=1),
            jnp.dot(scaled, router.astype(jnp.float32), precision=lax.Precision.HIGHEST),
        ),
        "tp",
    )
    row_scale = jnp.sqrt(squares / MODEL_WIDTH + EPSILON)[:, None]
    logits = raw_logits / row_scale
    normed = (scaled / row_scale).astype(jnp.bfloat16)
    chosen = jnp.take_along_axis(logits, routes, axis=1)
    weight_first = jax.nn.sigmoid(chosen[:, 0] - chosen[:, 1])
    weight_second = 1.0 - weight_first
    selector = (
        (
            (slot_index[:, None] == jnp.arange(slot_total, dtype=jnp.int32)[None, :])
            & flat_live[:, None]
        )
        .astype(jnp.bfloat16)
        .reshape(seq_count, 2, slot_total)
    )
    senders = selector[:, 0] + selector[:, 1]
    outgoing = lax.dot_general(
        senders, normed, (((0,), (0,)), ((), ())), preferred_element_type=jnp.float32
    )
    outgoing = outgoing.astype(jnp.bfloat16).reshape(expert_count, CAP, normed.shape[1])
    landed, at_row, at_column, totals = dispatch(outgoing, mine)
    largest = jnp.max(totals)
    branches = [
        functools.partial(lambda keep, views, *args: expert_layer(keep, *args, views[: 2 * (keep < ALL_ROWS)]), keep)
        for keep in SIZES
    ]
    choice = sum((largest > keep).astype(jnp.int32) for keep in SIZES[:-1])
    returned = lax.switch(choice, branches, (at_row, at_column), landed, w_gate, w_up, w_down, moved)
    returned = returned.reshape(slot_total, normed.shape[1])
    pick_first = jnp.dot(selector[:, 0], returned, preferred_element_type=jnp.float32)
    pick_second = jnp.dot(selector[:, 1], returned, preferred_element_type=jnp.float32)
    moe_sum = weight_first[:, None] * pick_first + weight_second[:, None] * pick_second
    delta = jnp.where(still_live[:, None], attention_output.astype(jnp.float32) + moe_sum, 0.0)
    return delta.astype(jnp.bfloat16)


def solution(mesh):
    in_specs = (
        P(("grp", "ep"), "tp"),
        P(("grp", "ep"), "tp"),
        P(("grp", "ep"), None, "tp"),
        P(("grp", "ep"), None, None, "tp"),
        P(("grp", "ep")),
        P(("grp", "ep")),
        P(("grp", "ep"), None),
        P("tp"),
        P("tp", None),
        P("ep", ("grp", "tp"), None),
        P("ep", ("grp", "tp"), None),
        P("ep", ("grp", "tp"), None),
    )
    out_specs = P(("grp", "ep"), "tp")
    return jax.shard_map(
        per_device, mesh=mesh, in_specs=in_specs, out_specs=out_specs, check_vma=False
    )
```

```python
import functools

import jax
import jax.numpy as jnp
from jax import lax
from jax.experimental import pallas as pl
from jax.experimental.pallas import tpu as pltpu
from jax.sharding import PartitionSpec as P

MODEL_WIDTH = 4096
QUERY_HEADS = 32
KEY_VALUE_HEADS = 8
HEAD_SIZE = 128


EPSILON = 1e-05

SIDE = 4
DEVICES = 128
CAP = 16
PIECES = 64
ALL_ROWS = PIECES * CAP
CHUNK = 128
SEQS = 4
SIZES = (512, 576, 704, ALL_ROWS)
DBLK = 256
DSET = SIDE * DBLK
FBLK = 2048
FT = 512
MESH_AXES = ("grp", "ep", "tp")
MESH_ID = pl.DeviceIdType.MESH


def line_permutation(step):
    pairs = []
    for grp in range(8):
        for ep in range(8):
            for tp in range(2):
                x, z = grp % 4, (grp // 4) * 2 + tp
                if ep % 2 == 0:
                    x2, z2 = (x + step) % SIDE, z
                else:
                    x2, z2 = x, (z + step) % SIDE
                pairs.append(((grp * 8 + ep) * 2 + tp, (((z2 // 2) * 4 + x2) * 8 + ep) * 2 + z2 % 2))
    return pairs


def coordinates():
    grp, ep, tp = (lax.axis_index(name) for name in MESH_AXES)
    x = lax.rem(grp, 4)
    z = lax.div(grp, 4) * 2 + tp
    core = lax.rem(ep, 2)
    return x + (z - x) * core, z + (x - z) * core, core, ep


def parts_of(keep):
    quarter = keep // SIDE
    upper = (quarter + 31) // 32 * 16
    return quarter, upper, quarter - upper


def peer_of(a, b, core, ep):
    x = a + (b - a) * core
    z = b + (a - b) * core
    return (lax.div(z, 2) * 4 + x, ep, lax.rem(z, 2))


def greet_all():
    itself = own_id()
    barrier = pltpu.get_barrier_semaphore()

    @pl.loop(1, DEVICES)
    def _(step):
        at = lax.rem(itself + step, DEVICES)
        to = (lax.div(at, 16), lax.rem(lax.div(at, 2), 8), lax.rem(at, 2))
        pl.semaphore_signal(barrier, inc=1, device_id=to, device_id_type=MESH_ID)

    return lambda: pl.semaphore_wait(barrier, DEVICES - 1)


def own_id():
    grp, ep, tp = (lax.axis_index(name) for name in MESH_AXES)
    return (grp * 8 + ep) * 2 + tp


def remote(src, dst, ssem, rsem, to):
    return pltpu.make_async_remote_copy(
        src_ref=src, dst_ref=dst, send_sem=ssem, recv_sem=rsem, device_id=to, device_id_type=MESH_ID
    )


def deliver(src_of, dst_of, to_of, sends, recvs, spare):
    itself = own_id()

    @pl.loop(0, PIECES)
    def _(step):
        to = to_of(step)
        far = (to[0] * 8 + to[1]) * 2 + to[2] != itself

        @pl.when(far)
        def _():
            remote(src_of(step), dst_of(step), sends.at[0], recvs.at[0], to).start()

        @pl.when(jnp.logical_not(far))
        def _():
            pltpu.make_async_copy(src_of(step), dst_of(step), recvs.at[0]).start()
            pltpu.make_async_copy(src_of(step), spare, sends.at[0]).start()


def dispatch_kernel(
    x_in, mine, w_down, landed, at_row, at_column, choice, moved,
    counts, x_send, x_recv, c_send, c_recv, d_send, d_recv, spare, c_spare,
):
    grp, ep, tp = (lax.axis_index(name) for name in MESH_AXES)
    source = grp * 8 + ep
    own_block = lax.rem(grp, 4) * 2 + tp
    greet_all()()

    def counts_to(step):
        at = lax.rem(source + step, PIECES)
        return (lax.div(at, 8), lax.rem(at, 8), tp)

    deliver(lambda step: mine, lambda step: counts.at[source], counts_to, c_send, c_recv, c_spare)

    def expert_of(step):
        return lax.rem(ep + lax.div(step, 8), 8)

    def block_of(step):
        return lax.rem(own_block + step, 8)

    deliver(
        lambda step: x_in.at[expert_of(step), :, pl.ds(pl.multiple_of(block_of(step) * DBLK, DBLK), DBLK)],
        lambda step: landed.at[source],
        lambda step: (tp * 4 + lax.div(block_of(step), 2), expert_of(step), lax.rem(block_of(step), 2)),
        x_send, x_recv, spare,
    )

    a, b, core, _ = coordinates()
    weights = []
    for index, step in enumerate((1, 3)):
        at = lax.rem(a + step, SIDE)
        copy = remote(
            w_down.at[:, pl.ds(pl.multiple_of(at * FBLK, FBLK), FBLK)], moved.at[index],
            d_send.at[index], d_recv.at[index], peer_of(at, b, core, ep),
        )
        copy.start()
        weights.append(copy)
    pltpu.make_async_copy(counts, counts, c_send.at[0]).wait()
    pltpu.make_async_copy(counts, counts, c_recv.at[0]).wait()

    table = counts[...].reshape(PIECES, 128)
    largest = jnp.max(jnp.sum(table, axis=0, keepdims=True), axis=1, keepdims=True)
    choice[...] = sum((largest > keep).astype(jnp.int32) for keep in SIZES[:-1])
    lane = lax.broadcasted_iota(jnp.int32, (PIECES, 128), 1)
    here = jnp.sum(jnp.where(lane == ep, table, 0.0), axis=1, keepdims=True)
    up = lax.broadcasted_iota(jnp.int32, (PIECES, PIECES), 0)
    along = lax.broadcasted_iota(jnp.int32, (PIECES, PIECES), 1)
    here_row = jnp.sum(jnp.where(up == along, here, 0.0), axis=0, keepdims=True)
    start = jnp.sum(jnp.where(along < up, here_row, 0.0), axis=1, keepdims=True)
    start_row = jnp.sum(jnp.where(up < along, here, 0.0), axis=0, keepdims=True)

    spot = lax.broadcasted_iota(jnp.int32, (PIECES, ALL_ROWS), 1)
    inside = lax.div(spot, CAP) == lax.broadcasted_iota(jnp.int32, (PIECES, ALL_ROWS), 0)
    place = lax.rem(spot, CAP).astype(jnp.float32)
    value = jnp.where(inside & (place < here), start + place + 1.0, 0.0)
    at_row[...] = jnp.sum(value, axis=0, keepdims=True).astype(jnp.int32) - 1

    spot = lax.broadcasted_iota(jnp.int32, (ALL_ROWS, PIECES), 0)
    inside = lax.div(spot, CAP) == lax.broadcasted_iota(jnp.int32, (ALL_ROWS, PIECES), 1)
    place = lax.rem(spot, CAP).astype(jnp.float32)
    value = jnp.where(inside & (place < here_row), start_row + place + 1.0, 0.0)
    at_column[...] = jnp.sum(value, axis=1, keepdims=True).astype(jnp.int32) - 1

    pltpu.make_async_copy(x_in, x_in, x_send.at[0]).wait()
    pltpu.make_async_copy(landed, landed, x_recv.at[0]).wait()
    for copy in weights:
        copy.wait()


def dispatch(x_in, mine, w_down):
    in_vmem, anywhere = pl.BlockSpec(memory_space=pltpu.VMEM), pl.BlockSpec(memory_space=pl.ANY)
    dma = pltpu.SemaphoreType.DMA
    return pl.pallas_call(
        dispatch_kernel,
        out_shape=(
            jax.ShapeDtypeStruct((PIECES, CAP, DBLK), jnp.bfloat16),
            jax.ShapeDtypeStruct((1, ALL_ROWS), jnp.int32),
            jax.ShapeDtypeStruct((ALL_ROWS, 1), jnp.int32),
            jax.ShapeDtypeStruct((1, 1), jnp.int32),
            jax.ShapeDtypeStruct((2, DBLK, FBLK), jnp.bfloat16),
        ),
        in_specs=[anywhere, in_vmem, anywhere],
        out_specs=(in_vmem,) * 4 + (anywhere,),
        scratch_shapes=[
            pltpu.VMEM((PIECES, 1, 128), jnp.float32),
            dma((1,)), dma((1,)), dma((1,)), dma((1,)), dma((2,)), dma((2,)),
            pltpu.VMEM((CAP, DBLK), jnp.bfloat16),
            pltpu.VMEM((1, 128), jnp.float32),
        ],
        compiler_params=pltpu.CompilerParams(collective_id=1, has_side_effects=True),
        name="dispatch",
    )(x_in, mine, w_down)


def moe_kernel(
    keep, landed, w_gate, w_up, w_down, g1, g2, g3, u1, u2, u3, d13, *refs
):
    if keep < ALL_ROWS:
        at_row, at_column, *refs = refs
    (
        y_out, rows, wg, wu, wd, send, fwd, got, raw, own, hid, part, part32, part_in, total, y_send,
        w_sem, xa_send, xa_recv, rs_send, rs_recv, ag_send, ag_recv,
        o_send, o_recv, y_ssem, y_rsem, d_send, d_recv, spare,
    ) = refs
    quarter, upper, lower = parts_of(keep)
    a, b, core, ep = coordinates()
    grp, tp = lax.axis_index("grp"), lax.axis_index("tp")
    z_hi = lax.div(grp, 4)
    own_block = lax.rem(grp, 4) * 2 + tp

    def peer(at_a, at_b):
        return peer_of(at_a, at_b, core, ep)

    def shifted(value, by):
        return lax.rem(value + by + SIDE, SIDE)

    right, left, across = shifted(b, 1), shifted(b, -1), shifted(b, 2)

    loads = []
    for which, (full, parts, dst) in enumerate(
        (
            (w_gate, ((1, g1), (2, g2), (3, g3)), wg),
            (w_up, ((1, u1), (2, u2), (3, u3)), wu),
            (w_down, ((1, d13.at[0]), (3, d13.at[1])), wd),
        )
    ):
        own_part = full.at[:, pl.ds(pl.multiple_of(a * FBLK, FBLK), FBLK)]
        for step, src in ((0, own_part), *parts):
            row = pl.ds(pl.multiple_of(shifted(a, -step) * DBLK, DBLK), DBLK)
            copy = pltpu.make_async_copy(src, dst.at[row], w_sem.at[which, step])
            copy.start()
            loads.append(copy)

    wait_for_all = greet_all()

    if keep < ALL_ROWS:
        @pl.loop(0, SIDE)
        def _(chunk):
            first = pl.multiple_of(chunk * quarter, 16)
            place = lax.broadcasted_iota(jnp.int32, (quarter, ALL_ROWS), 0) + first
            pick = jnp.where(place == at_row[...], 1.0, 0.0).astype(jnp.bfloat16)
            packed = jnp.dot(pick, landed[...].reshape(ALL_ROWS, DBLK), preferred_element_type=jnp.float32)
            rows[a, pl.ds(first, quarter), :] = packed.astype(jnp.bfloat16)
    else:
        rows[a] = landed[...].reshape(ALL_ROWS, DBLK)

    wait_for_all()

    copies = []
    for step in (2, 1, 3):
        copy = remote(
            rows.at[a], rows.at[a], xa_send.at[step - 1], xa_recv.at[step - 1], peer(shifted(a, step), b)
        )
        copy.start()
        copies.append(copy)
    at = shifted(a, 2)
    copy = remote(
        w_down.at[:, pl.ds(pl.multiple_of(at * FBLK, FBLK), FBLK)],
        wd.at[pl.ds(pl.multiple_of(a * DBLK, DBLK), DBLK)],
        d_send.at[0], d_recv.at[0], peer(at, b),
    )
    copy.start()
    loads.append(copy)
    for copy in loads[: 2 * SIDE]:
        copy.wait()
    for copy in copies:
        copy.wait()

    def product(group, store):
        first = pl.multiple_of(group * quarter, 16)

        @pl.loop(0, FBLK // FT)
        def _(tile):
            lhs = jnp.concatenate([rows[k, pl.ds(first, quarter), :] for k in range(SIDE)], axis=1)
            for part_index, weight in enumerate((wg, wu)):
                cols = pl.ds(pl.multiple_of(tile * FT, FT), FT)
                to = pl.ds(pl.multiple_of(tile * FT + part_index * FBLK, FT), FT)
                value = jnp.dot(lhs, weight[:, cols], preferred_element_type=jnp.float32)
                store(to, value[:upper], value[upper:])

    def store_across(to, top, bottom):
        send[0, :, to] = top.astype(jnp.bfloat16)
        send[1, :lower, to] = bottom.astype(jnp.bfloat16)

    def store_right(to, top, bottom):
        raw[0, :, to] = top
        send[2, :lower, to] = bottom.astype(jnp.bfloat16)

    def store_left(to, top, bottom):
        send[3, :, to] = top.astype(jnp.bfloat16)
        raw[1, :lower, to] = bottom

    def store_own(to, top, bottom):
        own[:upper, to] = top
        own[upper:, to] = bottom

    def add_arrived(slot, which, count):
        @pl.loop(0, 2 * FBLK // FT)
        def _(tile):
            to = pl.ds(pl.multiple_of(tile * FT, FT), FT)
            value = raw[which, :count, to] + fwd[which, :count, to].astype(jnp.float32)
            send[slot, :count, to] = value.astype(jnp.bfloat16)

    def pass_on(slot, count, dst, to):
        copy = remote(send.at[slot, pl.ds(0, count)], dst.at[pl.ds(0, count)], rs_send.at[slot], rs_recv.at[slot], to)
        copy.start()
        return copy

    to_right, to_left = peer(a, right), peer(a, left)
    product(across, store_across)
    over_right = pass_on(0, upper, fwd.at[0], to_right)
    over_left = pass_on(1, lower, fwd.at[1], to_left)
    product(right, store_right)
    plain_right = pass_on(2, lower, got.at[1], to_right)
    product(left, store_left)
    plain_left = pass_on(3, upper, got.at[2], to_left)
    product(b, store_own)
    over_right.wait()
    add_arrived(4, 0, upper)
    sum_right = pass_on(4, upper, got.at[0], to_right)
    over_left.wait()
    add_arrived(5, 1, lower)
    sum_left = pass_on(5, lower, got.at[3], to_left)

    for copy in (plain_right, plain_left, sum_right, sum_left):
        copy.wait()

    @pl.loop(0, FBLK // FT)
    def _(tile):
        cols = pl.ds(pl.multiple_of(tile * FT, FT), FT)
        ups = pl.ds(pl.multiple_of(tile * FT + FBLK, FT), FT)
        for half, (begin, count) in enumerate(((0, upper), (upper, lower))):

            def whole(which):
                return (
                    own[begin : begin + count, which]
                    + got[half, :count, which].astype(jnp.float32)
                    + got[2 + half, :count, which].astype(jnp.float32)
                )

            gate, up = whole(cols), whole(ups)
            hid[b, begin : begin + count, cols] = (gate / (1.0 + jnp.exp(-gate)) * up).astype(jnp.bfloat16)

    own_right = remote(hid.at[b], hid.at[b], ag_send.at[0], ag_recv.at[0], to_right)
    own_left = remote(hid.at[b], hid.at[b], ag_send.at[1], ag_recv.at[1], to_left)
    own_right.start()
    own_left.start()
    for copy in loads[2 * SIDE :]:
        copy.wait()

    o_copies = {}

    def down(order, group):
        lhs = hid[group]

        def block(step):
            cols = pl.ds(pl.multiple_of(lax.rem(a + step, SIDE) * DBLK, DBLK), DBLK)
            return lax.dot_general(lhs, wd[cols, :], (((1,), (1,)), ((), ())), preferred_element_type=jnp.float32)

        @pl.loop(1, SIDE)
        def _(step):
            part[order, step - 1] = block(step).astype(jnp.bfloat16)

        for step in (2, 1, 3):
            copy = remote(
                part.at[order, step - 1], part_in.at[order, step - 1],
                o_send.at[order, step - 1], o_recv.at[order, step - 1], peer(shifted(a, step), b),
            )
            copy.start()
            o_copies[order, step] = copy
        part32[order] = block(0)

    def finish(order, group):
        value = part32[order]
        for step in range(1, SIDE):
            o_copies[order, step].wait()
            value = value + part_in[order, step - 1].astype(jnp.float32)
        total[pl.ds(pl.multiple_of(group * quarter, 16), quarter), :] = value.astype(jnp.bfloat16)

    down(0, b)
    own_right.wait()
    top, bottom = pl.ds(0, upper), pl.ds(upper, lower)
    on_right = remote(hid.at[left, top], hid.at[left, top], ag_send.at[2], ag_recv.at[2], to_right)
    on_right.start()
    own_left.wait()
    on_left = remote(hid.at[right, bottom], hid.at[right, bottom], ag_send.at[3], ag_recv.at[3], to_left)
    on_left.start()
    down(1, left)
    down(3, right)
    finish(0, b)
    on_right.wait()
    on_left.wait()
    down(2, across)
    finish(1, left)
    finish(3, right)
    finish(2, across)

    if keep < ALL_ROWS:
        @pl.loop(0, ALL_ROWS // CHUNK)
        def _(chunk):
            place = lax.broadcasted_iota(jnp.int32, (CHUNK, keep), 1)
            at = at_column[pl.ds(pl.multiple_of(chunk * CHUNK, CHUNK), CHUNK), :]
            pick = jnp.where(place == at, 1.0, 0.0).astype(jnp.bfloat16)
            spread = jnp.dot(pick, total[...], preferred_element_type=jnp.float32)
            first = pl.multiple_of(chunk * (CHUNK // CAP), CHUNK // CAP)
            y_send[pl.ds(first, CHUNK // CAP)] = spread.astype(jnp.bfloat16).reshape(CHUNK // CAP, CAP, DBLK)
    else:
        y_send[...] = total[...].reshape(PIECES, CAP, DBLK)

    def source_of(step):
        return lax.rem(grp * 8 + ep + step, PIECES)

    deliver(
        lambda step: y_send.at[source_of(step)],
        lambda step: y_out.at[ep, :, pl.ds(pl.multiple_of(own_block * DBLK, DBLK), DBLK)],
        lambda step: (lax.div(source_of(step), 8), lax.rem(source_of(step), 8), z_hi),
        y_ssem, y_rsem, spare,
    )
    pltpu.make_async_copy(y_send, y_send, y_ssem.at[0]).wait()
    pltpu.make_async_copy(y_out, y_out, y_rsem.at[0]).wait()


def expert_layer(keep, landed, w_gate, w_up, w_down, moved, places=()):
    bf16, f32 = jnp.bfloat16, jnp.float32
    dma = pltpu.SemaphoreType.DMA
    quarter, upper, _ = parts_of(keep)
    scratch = [
        pltpu.VMEM((SIDE, keep, DBLK), bf16),
        pltpu.VMEM((DSET, FBLK), bf16),
        pltpu.VMEM((DSET, FBLK), bf16),
        pltpu.VMEM((DSET, FBLK), bf16),
        pltpu.VMEM((6, upper, 2 * FBLK), bf16),
        pltpu.VMEM((2, upper, 2 * FBLK), bf16),
        pltpu.VMEM((4, upper, 2 * FBLK), bf16),
        pltpu.VMEM((2, upper, 2 * FBLK), f32),
        pltpu.VMEM((quarter, 2 * FBLK), f32),
        pltpu.VMEM((SIDE, quarter, FBLK), bf16),
        pltpu.VMEM((SIDE, SIDE - 1, quarter, DBLK), bf16),
        pltpu.VMEM((SIDE, quarter, DBLK), f32),
        pltpu.VMEM((SIDE, SIDE - 1, quarter, DBLK), bf16),
        pltpu.VMEM((keep, DBLK), bf16),
        pltpu.VMEM((PIECES, CAP, DBLK), bf16),
        dma((3, SIDE)),
        dma((3,)), dma((3,)),
        dma((6,)), dma((6,)),
        dma((4,)), dma((4,)),
        dma((SIDE, 3)), dma((SIDE, 3)),
        dma((1,)), dma((1,)),
        dma((1,)), dma((1,)),
        pltpu.VMEM((CAP, DBLK), bf16),
    ]
    anywhere, in_vmem = pl.BlockSpec(memory_space=pl.ANY), pl.BlockSpec(memory_space=pltpu.VMEM)
    return pl.pallas_call(
        functools.partial(moe_kernel, keep),
        out_shape=jax.ShapeDtypeStruct((8, CAP, 8 * DBLK), bf16),
        in_specs=[in_vmem] + [anywhere] * 10 + [in_vmem] * len(places),
        out_specs=anywhere,
        scratch_shapes=scratch,
        compiler_params=pltpu.CompilerParams(
            collective_id=keep // 64, has_side_effects=True, vmem_limit_bytes=60 * 1024 * 1024
        ),
        cost_estimate=pl.CostEstimate(
            flops=13 * 10**6 * keep, bytes_accessed=14 * 10**6, transcendentals=10**6
        ),
        name="expert_layer",
    )(landed, w_gate, w_up, w_down, *moved, *places)


def attend_kernel(lengths, queries, token_key_value, cache, attended):
    step = pl.program_id(0)
    share = QUERY_HEADS // KEY_VALUE_HEADS
    heads = queries.shape[1]
    width = cache.shape[3]
    score_scale = HEAD_SIZE ** (-0.5)
    head = lax.broadcasted_iota(jnp.int32, (heads, width), 0)
    column = lax.broadcasted_iota(jnp.int32, (heads, width), 1)
    matches = lax.div(head, share) == lax.div(column, HEAD_SIZE)
    position = lax.broadcasted_iota(jnp.int32, (heads, cache.shape[2]), 1)

    def own_part(wide):
        wide = jnp.where(matches, wide, 0.0)
        return sum(wide[:, k * HEAD_SIZE : (k + 1) * HEAD_SIZE] for k in range(width // HEAD_SIZE))

    for i in range(SEQS):
        query = queries[i].astype(jnp.float32)
        query = jnp.where(matches, jnp.concatenate([query] * (width // HEAD_SIZE), axis=1), 0.0)
        new = token_key_value[i].astype(jnp.float32)
        scores = lax.dot_general(
            query.astype(jnp.bfloat16), cache[i, 0], (((1,), (1,)), ((), ())), preferred_element_type=jnp.float32
        )
        scores = jnp.where(position < lengths[step * SEQS + i], scores * score_scale, -jnp.inf)
        self_score = jnp.sum(query * new[0:1, :], axis=1, keepdims=True) * score_scale
        highest = jnp.maximum(jnp.max(scores, axis=1, keepdims=True), self_score)
        exponent = jnp.exp(scores - highest)
        own_exp = jnp.exp(self_score - highest)
        totals = jnp.sum(exponent, axis=1, keepdims=True) + own_exp
        normalized = (exponent / totals).astype(jnp.bfloat16)
        own_weight = (own_exp / totals).astype(jnp.bfloat16).astype(jnp.float32)
        mixture = jnp.dot(normalized, cache[i, 1], preferred_element_type=jnp.float32)
        mixture = own_part(mixture) + own_weight * own_part(jnp.broadcast_to(new[1:2, :], (heads, width)))
        attended[i] = mixture.astype(jnp.bfloat16)


def attend_local(queries, token_key_value, cache, cache_length):
    seq_count, _, positions, width = cache.shape
    heads = queries.shape[1] // HEAD_SIZE
    attended = pl.pallas_call(
        attend_kernel,
        out_shape=jax.ShapeDtypeStruct((seq_count, heads, HEAD_SIZE), jnp.bfloat16),
        grid_spec=pltpu.PrefetchScalarGridSpec(
            num_scalar_prefetch=1,
            grid=(seq_count // SEQS,),
            in_specs=[
                pl.BlockSpec((SEQS, heads, HEAD_SIZE), lambda i, _: (i, 0, 0)),
                pl.BlockSpec((SEQS, 2, width), lambda i, _: (i, 0, 0)),
                pl.BlockSpec((SEQS, 2, positions, width), lambda i, _: (i, 0, 0, 0)),
            ],
            out_specs=pl.BlockSpec((SEQS, heads, HEAD_SIZE), lambda i, _: (i, 0, 0)),
        ),
        cost_estimate=pl.CostEstimate(
            flops=4 * seq_count * heads * positions * width,
            bytes_accessed=2 * cache.size,
            transcendentals=seq_count * heads * positions,
        ),
        name="attention",
    )(cache_length, queries.reshape(seq_count, heads, HEAD_SIZE), token_key_value, cache)
    return attended.reshape(seq_count, heads * HEAD_SIZE)


def per_device(
    residual,
    queries,
    token_key_value,
    cache,
    cache_length,
    active,
    routes,
    norm_gain,
    router,
    w_gate,
    w_up,
    w_down,
):
    seq_count = residual.shape[0]
    expert_count = router.shape[1]
    slot_total = CAP * expert_count
    still_live = active == 1
    flat_expert = routes.reshape(-1)
    flat_live = jnp.repeat(still_live, 2)
    onehot = (
        (flat_expert[:, None] == jnp.arange(expert_count, dtype=jnp.int32)[None, :])
        & flat_live[:, None]
    ).astype(jnp.int32)
    before = jnp.cumsum(onehot, axis=0) - onehot
    rank_order = jnp.sum(before * onehot, axis=1)
    slot_index = flat_expert * CAP + rank_order
    mine = jnp.pad(jnp.sum(onehot, axis=0).astype(jnp.float32), (0, 128 - expert_count)).reshape(1, 128)
    w_gate, w_up, w_down = w_gate[0], w_up[0], w_down[0]
    line_rank = coordinates()[0]
    moved = []
    for weight in (w_gate, w_up):
        for step in range(1, SIDE):
            column = lax.rem(line_rank + step, SIDE) * FBLK
            piece = lax.dynamic_slice(weight, (0, column), (DBLK, FBLK))
            moved.append(lax.ppermute(piece, MESH_AXES, line_permutation(step)))
    attention_output = attend_local(queries, token_key_value, cache, cache_length)
    state = residual.astype(jnp.float32) + attention_output.astype(jnp.float32)
    scaled = state * norm_gain.astype(jnp.float32)[None, :]
    squares, raw_logits = lax.psum(
        (
            jnp.sum(state * state, axis=1),
            jnp.dot(scaled, router.astype(jnp.float32), precision=lax.Precision.HIGHEST),
        ),
        "tp",
    )
    row_scale = jnp.sqrt(squares / MODEL_WIDTH + EPSILON)[:, None]
    logits = raw_logits / row_scale
    normed = (scaled / row_scale).astype(jnp.bfloat16)
    chosen = jnp.take_along_axis(logits, routes, axis=1)
    weight_first = jax.nn.sigmoid(chosen[:, 0] - chosen[:, 1])
    weight_second = 1.0 - weight_first
    selector = (
        (
            (slot_index[:, None] == jnp.arange(slot_total, dtype=jnp.int32)[None, :])
            & flat_live[:, None]
        )
        .astype(jnp.bfloat16)
        .reshape(seq_count, 2, slot_total)
    )
    senders = selector[:, 0] + selector[:, 1]
    outgoing = lax.dot_general(
        senders, normed, (((0,), (0,)), ((), ())), preferred_element_type=jnp.float32
    )
    outgoing = outgoing.astype(jnp.bfloat16).reshape(expert_count, CAP, normed.shape[1])
    landed, at_row, at_column, choice, down_moved = dispatch(outgoing, mine, w_down)
    branches = [
        functools.partial(lambda keep, views, *args: expert_layer(keep, *args, views[: 2 * (keep < ALL_ROWS)]), keep)
        for keep in SIZES
    ]
    returned = lax.switch(
        choice[0, 0], branches, (at_row, at_column), landed, w_gate, w_up, w_down, (*moved, down_moved)
    )
    returned = returned.reshape(slot_total, normed.shape[1])
    pick_first = jnp.dot(selector[:, 0], returned, preferred_element_type=jnp.float32)
    pick_second = jnp.dot(selector[:, 1], returned, preferred_element_type=jnp.float32)
    moe_sum = weight_first[:, None] * pick_first + weight_second[:, None] * pick_second
    delta = jnp.where(still_live[:, None], attention_output.astype(jnp.float32) + moe_sum, 0.0)
    return delta.astype(jnp.bfloat16)


def solution(mesh):
    in_specs = (
        P(("grp", "ep"), "tp"),
        P(("grp", "ep"), "tp"),
        P(("grp", "ep"), None, "tp"),
        P(("grp", "ep"), None, None, "tp"),
        P(("grp", "ep")),
        P(("grp", "ep")),
        P(("grp", "ep"), None),
        P("tp"),
        P("tp", None),
        P("ep", ("grp", "tp"), None),
        P("ep", ("grp", "tp"), None),
        P("ep", ("grp", "tp"), None),
    )
    out_specs = P(("grp", "ep"), "tp")
    return jax.shard_map(
        per_device, mesh=mesh, in_specs=in_specs, out_specs=out_specs, check_vma=False
    )
```

```python
import functools

import jax
import jax.numpy as jnp
from jax import lax
from jax.experimental import pallas as pl
from jax.experimental.pallas import tpu as pltpu
from jax.sharding import PartitionSpec as P

MODEL_WIDTH = 4096
QUERY_HEADS = 32
KEY_VALUE_HEADS = 8
HEAD_SIZE = 128


EPSILON = 1e-05

SIDE = 4
DEVICES = 128
CAP = 16
PIECES = 64
ALL_ROWS = PIECES * CAP
CHUNK = 128
SEQS = 4
SIZES = (512, 576, 704, ALL_ROWS)
DBLK = 256
DSET = SIDE * DBLK
FBLK = 2048
FT = 512
MESH_AXES = ("grp", "ep", "tp")
MESH_ID = pl.DeviceIdType.MESH


def line_permutation(step):
    pairs = []
    for grp in range(8):
        for ep in range(8):
            for tp in range(2):
                x, z = grp % 4, (grp // 4) * 2 + tp
                if ep % 2 == 0:
                    x2, z2 = (x + step) % SIDE, z
                else:
                    x2, z2 = x, (z + step) % SIDE
                pairs.append(((grp * 8 + ep) * 2 + tp, (((z2 // 2) * 4 + x2) * 8 + ep) * 2 + z2 % 2))
    return pairs


def coordinates():
    grp, ep, tp = (lax.axis_index(name) for name in MESH_AXES)
    x = lax.rem(grp, 4)
    z = lax.div(grp, 4) * 2 + tp
    core = lax.rem(ep, 2)
    return x + (z - x) * core, z + (x - z) * core, core, ep


def parts_of(keep):
    quarter = keep // SIDE
    upper = (quarter + 31) // 32 * 16
    return quarter, upper, quarter - upper


def peer_of(a, b, core, ep):
    x = a + (b - a) * core
    z = b + (a - b) * core
    return (lax.div(z, 2) * 4 + x, ep, lax.rem(z, 2))


def greet_all():
    itself = own_id()
    barrier = pltpu.get_barrier_semaphore()

    @pl.loop(1, DEVICES)
    def _(step):
        at = lax.rem(itself + step, DEVICES)
        to = (lax.div(at, 16), lax.rem(lax.div(at, 2), 8), lax.rem(at, 2))
        pl.semaphore_signal(barrier, inc=1, device_id=to, device_id_type=MESH_ID)

    return lambda: pl.semaphore_wait(barrier, DEVICES - 1)


def own_id():
    grp, ep, tp = (lax.axis_index(name) for name in MESH_AXES)
    return (grp * 8 + ep) * 2 + tp


def remote(src, dst, ssem, rsem, to):
    return pltpu.make_async_remote_copy(
        src_ref=src, dst_ref=dst, send_sem=ssem, recv_sem=rsem, device_id=to, device_id_type=MESH_ID
    )


def deliver(count, src_of, dst_of, to_of, sends, recvs, spare):
    itself = own_id()

    @pl.loop(0, count)
    def _(step):
        to = to_of(step)
        far = (to[0] * 8 + to[1]) * 2 + to[2] != itself

        @pl.when(far)
        def _():
            remote(src_of(step), dst_of(step), sends.at[0], recvs.at[0], to).start()

        @pl.when(jnp.logical_not(far))
        def _():
            pltpu.make_async_copy(src_of(step), dst_of(step), recvs.at[0]).start()
            pltpu.make_async_copy(src_of(step), spare, sends.at[0]).start()


def dispatch_kernel(
    x_in, notes, halves, w_down, landed, at_row, at_column, choice, moved, other_half,
    arrived, table, x_send, x_recv, c_send, c_recv, d_send, d_recv, h_send, h_recv, spare, c_spare,
):
    grp, ep, tp = (lax.axis_index(name) for name in MESH_AXES)
    source = grp * 8 + ep
    own_block = lax.rem(grp, 4) * 2 + tp
    greet_all()()

    half_copy = remote(halves, other_half, h_send.at[0], h_recv.at[0], (grp, ep, 1 - tp))
    half_copy.start()

    def notes_to(step):
        at = lax.rem(own_id() + step, DEVICES)
        return (lax.div(at, 16), lax.rem(lax.div(at, 2), 8), lax.rem(at, 2))

    deliver(
        DEVICES, lambda step: notes.at[notes_to(step)[1]], lambda step: table.at[source * 2 + tp], notes_to,
        c_send, c_recv, c_spare,
    )

    def expert_of(step):
        return lax.rem(ep + lax.div(step, 8), 8)

    def block_of(step):
        return lax.rem(own_block + step, 8)

    deliver(
        PIECES,
        lambda step: x_in.at[expert_of(step), :, pl.ds(pl.multiple_of(block_of(step) * DBLK, DBLK), DBLK)],
        lambda step: arrived.at[source],
        lambda step: (tp * 4 + lax.div(block_of(step), 2), expert_of(step), lax.rem(block_of(step), 2)),
        x_send, x_recv, spare,
    )

    a, b, core, _ = coordinates()
    weights = []
    for index, step in enumerate((1, 3)):
        at = lax.rem(a + step, SIDE)
        copy = remote(
            w_down.at[:, pl.ds(pl.multiple_of(at * FBLK, FBLK), FBLK)], moved.at[index],
            d_send.at[index], d_recv.at[index], peer_of(at, b, core, ep),
        )
        copy.start()
        weights.append(copy)
    pltpu.make_async_copy(table, table, c_send.at[0]).wait()
    pltpu.make_async_copy(table, table, c_recv.at[0]).wait()

    both = table[...].reshape(PIECES, 2, 128)
    both = both[:, 0, :] + both[:, 1, :]
    lane = lax.broadcasted_iota(jnp.int32, (PIECES, 128), 1)
    counts = jnp.where((lane >= CAP) & (lane < CAP + 8), both * 0.5, 0.0)
    largest = jnp.max(jnp.sum(counts, axis=0, keepdims=True), axis=1, keepdims=True)
    choice[...] = sum((largest > keep).astype(jnp.int32) for keep in SIZES[:-1])
    here = jnp.sum(jnp.where(lane == CAP + ep, counts, 0.0), axis=1, keepdims=True)
    up = lax.broadcasted_iota(jnp.int32, (PIECES, PIECES), 0)
    along = lax.broadcasted_iota(jnp.int32, (PIECES, PIECES), 1)
    here_row = jnp.sum(jnp.where(up == along, here, 0.0), axis=0, keepdims=True)
    start = jnp.sum(jnp.where(along < up, here_row, 0.0), axis=1, keepdims=True)
    start_row = jnp.sum(jnp.where(up < along, here, 0.0), axis=0, keepdims=True)

    spot = lax.broadcasted_iota(jnp.int32, (PIECES, ALL_ROWS), 1)
    inside = lax.div(spot, CAP) == lax.broadcasted_iota(jnp.int32, (PIECES, ALL_ROWS), 0)
    place = lax.rem(spot, CAP).astype(jnp.float32)
    value = jnp.where(inside & (place < here), start + place + 1.0, 0.0)
    at_row[...] = jnp.sum(value, axis=0, keepdims=True).astype(jnp.int32) - 1

    spot = lax.broadcasted_iota(jnp.int32, (ALL_ROWS, PIECES), 0)
    inside = lax.div(spot, CAP) == lax.broadcasted_iota(jnp.int32, (ALL_ROWS, PIECES), 1)
    place = lax.rem(spot, CAP).astype(jnp.float32)
    value = jnp.where(inside & (place < here_row), start_row + place + 1.0, 0.0)
    at_column[...] = jnp.sum(value, axis=1, keepdims=True).astype(jnp.int32) - 1

    squares = jnp.dot(
        jnp.where(inside, 1.0, 0.0), both, preferred_element_type=jnp.float32, precision=lax.Precision.HIGHEST
    )
    spot = lax.broadcasted_iota(jnp.int32, (ALL_ROWS, 128), 0)
    chosen = lax.rem(spot, CAP) == lax.broadcasted_iota(jnp.int32, (ALL_ROWS, 128), 1)
    squares = jnp.sum(jnp.where(chosen, squares, 0.0), axis=1, keepdims=True)
    row_scale = jnp.sqrt(squares / MODEL_WIDTH + EPSILON)
    half_copy.wait()

    pltpu.make_async_copy(x_in, x_in, x_send.at[0]).wait()
    pltpu.make_async_copy(arrived, arrived, x_recv.at[0]).wait()
    pieces = CHUNK // CAP
    for chunk in range(ALL_ROWS // CHUNK):
        part = arrived[chunk * pieces : (chunk + 1) * pieces].reshape(CHUNK, DBLK).astype(jnp.float32)
        part = part / row_scale[chunk * CHUNK : (chunk + 1) * CHUNK]
        landed[chunk * pieces : (chunk + 1) * pieces] = part.astype(jnp.bfloat16).reshape(pieces, CAP, DBLK)
    for copy in weights:
        copy.wait()


def dispatch(x_in, notes, halves, w_down):
    in_vmem, anywhere = pl.BlockSpec(memory_space=pltpu.VMEM), pl.BlockSpec(memory_space=pl.ANY)
    dma = pltpu.SemaphoreType.DMA
    return pl.pallas_call(
        dispatch_kernel,
        out_shape=(
            jax.ShapeDtypeStruct((PIECES, CAP, DBLK), jnp.bfloat16),
            jax.ShapeDtypeStruct((1, ALL_ROWS), jnp.int32),
            jax.ShapeDtypeStruct((ALL_ROWS, 1), jnp.int32),
            jax.ShapeDtypeStruct((1, 1), jnp.int32),
            jax.ShapeDtypeStruct((2, DBLK, FBLK), jnp.bfloat16),
            jax.ShapeDtypeStruct(halves.shape, jnp.float32),
        ),
        in_specs=[anywhere, in_vmem, in_vmem, anywhere],
        out_specs=(in_vmem,) * 4 + (anywhere, in_vmem),
        scratch_shapes=[
            pltpu.VMEM((PIECES, CAP, DBLK), jnp.bfloat16),
            pltpu.VMEM((2 * PIECES, 1, 128), jnp.float32),
            dma((1,)), dma((1,)), dma((1,)), dma((1,)), dma((2,)), dma((2,)), dma((1,)), dma((1,)),
            pltpu.VMEM((CAP, DBLK), jnp.bfloat16),
            pltpu.VMEM((1, 128), jnp.float32),
        ],
        compiler_params=pltpu.CompilerParams(collective_id=1, has_side_effects=True),
        name="dispatch",
    )(x_in, notes, halves, w_down)


def moe_kernel(
    keep, landed, w_gate, w_up, w_down, g1, g2, g3, u1, u2, u3, d13, *refs
):
    if keep < ALL_ROWS:
        at_row, at_column, *refs = refs
    (
        y_out, rows, wg, wu, wd, send, fwd, got, raw, own, hid, part, part32, part_in, total, y_send,
        w_sem, xa_send, xa_recv, rs_send, rs_recv, ag_send, ag_recv,
        o_send, o_recv, y_ssem, y_rsem, d_send, d_recv, spare,
    ) = refs
    quarter, upper, lower = parts_of(keep)
    a, b, core, ep = coordinates()
    grp, tp = lax.axis_index("grp"), lax.axis_index("tp")
    z_hi = lax.div(grp, 4)
    own_block = lax.rem(grp, 4) * 2 + tp

    def peer(at_a, at_b):
        return peer_of(at_a, at_b, core, ep)

    def shifted(value, by):
        return lax.rem(value + by + SIDE, SIDE)

    right, left, across = shifted(b, 1), shifted(b, -1), shifted(b, 2)

    loads = []
    for which, (full, parts, dst) in enumerate(
        (
            (w_gate, ((1, g1), (2, g2), (3, g3)), wg),
            (w_up, ((1, u1), (2, u2), (3, u3)), wu),
            (w_down, ((1, d13.at[0]), (3, d13.at[1])), wd),
        )
    ):
        own_part = full.at[:, pl.ds(pl.multiple_of(a * FBLK, FBLK), FBLK)]
        for step, src in ((0, own_part), *parts):
            row = pl.ds(pl.multiple_of(shifted(a, -step) * DBLK, DBLK), DBLK)
            copy = pltpu.make_async_copy(src, dst.at[row], w_sem.at[which, step])
            copy.start()
            loads.append(copy)

    wait_for_all = greet_all()

    if keep < ALL_ROWS:
        @pl.loop(0, SIDE)
        def _(chunk):
            first = pl.multiple_of(chunk * quarter, 16)
            place = lax.broadcasted_iota(jnp.int32, (quarter, ALL_ROWS), 0) + first
            pick = jnp.where(place == at_row[...], 1.0, 0.0).astype(jnp.bfloat16)
            packed = jnp.dot(pick, landed[...].reshape(ALL_ROWS, DBLK), preferred_element_type=jnp.float32)
            rows[a, pl.ds(first, quarter), :] = packed.astype(jnp.bfloat16)
    else:
        rows[a] = landed[...].reshape(ALL_ROWS, DBLK)

    wait_for_all()

    copies = []
    for step in (2, 1, 3):
        copy = remote(
            rows.at[a], rows.at[a], xa_send.at[step - 1], xa_recv.at[step - 1], peer(shifted(a, step), b)
        )
        copy.start()
        copies.append(copy)
    at = shifted(a, 2)
    copy = remote(
        w_down.at[:, pl.ds(pl.multiple_of(at * FBLK, FBLK), FBLK)],
        wd.at[pl.ds(pl.multiple_of(a * DBLK, DBLK), DBLK)],
        d_send.at[0], d_recv.at[0], peer(at, b),
    )
    copy.start()
    loads.append(copy)
    for copy in loads[: 2 * SIDE]:
        copy.wait()
    for copy in copies:
        copy.wait()

    def product(group, store):
        first = pl.multiple_of(group * quarter, 16)

        @pl.loop(0, FBLK // FT)
        def _(tile):
            lhs = jnp.concatenate([rows[k, pl.ds(first, quarter), :] for k in range(SIDE)], axis=1)
            for part_index, weight in enumerate((wg, wu)):
                cols = pl.ds(pl.multiple_of(tile * FT, FT), FT)
                to = pl.ds(pl.multiple_of(tile * FT + part_index * FBLK, FT), FT)
                value = jnp.dot(lhs, weight[:, cols], preferred_element_type=jnp.float32)
                store(to, value[:upper], value[upper:])

    def store_across(to, top, bottom):
        send[0, :, to] = top.astype(jnp.bfloat16)
        send[1, :lower, to] = bottom.astype(jnp.bfloat16)

    def store_right(to, top, bottom):
        raw[0, :, to] = top
        send[2, :lower, to] = bottom.astype(jnp.bfloat16)

    def store_left(to, top, bottom):
        send[3, :, to] = top.astype(jnp.bfloat16)
        raw[1, :lower, to] = bottom

    def store_own(to, top, bottom):
        own[:upper, to] = top
        own[upper:, to] = bottom

    def add_arrived(slot, which, count):
        @pl.loop(0, 2 * FBLK // FT)
        def _(tile):
            to = pl.ds(pl.multiple_of(tile * FT, FT), FT)
            value = raw[which, :count, to] + fwd[which, :count, to].astype(jnp.float32)
            send[slot, :count, to] = value.astype(jnp.bfloat16)

    def pass_on(slot, count, dst, to):
        copy = remote(send.at[slot, pl.ds(0, count)], dst.at[pl.ds(0, count)], rs_send.at[slot], rs_recv.at[slot], to)
        copy.start()
        return copy

    to_right, to_left = peer(a, right), peer(a, left)
    product(across, store_across)
    over_right = pass_on(0, upper, fwd.at[0], to_right)
    over_left = pass_on(1, lower, fwd.at[1], to_left)
    product(right, store_right)
    plain_right = pass_on(2, lower, got.at[1], to_right)
    product(left, store_left)
    plain_left = pass_on(3, upper, got.at[2], to_left)
    product(b, store_own)
    over_right.wait()
    add_arrived(4, 0, upper)
    sum_right = pass_on(4, upper, got.at[0], to_right)
    over_left.wait()
    add_arrived(5, 1, lower)
    sum_left = pass_on(5, lower, got.at[3], to_left)

    for copy in (plain_right, plain_left, sum_right, sum_left):
        copy.wait()

    @pl.loop(0, FBLK // FT)
    def _(tile):
        cols = pl.ds(pl.multiple_of(tile * FT, FT), FT)
        ups = pl.ds(pl.multiple_of(tile * FT + FBLK, FT), FT)
        for half, (begin, count) in enumerate(((0, upper), (upper, lower))):

            def whole(which):
                return (
                    own[begin : begin + count, which]
                    + got[half, :count, which].astype(jnp.float32)
                    + got[2 + half, :count, which].astype(jnp.float32)
                )

            gate, up = whole(cols), whole(ups)
            hid[b, begin : begin + count, cols] = (gate / (1.0 + jnp.exp(-gate)) * up).astype(jnp.bfloat16)

    own_right = remote(hid.at[b], hid.at[b], ag_send.at[0], ag_recv.at[0], to_right)
    own_left = remote(hid.at[b], hid.at[b], ag_send.at[1], ag_recv.at[1], to_left)
    own_right.start()
    own_left.start()
    for copy in loads[2 * SIDE :]:
        copy.wait()

    o_copies = {}

    def down(order, group):
        lhs = hid[group]

        def block(step):
            cols = pl.ds(pl.multiple_of(lax.rem(a + step, SIDE) * DBLK, DBLK), DBLK)
            return lax.dot_general(lhs, wd[cols, :], (((1,), (1,)), ((), ())), preferred_element_type=jnp.float32)

        @pl.loop(1, SIDE)
        def _(step):
            part[order, step - 1] = block(step).astype(jnp.bfloat16)

        for step in (2, 1, 3):
            copy = remote(
                part.at[order, step - 1], part_in.at[order, step - 1],
                o_send.at[order, step - 1], o_recv.at[order, step - 1], peer(shifted(a, step), b),
            )
            copy.start()
            o_copies[order, step] = copy
        part32[order] = block(0)

    def finish(order, group):
        value = part32[order]
        for step in range(1, SIDE):
            o_copies[order, step].wait()
            value = value + part_in[order, step - 1].astype(jnp.float32)
        total[pl.ds(pl.multiple_of(group * quarter, 16), quarter), :] = value.astype(jnp.bfloat16)

    down(0, b)
    own_right.wait()
    top, bottom = pl.ds(0, upper), pl.ds(upper, lower)
    on_right = remote(hid.at[left, top], hid.at[left, top], ag_send.at[2], ag_recv.at[2], to_right)
    on_right.start()
    own_left.wait()
    on_left = remote(hid.at[right, bottom], hid.at[right, bottom], ag_send.at[3], ag_recv.at[3], to_left)
    on_left.start()
    down(1, left)
    down(3, right)
    finish(0, b)
    on_right.wait()
    on_left.wait()
    down(2, across)
    finish(1, left)
    finish(3, right)
    finish(2, across)

    if keep < ALL_ROWS:
        @pl.loop(0, ALL_ROWS // CHUNK)
        def _(chunk):
            place = lax.broadcasted_iota(jnp.int32, (CHUNK, keep), 1)
            at = at_column[pl.ds(pl.multiple_of(chunk * CHUNK, CHUNK), CHUNK), :]
            pick = jnp.where(place == at, 1.0, 0.0).astype(jnp.bfloat16)
            spread = jnp.dot(pick, total[...], preferred_element_type=jnp.float32)
            first = pl.multiple_of(chunk * (CHUNK // CAP), CHUNK // CAP)
            y_send[pl.ds(first, CHUNK // CAP)] = spread.astype(jnp.bfloat16).reshape(CHUNK // CAP, CAP, DBLK)
    else:
        y_send[...] = total[...].reshape(PIECES, CAP, DBLK)

    def source_of(step):
        return lax.rem(grp * 8 + ep + step, PIECES)

    deliver(
        PIECES,
        lambda step: y_send.at[source_of(step)],
        lambda step: y_out.at[ep, :, pl.ds(pl.multiple_of(own_block * DBLK, DBLK), DBLK)],
        lambda step: (lax.div(source_of(step), 8), lax.rem(source_of(step), 8), z_hi),
        y_ssem, y_rsem, spare,
    )
    pltpu.make_async_copy(y_send, y_send, y_ssem.at[0]).wait()
    pltpu.make_async_copy(y_out, y_out, y_rsem.at[0]).wait()


def expert_layer(keep, landed, w_gate, w_up, w_down, moved, places=()):
    bf16, f32 = jnp.bfloat16, jnp.float32
    dma = pltpu.SemaphoreType.DMA
    quarter, upper, _ = parts_of(keep)
    scratch = [
        pltpu.VMEM((SIDE, keep, DBLK), bf16),
        pltpu.VMEM((DSET, FBLK), bf16),
        pltpu.VMEM((DSET, FBLK), bf16),
        pltpu.VMEM((DSET, FBLK), bf16),
        pltpu.VMEM((6, upper, 2 * FBLK), bf16),
        pltpu.VMEM((2, upper, 2 * FBLK), bf16),
        pltpu.VMEM((4, upper, 2 * FBLK), bf16),
        pltpu.VMEM((2, upper, 2 * FBLK), f32),
        pltpu.VMEM((quarter, 2 * FBLK), f32),
        pltpu.VMEM((SIDE, quarter, FBLK), bf16),
        pltpu.VMEM((SIDE, SIDE - 1, quarter, DBLK), bf16),
        pltpu.VMEM((SIDE, quarter, DBLK), f32),
        pltpu.VMEM((SIDE, SIDE - 1, quarter, DBLK), bf16),
        pltpu.VMEM((keep, DBLK), bf16),
        pltpu.VMEM((PIECES, CAP, DBLK), bf16),
        dma((3, SIDE)),
        dma((3,)), dma((3,)),
        dma((6,)), dma((6,)),
        dma((4,)), dma((4,)),
        dma((SIDE, 3)), dma((SIDE, 3)),
        dma((1,)), dma((1,)),
        dma((1,)), dma((1,)),
        pltpu.VMEM((CAP, DBLK), bf16),
    ]
    anywhere, in_vmem = pl.BlockSpec(memory_space=pl.ANY), pl.BlockSpec(memory_space=pltpu.VMEM)
    return pl.pallas_call(
        functools.partial(moe_kernel, keep),
        out_shape=jax.ShapeDtypeStruct((8, CAP, 8 * DBLK), bf16),
        in_specs=[in_vmem] + [anywhere] * 10 + [in_vmem] * len(places),
        out_specs=anywhere,
        scratch_shapes=scratch,
        compiler_params=pltpu.CompilerParams(
            collective_id=keep // 64, has_side_effects=True, vmem_limit_bytes=60 * 1024 * 1024
        ),
        cost_estimate=pl.CostEstimate(
            flops=13 * 10**6 * keep, bytes_accessed=14 * 10**6, transcendentals=10**6
        ),
        name="expert_layer",
    )(landed, w_gate, w_up, w_down, *moved, *places)


def attend_kernel(lengths, queries, token_key_value, cache, attended):
    step = pl.program_id(0)
    share = QUERY_HEADS // KEY_VALUE_HEADS
    heads = queries.shape[1]
    width = cache.shape[3]
    score_scale = HEAD_SIZE ** (-0.5)
    head = lax.broadcasted_iota(jnp.int32, (heads, width), 0)
    column = lax.broadcasted_iota(jnp.int32, (heads, width), 1)
    matches = lax.div(head, share) == lax.div(column, HEAD_SIZE)
    position = lax.broadcasted_iota(jnp.int32, (heads, cache.shape[2]), 1)

    def own_part(wide):
        wide = jnp.where(matches, wide, 0.0)
        return sum(wide[:, k * HEAD_SIZE : (k + 1) * HEAD_SIZE] for k in range(width // HEAD_SIZE))

    for i in range(SEQS):
        query = queries[i].astype(jnp.float32)
        query = jnp.where(matches, jnp.concatenate([query] * (width // HEAD_SIZE), axis=1), 0.0)
        new = token_key_value[i].astype(jnp.float32)
        scores = lax.dot_general(
            query.astype(jnp.bfloat16), cache[i, 0], (((1,), (1,)), ((), ())), preferred_element_type=jnp.float32
        )
        scores = jnp.where(position < lengths[step * SEQS + i], scores * score_scale, -jnp.inf)
        self_score = jnp.sum(query * new[0:1, :], axis=1, keepdims=True) * score_scale
        highest = jnp.maximum(jnp.max(scores, axis=1, keepdims=True), self_score)
        exponent = jnp.exp(scores - highest)
        own_exp = jnp.exp(self_score - highest)
        totals = jnp.sum(exponent, axis=1, keepdims=True) + own_exp
        normalized = (exponent / totals).astype(jnp.bfloat16)
        own_weight = (own_exp / totals).astype(jnp.bfloat16).astype(jnp.float32)
        mixture = jnp.dot(normalized, cache[i, 1], preferred_element_type=jnp.float32)
        mixture = own_part(mixture) + own_weight * own_part(jnp.broadcast_to(new[1:2, :], (heads, width)))
        attended[i] = mixture.astype(jnp.bfloat16)


def attend_local(queries, token_key_value, cache, cache_length):
    seq_count, _, positions, width = cache.shape
    heads = queries.shape[1] // HEAD_SIZE
    attended = pl.pallas_call(
        attend_kernel,
        out_shape=jax.ShapeDtypeStruct((seq_count, heads, HEAD_SIZE), jnp.bfloat16),
        grid_spec=pltpu.PrefetchScalarGridSpec(
            num_scalar_prefetch=1,
            grid=(seq_count // SEQS,),
            in_specs=[
                pl.BlockSpec((SEQS, heads, HEAD_SIZE), lambda i, _: (i, 0, 0)),
                pl.BlockSpec((SEQS, 2, width), lambda i, _: (i, 0, 0)),
                pl.BlockSpec((SEQS, 2, positions, width), lambda i, _: (i, 0, 0, 0)),
            ],
            out_specs=pl.BlockSpec((SEQS, heads, HEAD_SIZE), lambda i, _: (i, 0, 0)),
        ),
        cost_estimate=pl.CostEstimate(
            flops=4 * seq_count * heads * positions * width,
            bytes_accessed=2 * cache.size,
            transcendentals=seq_count * heads * positions,
        ),
        name="attention",
    )(cache_length, queries.reshape(seq_count, heads, HEAD_SIZE), token_key_value, cache)
    return attended.reshape(seq_count, heads * HEAD_SIZE)


def per_device(
    residual,
    queries,
    token_key_value,
    cache,
    cache_length,
    active,
    routes,
    norm_gain,
    router,
    w_gate,
    w_up,
    w_down,
):
    seq_count = residual.shape[0]
    expert_count = router.shape[1]
    slot_total = CAP * expert_count
    still_live = active == 1
    flat_expert = routes.reshape(-1)
    flat_live = jnp.repeat(still_live, 2)
    onehot = (
        (flat_expert[:, None] == jnp.arange(expert_count, dtype=jnp.int32)[None, :])
        & flat_live[:, None]
    ).astype(jnp.int32)
    before = jnp.cumsum(onehot, axis=0) - onehot
    rank_order = jnp.sum(before * onehot, axis=1)
    slot_index = flat_expert * CAP + rank_order
    w_gate, w_up, w_down = w_gate[0], w_up[0], w_down[0]
    line_rank = coordinates()[0]
    moved = []
    for weight in (w_gate, w_up):
        for step in range(1, SIDE):
            column = lax.rem(line_rank + step, SIDE) * FBLK
            piece = lax.dynamic_slice(weight, (0, column), (DBLK, FBLK))
            moved.append(lax.ppermute(piece, MESH_AXES, line_permutation(step)))
    attention_output = attend_local(queries, token_key_value, cache, cache_length)
    state = residual.astype(jnp.float32) + attention_output.astype(jnp.float32)
    scaled = state * norm_gain.astype(jnp.float32)[None, :]
    squares = jnp.sum(state * state, axis=1)
    raw_logits = jnp.dot(scaled, router.astype(jnp.float32), precision=lax.Precision.HIGHEST)
    selector = (
        (
            (slot_index[:, None] == jnp.arange(slot_total, dtype=jnp.int32)[None, :])
            & flat_live[:, None]
        )
        .astype(jnp.bfloat16)
        .reshape(seq_count, 2, slot_total)
    )
    senders = selector[:, 0] + selector[:, 1]
    outgoing = lax.dot_general(
        senders, scaled.astype(jnp.bfloat16), (((0,), (0,)), ((), ())), preferred_element_type=jnp.float32
    )
    outgoing = outgoing.astype(jnp.bfloat16).reshape(expert_count, CAP, residual.shape[1])
    slot_squares = jnp.sum(senders.astype(jnp.float32) * squares[:, None], axis=0).reshape(expert_count, CAP)
    counts = jnp.broadcast_to(jnp.sum(onehot, axis=0).astype(jnp.float32), (expert_count, expert_count))
    notes = jnp.concatenate([slot_squares, counts, jnp.zeros((expert_count, 128 - CAP - 8), jnp.float32)], axis=1)
    own_half = jnp.concatenate(
        [raw_logits, squares[:, None], jnp.zeros((seq_count, 128 - expert_count - 1), jnp.float32)], axis=1
    )
    landed, at_row, at_column, choice, down_moved, other_half = dispatch(
        outgoing, notes.reshape(expert_count, 1, 128), own_half, w_down
    )
    both_halves = own_half + other_half
    row_scale = jnp.sqrt(both_halves[:, expert_count] / MODEL_WIDTH + EPSILON)[:, None]
    logits = both_halves[:, :expert_count] / row_scale
    chosen = jnp.take_along_axis(logits, routes, axis=1)
    weight_first = jax.nn.sigmoid(chosen[:, 0] - chosen[:, 1])
    weight_second = 1.0 - weight_first
    branches = [
        functools.partial(lambda keep, views, *args: expert_layer(keep, *args, views[: 2 * (keep < ALL_ROWS)]), keep)
        for keep in SIZES
    ]
    returned = lax.switch(
        choice[0, 0], branches, (at_row, at_column), landed, w_gate, w_up, w_down, (*moved, down_moved)
    )
    returned = returned.reshape(slot_total, residual.shape[1])
    pick_first = jnp.dot(selector[:, 0], returned, preferred_element_type=jnp.float32)
    pick_second = jnp.dot(selector[:, 1], returned, preferred_element_type=jnp.float32)
    moe_sum = weight_first[:, None] * pick_first + weight_second[:, None] * pick_second
    delta = jnp.where(still_live[:, None], attention_output.astype(jnp.float32) + moe_sum, 0.0)
    return delta.astype(jnp.bfloat16)


def solution(mesh):
    in_specs = (
        P(("grp", "ep"), "tp"),
        P(("grp", "ep"), "tp"),
        P(("grp", "ep"), None, "tp"),
        P(("grp", "ep"), None, None, "tp"),
        P(("grp", "ep")),
        P(("grp", "ep")),
        P(("grp", "ep"), None),
        P("tp"),
        P("tp", None),
        P("ep", ("grp", "tp"), None),
        P("ep", ("grp", "tp"), None),
        P("ep", ("grp", "tp"), None),
    )
    out_specs = P(("grp", "ep"), "tp")
    return jax.shard_map(
        per_device, mesh=mesh, in_specs=in_specs, out_specs=out_specs, check_vma=False
    )
```

```python
import functools

import jax
import jax.numpy as jnp
from jax import lax
from jax.experimental import pallas as pl
from jax.experimental.pallas import tpu as pltpu
from jax.sharding import PartitionSpec as P

MODEL_WIDTH = 4096
QUERY_HEADS = 32
KEY_VALUE_HEADS = 8
HEAD_SIZE = 128


EPSILON = 1e-05

SIDE = 4
DEVICES = 128
CAP = 16
PIECES = 64
ALL_ROWS = PIECES * CAP
CHUNK = 128
SEQS = 4
SIZES = (512, 576, 704, ALL_ROWS)
DBLK = 256
DSET = SIDE * DBLK
FBLK = 2048
FT = 512
MESH_AXES = ("grp", "ep", "tp")
MESH_ID = pl.DeviceIdType.MESH


def line_permutation(step):
    pairs = []
    for grp in range(8):
        for ep in range(8):
            for tp in range(2):
                x, z = grp % 4, (grp // 4) * 2 + tp
                if ep % 2 == 0:
                    x2, z2 = (x + step) % SIDE, z
                else:
                    x2, z2 = x, (z + step) % SIDE
                pairs.append(((grp * 8 + ep) * 2 + tp, (((z2 // 2) * 4 + x2) * 8 + ep) * 2 + z2 % 2))
    return pairs


def coordinates():
    grp, ep, tp = (lax.axis_index(name) for name in MESH_AXES)
    x = lax.rem(grp, 4)
    z = lax.div(grp, 4) * 2 + tp
    core = lax.rem(ep, 2)
    return x + (z - x) * core, z + (x - z) * core, core, ep


def parts_of(keep):
    quarter = keep // SIDE
    upper = (quarter + 31) // 32 * 16
    return quarter, upper, quarter - upper


def peer_of(a, b, core, ep):
    x = a + (b - a) * core
    z = b + (a - b) * core
    return (lax.div(z, 2) * 4 + x, ep, lax.rem(z, 2))


def greet_all():
    itself = own_id()
    barrier = pltpu.get_barrier_semaphore()

    @pl.loop(1, DEVICES)
    def _(step):
        at = lax.rem(itself + step, DEVICES)
        to = (lax.div(at, 16), lax.rem(lax.div(at, 2), 8), lax.rem(at, 2))
        pl.semaphore_signal(barrier, inc=1, device_id=to, device_id_type=MESH_ID)

    return lambda: pl.semaphore_wait(barrier, DEVICES - 1)


def own_id():
    grp, ep, tp = (lax.axis_index(name) for name in MESH_AXES)
    return (grp * 8 + ep) * 2 + tp


def remote(src, dst, ssem, rsem, to):
    return pltpu.make_async_remote_copy(
        src_ref=src, dst_ref=dst, send_sem=ssem, recv_sem=rsem, device_id=to, device_id_type=MESH_ID
    )


def deliver(count, src_of, dst_of, to_of, sends, recvs, spare):
    itself = own_id()

    @pl.loop(0, count)
    def _(step):
        to = to_of(step)
        far = (to[0] * 8 + to[1]) * 2 + to[2] != itself

        @pl.when(far)
        def _():
            remote(src_of(step), dst_of(step), sends.at[0], recvs.at[0], to).start()

        @pl.when(jnp.logical_not(far))
        def _():
            pltpu.make_async_copy(src_of(step), dst_of(step), recvs.at[0]).start()
            pltpu.make_async_copy(src_of(step), spare, sends.at[0]).start()


def dispatch_kernel(
    x_in, notes, halves, picks, w_down, landed, at_row, at_column, choice, moved, weight_first,
    other_half, arrived, table, x_send, x_recv, c_send, c_recv, d_send, d_recv, h_send, h_recv, spare, c_spare,
):
    grp, ep, tp = (lax.axis_index(name) for name in MESH_AXES)
    source = grp * 8 + ep
    own_block = lax.rem(grp, 4) * 2 + tp
    greet_all()()

    half_copy = remote(halves, other_half, h_send.at[0], h_recv.at[0], (grp, ep, 1 - tp))
    half_copy.start()

    def notes_to(step):
        at = lax.rem(own_id() + step, DEVICES)
        return (lax.div(at, 16), lax.rem(lax.div(at, 2), 8), lax.rem(at, 2))

    deliver(
        DEVICES, lambda step: notes.at[notes_to(step)[1]], lambda step: table.at[source * 2 + tp], notes_to,
        c_send, c_recv, c_spare,
    )

    def expert_of(step):
        return lax.rem(ep + lax.div(step, 8), 8)

    def block_of(step):
        return lax.rem(own_block + step, 8)

    deliver(
        PIECES,
        lambda step: x_in.at[expert_of(step), :, pl.ds(pl.multiple_of(block_of(step) * DBLK, DBLK), DBLK)],
        lambda step: arrived.at[source],
        lambda step: (tp * 4 + lax.div(block_of(step), 2), expert_of(step), lax.rem(block_of(step), 2)),
        x_send, x_recv, spare,
    )

    a, b, core, _ = coordinates()
    weights = []
    for index, step in enumerate((1, 3)):
        at = lax.rem(a + step, SIDE)
        copy = remote(
            w_down.at[:, pl.ds(pl.multiple_of(at * FBLK, FBLK), FBLK)], moved.at[index],
            d_send.at[index], d_recv.at[index], peer_of(at, b, core, ep),
        )
        copy.start()
        weights.append(copy)
    pltpu.make_async_copy(table, table, c_send.at[0]).wait()
    pltpu.make_async_copy(table, table, c_recv.at[0]).wait()

    both = table[...].reshape(PIECES, 2, 128)
    both = both[:, 0, :] + both[:, 1, :]
    lane = lax.broadcasted_iota(jnp.int32, (PIECES, 128), 1)
    counts = jnp.where((lane >= CAP) & (lane < CAP + 8), both * 0.5, 0.0)
    largest = jnp.max(jnp.sum(counts, axis=0, keepdims=True), axis=1, keepdims=True)
    choice[...] = sum((largest > keep).astype(jnp.int32) for keep in SIZES[:-1])
    here = jnp.sum(jnp.where(lane == CAP + ep, counts, 0.0), axis=1, keepdims=True)
    up = lax.broadcasted_iota(jnp.int32, (PIECES, PIECES), 0)
    along = lax.broadcasted_iota(jnp.int32, (PIECES, PIECES), 1)
    here_row = jnp.sum(jnp.where(up == along, here, 0.0), axis=0, keepdims=True)
    start = jnp.sum(jnp.where(along < up, here_row, 0.0), axis=1, keepdims=True)
    start_row = jnp.sum(jnp.where(up < along, here, 0.0), axis=0, keepdims=True)

    spot = lax.broadcasted_iota(jnp.int32, (PIECES, ALL_ROWS), 1)
    inside = lax.div(spot, CAP) == lax.broadcasted_iota(jnp.int32, (PIECES, ALL_ROWS), 0)
    place = lax.rem(spot, CAP).astype(jnp.float32)
    value = jnp.where(inside & (place < here), start + place + 1.0, 0.0)
    at_row[...] = jnp.sum(value, axis=0, keepdims=True).astype(jnp.int32) - 1

    spot = lax.broadcasted_iota(jnp.int32, (ALL_ROWS, PIECES), 0)
    inside = lax.div(spot, CAP) == lax.broadcasted_iota(jnp.int32, (ALL_ROWS, PIECES), 1)
    place = lax.rem(spot, CAP).astype(jnp.float32)
    value = jnp.where(inside & (place < here_row), start_row + place + 1.0, 0.0)
    at_column[...] = jnp.sum(value, axis=1, keepdims=True).astype(jnp.int32) - 1

    squares = jnp.dot(
        jnp.where(inside, 1.0, 0.0), both, preferred_element_type=jnp.float32, precision=lax.Precision.HIGHEST
    )
    spot = lax.broadcasted_iota(jnp.int32, (ALL_ROWS, 128), 0)
    chosen = lax.rem(spot, CAP) == lax.broadcasted_iota(jnp.int32, (ALL_ROWS, 128), 1)
    squares = jnp.sum(jnp.where(chosen, squares, 0.0), axis=1, keepdims=True)
    row_scale = jnp.sqrt(squares / MODEL_WIDTH + EPSILON)

    half_copy.wait()
    both = halves[...] + other_half[...]
    lane = lax.broadcasted_iota(jnp.int32, both.shape, 1)
    scale = jnp.sum(jnp.where(lane == 8, both, 0.0), axis=1, keepdims=True)
    scale = jnp.sqrt(scale / MODEL_WIDTH + EPSILON)
    difference = jnp.sum(picks[...] * (both / scale), axis=1, keepdims=True)
    weight_first[...] = 1.0 / (1.0 + jnp.exp(-difference))

    pltpu.make_async_copy(x_in, x_in, x_send.at[0]).wait()
    pltpu.make_async_copy(arrived, arrived, x_recv.at[0]).wait()
    pieces = CHUNK // CAP
    for chunk in range(ALL_ROWS // CHUNK):
        part = arrived[chunk * pieces : (chunk + 1) * pieces].reshape(CHUNK, DBLK).astype(jnp.float32)
        part = part / row_scale[chunk * CHUNK : (chunk + 1) * CHUNK]
        landed[chunk * pieces : (chunk + 1) * pieces] = part.astype(jnp.bfloat16).reshape(pieces, CAP, DBLK)
    for copy in weights:
        copy.wait()


def dispatch(x_in, notes, halves, picks, w_down):
    in_vmem, anywhere = pl.BlockSpec(memory_space=pltpu.VMEM), pl.BlockSpec(memory_space=pl.ANY)
    dma = pltpu.SemaphoreType.DMA
    return pl.pallas_call(
        dispatch_kernel,
        out_shape=(
            jax.ShapeDtypeStruct((PIECES, CAP, DBLK), jnp.bfloat16),
            jax.ShapeDtypeStruct((1, ALL_ROWS), jnp.int32),
            jax.ShapeDtypeStruct((ALL_ROWS, 1), jnp.int32),
            jax.ShapeDtypeStruct((1, 1), jnp.int32),
            jax.ShapeDtypeStruct((2, DBLK, FBLK), jnp.bfloat16),
            jax.ShapeDtypeStruct((halves.shape[0], 1), jnp.float32),
        ),
        in_specs=[anywhere, in_vmem, in_vmem, in_vmem, anywhere],
        out_specs=(in_vmem,) * 4 + (anywhere, in_vmem),
        scratch_shapes=[
            pltpu.VMEM(halves.shape, jnp.float32),
            pltpu.VMEM((PIECES, CAP, DBLK), jnp.bfloat16),
            pltpu.VMEM((2 * PIECES, 1, 128), jnp.float32),
            dma((1,)), dma((1,)), dma((1,)), dma((1,)), dma((2,)), dma((2,)), dma((1,)), dma((1,)),
            pltpu.VMEM((CAP, DBLK), jnp.bfloat16),
            pltpu.VMEM((1, 128), jnp.float32),
        ],
        compiler_params=pltpu.CompilerParams(collective_id=1, has_side_effects=True),
        name="dispatch",
    )(x_in, notes, halves, picks, w_down)


def moe_kernel(
    keep, landed, w_gate, w_up, w_down, g1, g2, g3, u1, u2, u3, d13, *refs
):
    if keep < ALL_ROWS:
        at_row, at_column, *refs = refs
    (
        y_out, rows, wg, wu, wd, send, fwd, got, raw, own, hid, part, part32, part_in, total, y_send,
        w_sem, xa_send, xa_recv, rs_send, rs_recv, ag_send, ag_recv,
        o_send, o_recv, y_ssem, y_rsem, d_send, d_recv, spare,
    ) = refs
    quarter, upper, lower = parts_of(keep)
    a, b, core, ep = coordinates()
    grp, tp = lax.axis_index("grp"), lax.axis_index("tp")
    z_hi = lax.div(grp, 4)
    own_block = lax.rem(grp, 4) * 2 + tp

    def peer(at_a, at_b):
        return peer_of(at_a, at_b, core, ep)

    def shifted(value, by):
        return lax.rem(value + by + SIDE, SIDE)

    right, left, across = shifted(b, 1), shifted(b, -1), shifted(b, 2)

    loads = []
    for which, (full, parts, dst) in enumerate(
        (
            (w_gate, ((1, g1), (2, g2), (3, g3)), wg),
            (w_up, ((1, u1), (2, u2), (3, u3)), wu),
            (w_down, ((1, d13.at[0]), (3, d13.at[1])), wd),
        )
    ):
        own_part = full.at[:, pl.ds(pl.multiple_of(a * FBLK, FBLK), FBLK)]
        for step, src in ((0, own_part), *parts):
            row = pl.ds(pl.multiple_of(shifted(a, -step) * DBLK, DBLK), DBLK)
            copy = pltpu.make_async_copy(src, dst.at[row], w_sem.at[which, step])
            copy.start()
            loads.append(copy)

    wait_for_all = greet_all()

    if keep < ALL_ROWS:
        @pl.loop(0, SIDE)
        def _(chunk):
            first = pl.multiple_of(chunk * quarter, 16)
            place = lax.broadcasted_iota(jnp.int32, (quarter, ALL_ROWS), 0) + first
            pick = jnp.where(place == at_row[...], 1.0, 0.0).astype(jnp.bfloat16)
            packed = jnp.dot(pick, landed[...].reshape(ALL_ROWS, DBLK), preferred_element_type=jnp.float32)
            rows[a, pl.ds(first, quarter), :] = packed.astype(jnp.bfloat16)
    else:
        rows[a] = landed[...].reshape(ALL_ROWS, DBLK)

    wait_for_all()

    turns = (across, right, left, b)
    copies = {}
    for turn, group in enumerate(turns):
        piece = pl.ds(pl.multiple_of(group * quarter, 16), quarter)
        for step in (2, 1, 3):
            copy = remote(
                rows.at[a, piece], rows.at[a, piece],
                xa_send.at[turn, step - 1], xa_recv.at[turn, step - 1], peer(shifted(a, step), b),
            )
            copy.start()
            copies[turn, step] = copy
    at = shifted(a, 2)
    copy = remote(
        w_down.at[:, pl.ds(pl.multiple_of(at * FBLK, FBLK), FBLK)],
        wd.at[pl.ds(pl.multiple_of(a * DBLK, DBLK), DBLK)],
        d_send.at[0], d_recv.at[0], peer(at, b),
    )
    copy.start()
    loads.append(copy)
    for copy in loads[: 2 * SIDE]:
        copy.wait()

    def product(turn, store):
        group = turns[turn]
        for step in range(1, SIDE):
            copies[turn, step].wait()
        first = pl.multiple_of(group * quarter, 16)

        @pl.loop(0, FBLK // FT)
        def _(tile):
            lhs = jnp.concatenate([rows[k, pl.ds(first, quarter), :] for k in range(SIDE)], axis=1)
            for part_index, weight in enumerate((wg, wu)):
                cols = pl.ds(pl.multiple_of(tile * FT, FT), FT)
                to = pl.ds(pl.multiple_of(tile * FT + part_index * FBLK, FT), FT)
                value = jnp.dot(lhs, weight[:, cols], preferred_element_type=jnp.float32)
                store(to, value[:upper], value[upper:])

    def store_across(to, top, bottom):
        send[0, :, to] = top.astype(jnp.bfloat16)
        send[1, :lower, to] = bottom.astype(jnp.bfloat16)

    def store_right(to, top, bottom):
        raw[0, :, to] = top
        send[2, :lower, to] = bottom.astype(jnp.bfloat16)

    def store_left(to, top, bottom):
        send[3, :, to] = top.astype(jnp.bfloat16)
        raw[1, :lower, to] = bottom

    def store_own(to, top, bottom):
        own[:upper, to] = top
        own[upper:, to] = bottom

    def add_arrived(slot, which, count):
        @pl.loop(0, 2 * FBLK // FT)
        def _(tile):
            to = pl.ds(pl.multiple_of(tile * FT, FT), FT)
            value = raw[which, :count, to] + fwd[which, :count, to].astype(jnp.float32)
            send[slot, :count, to] = value.astype(jnp.bfloat16)

    def pass_on(slot, count, dst, to):
        copy = remote(send.at[slot, pl.ds(0, count)], dst.at[pl.ds(0, count)], rs_send.at[slot], rs_recv.at[slot], to)
        copy.start()
        return copy

    to_right, to_left = peer(a, right), peer(a, left)
    product(0, store_across)
    over_right = pass_on(0, upper, fwd.at[0], to_right)
    over_left = pass_on(1, lower, fwd.at[1], to_left)
    product(1, store_right)
    plain_right = pass_on(2, lower, got.at[1], to_right)
    product(2, store_left)
    plain_left = pass_on(3, upper, got.at[2], to_left)
    product(3, store_own)
    over_right.wait()
    add_arrived(4, 0, upper)
    sum_right = pass_on(4, upper, got.at[0], to_right)
    over_left.wait()
    add_arrived(5, 1, lower)
    sum_left = pass_on(5, lower, got.at[3], to_left)

    def activate(half, begin, count):
        @pl.loop(0, FBLK // FT)
        def _(tile):
            def whole(which):
                return (
                    own[begin : begin + count, which]
                    + got[half, :count, which].astype(jnp.float32)
                    + got[2 + half, :count, which].astype(jnp.float32)
                )

            cols = pl.ds(pl.multiple_of(tile * FT, FT), FT)
            gate, up = whole(cols), whole(pl.ds(pl.multiple_of(tile * FT + FBLK, FT), FT))
            hid[b, begin : begin + count, cols] = (gate / (1.0 + jnp.exp(-gate)) * up).astype(jnp.bfloat16)

    def spread_half(index, owner, which, to):
        copy = remote(hid.at[owner, which], hid.at[owner, which], ag_send.at[index], ag_recv.at[index], to)
        copy.start()
        return copy

    top, bottom = pl.ds(0, upper), pl.ds(upper, lower)
    plain_right.wait()
    plain_left.wait()
    sum_right.wait()
    activate(0, 0, upper)
    top_right = spread_half(0, b, top, to_right)
    top_left = spread_half(1, b, top, to_left)
    sum_left.wait()
    activate(1, upper, lower)
    bottom_left = spread_half(3, b, bottom, to_left)
    bottom_right = spread_half(2, b, bottom, to_right)
    for copy in loads[2 * SIDE :]:
        copy.wait()

    o_copies = {}

    def down(order, group):
        lhs = hid[group]

        def block(step):
            cols = pl.ds(pl.multiple_of(lax.rem(a + step, SIDE) * DBLK, DBLK), DBLK)
            return lax.dot_general(lhs, wd[cols, :], (((1,), (1,)), ((), ())), preferred_element_type=jnp.float32)

        @pl.loop(1, SIDE)
        def _(step):
            part[order, step - 1] = block(step).astype(jnp.bfloat16)

        for step in (2, 1, 3):
            copy = remote(
                part.at[order, step - 1], part_in.at[order, step - 1],
                o_send.at[order, step - 1], o_recv.at[order, step - 1], peer(shifted(a, step), b),
            )
            copy.start()
            o_copies[order, step] = copy
        part32[order] = block(0)

    def finish(order, group):
        value = part32[order]
        for step in range(1, SIDE):
            o_copies[order, step].wait()
            value = value + part_in[order, step - 1].astype(jnp.float32)
        total[pl.ds(pl.multiple_of(group * quarter, 16), quarter), :] = value.astype(jnp.bfloat16)

    down(0, b)
    top_right.wait()
    on_right = spread_half(4, left, top, to_right)
    bottom_left.wait()
    on_left = spread_half(5, right, bottom, to_left)
    top_left.wait()
    bottom_right.wait()
    down(1, left)
    down(3, right)
    finish(0, b)
    on_right.wait()
    on_left.wait()
    down(2, across)
    finish(1, left)
    finish(3, right)
    finish(2, across)

    if keep < ALL_ROWS:
        @pl.loop(0, ALL_ROWS // CHUNK)
        def _(chunk):
            place = lax.broadcasted_iota(jnp.int32, (CHUNK, keep), 1)
            at = at_column[pl.ds(pl.multiple_of(chunk * CHUNK, CHUNK), CHUNK), :]
            pick = jnp.where(place == at, 1.0, 0.0).astype(jnp.bfloat16)
            spread = jnp.dot(pick, total[...], preferred_element_type=jnp.float32)
            first = pl.multiple_of(chunk * (CHUNK // CAP), CHUNK // CAP)
            y_send[pl.ds(first, CHUNK // CAP)] = spread.astype(jnp.bfloat16).reshape(CHUNK // CAP, CAP, DBLK)
    else:
        y_send[...] = total[...].reshape(PIECES, CAP, DBLK)

    def source_of(step):
        return lax.rem(grp * 8 + ep + step, PIECES)

    deliver(
        PIECES,
        lambda step: y_send.at[source_of(step)],
        lambda step: y_out.at[ep, :, pl.ds(pl.multiple_of(own_block * DBLK, DBLK), DBLK)],
        lambda step: (lax.div(source_of(step), 8), lax.rem(source_of(step), 8), z_hi),
        y_ssem, y_rsem, spare,
    )
    pltpu.make_async_copy(y_send, y_send, y_ssem.at[0]).wait()
    pltpu.make_async_copy(y_out, y_out, y_rsem.at[0]).wait()


def expert_layer(keep, landed, w_gate, w_up, w_down, moved, places=()):
    bf16, f32 = jnp.bfloat16, jnp.float32
    dma = pltpu.SemaphoreType.DMA
    quarter, upper, _ = parts_of(keep)
    scratch = [
        pltpu.VMEM((SIDE, keep, DBLK), bf16),
        pltpu.VMEM((DSET, FBLK), bf16),
        pltpu.VMEM((DSET, FBLK), bf16),
        pltpu.VMEM((DSET, FBLK), bf16),
        pltpu.VMEM((6, upper, 2 * FBLK), bf16),
        pltpu.VMEM((2, upper, 2 * FBLK), bf16),
        pltpu.VMEM((4, upper, 2 * FBLK), bf16),
        pltpu.VMEM((2, upper, 2 * FBLK), f32),
        pltpu.VMEM((quarter, 2 * FBLK), f32),
        pltpu.VMEM((SIDE, quarter, FBLK), bf16),
        pltpu.VMEM((SIDE, SIDE - 1, quarter, DBLK), bf16),
        pltpu.VMEM((SIDE, quarter, DBLK), f32),
        pltpu.VMEM((SIDE, SIDE - 1, quarter, DBLK), bf16),
        pltpu.VMEM((keep, DBLK), bf16),
        pltpu.VMEM((PIECES, CAP, DBLK), bf16),
        dma((3, SIDE)),
        dma((SIDE, 3)), dma((SIDE, 3)),
        dma((6,)), dma((6,)),
        dma((6,)), dma((6,)),
        dma((SIDE, 3)), dma((SIDE, 3)),
        dma((1,)), dma((1,)),
        dma((1,)), dma((1,)),
        pltpu.VMEM((CAP, DBLK), bf16),
    ]
    anywhere, in_vmem = pl.BlockSpec(memory_space=pl.ANY), pl.BlockSpec(memory_space=pltpu.VMEM)
    return pl.pallas_call(
        functools.partial(moe_kernel, keep),
        out_shape=jax.ShapeDtypeStruct((8, CAP, 8 * DBLK), bf16),
        in_specs=[in_vmem] + [anywhere] * 10 + [in_vmem] * len(places),
        out_specs=anywhere,
        scratch_shapes=scratch,
        compiler_params=pltpu.CompilerParams(
            collective_id=keep // 64, has_side_effects=True, vmem_limit_bytes=60 * 1024 * 1024
        ),
        cost_estimate=pl.CostEstimate(
            flops=13 * 10**6 * keep, bytes_accessed=14 * 10**6, transcendentals=10**6
        ),
        name="expert_layer",
    )(landed, w_gate, w_up, w_down, *moved, *places)


def attend_kernel(lengths, queries, token_key_value, cache, attended):
    step = pl.program_id(0)
    share = QUERY_HEADS // KEY_VALUE_HEADS
    heads = queries.shape[1]
    width = cache.shape[3]
    score_scale = HEAD_SIZE ** (-0.5)
    head = lax.broadcasted_iota(jnp.int32, (heads, width), 0)
    column = lax.broadcasted_iota(jnp.int32, (heads, width), 1)
    matches = lax.div(head, share) == lax.div(column, HEAD_SIZE)
    position = lax.broadcasted_iota(jnp.int32, (heads, cache.shape[2]), 1)

    def own_part(wide):
        wide = jnp.where(matches, wide, 0.0)
        return sum(wide[:, k * HEAD_SIZE : (k + 1) * HEAD_SIZE] for k in range(width // HEAD_SIZE))

    for i in range(SEQS):
        query = queries[i].astype(jnp.float32)
        query = jnp.where(matches, jnp.concatenate([query] * (width // HEAD_SIZE), axis=1), 0.0)
        new = token_key_value[i].astype(jnp.float32)
        scores = lax.dot_general(
            query.astype(jnp.bfloat16), cache[i, 0], (((1,), (1,)), ((), ())), preferred_element_type=jnp.float32
        )
        scores = jnp.where(position < lengths[step * SEQS + i], scores * score_scale, -jnp.inf)
        self_score = jnp.sum(query * new[0:1, :], axis=1, keepdims=True) * score_scale
        highest = jnp.maximum(jnp.max(scores, axis=1, keepdims=True), self_score)
        exponent = jnp.exp(scores - highest)
        own_exp = jnp.exp(self_score - highest)
        totals = jnp.sum(exponent, axis=1, keepdims=True) + own_exp
        normalized = (exponent / totals).astype(jnp.bfloat16)
        own_weight = (own_exp / totals).astype(jnp.bfloat16).astype(jnp.float32)
        mixture = jnp.dot(normalized, cache[i, 1], preferred_element_type=jnp.float32)
        mixture = own_part(mixture) + own_weight * own_part(jnp.broadcast_to(new[1:2, :], (heads, width)))
        attended[i] = mixture.astype(jnp.bfloat16)


def attend_local(queries, token_key_value, cache, cache_length):
    seq_count, _, positions, width = cache.shape
    heads = queries.shape[1] // HEAD_SIZE
    attended = pl.pallas_call(
        attend_kernel,
        out_shape=jax.ShapeDtypeStruct((seq_count, heads, HEAD_SIZE), jnp.bfloat16),
        grid_spec=pltpu.PrefetchScalarGridSpec(
            num_scalar_prefetch=1,
            grid=(seq_count // SEQS,),
            in_specs=[
                pl.BlockSpec((SEQS, heads, HEAD_SIZE), lambda i, _: (i, 0, 0)),
                pl.BlockSpec((SEQS, 2, width), lambda i, _: (i, 0, 0)),
                pl.BlockSpec((SEQS, 2, positions, width), lambda i, _: (i, 0, 0, 0)),
            ],
            out_specs=pl.BlockSpec((SEQS, heads, HEAD_SIZE), lambda i, _: (i, 0, 0)),
        ),
        cost_estimate=pl.CostEstimate(
            flops=4 * seq_count * heads * positions * width,
            bytes_accessed=2 * cache.size,
            transcendentals=seq_count * heads * positions,
        ),
        name="attention",
    )(cache_length, queries.reshape(seq_count, heads, HEAD_SIZE), token_key_value, cache)
    return attended.reshape(seq_count, heads * HEAD_SIZE)


def per_device(
    residual,
    queries,
    token_key_value,
    cache,
    cache_length,
    active,
    routes,
    norm_gain,
    router,
    w_gate,
    w_up,
    w_down,
):
    seq_count = residual.shape[0]
    expert_count = router.shape[1]
    slot_total = CAP * expert_count
    still_live = active == 1
    flat_expert = routes.reshape(-1)
    flat_live = jnp.repeat(still_live, 2)
    onehot = (
        (flat_expert[:, None] == jnp.arange(expert_count, dtype=jnp.int32)[None, :])
        & flat_live[:, None]
    ).astype(jnp.int32)
    before = jnp.cumsum(onehot, axis=0) - onehot
    rank_order = jnp.sum(before * onehot, axis=1)
    slot_index = flat_expert * CAP + rank_order
    w_gate, w_up, w_down = w_gate[0], w_up[0], w_down[0]
    line_rank = coordinates()[0]
    moved = []
    for weight in (w_gate, w_up):
        for step in range(1, SIDE):
            column = lax.rem(line_rank + step, SIDE) * FBLK
            piece = lax.dynamic_slice(weight, (0, column), (DBLK, FBLK))
            moved.append(lax.ppermute(piece, MESH_AXES, line_permutation(step)))
    attention_output = attend_local(queries, token_key_value, cache, cache_length)
    state = residual.astype(jnp.float32) + attention_output.astype(jnp.float32)
    scaled = state * norm_gain.astype(jnp.float32)[None, :]
    squares = jnp.sum(state * state, axis=1)
    raw_logits = jnp.dot(scaled, router.astype(jnp.float32), precision=lax.Precision.HIGHEST)
    selector = (
        (
            (slot_index[:, None] == jnp.arange(slot_total, dtype=jnp.int32)[None, :])
            & flat_live[:, None]
        )
        .astype(jnp.bfloat16)
        .reshape(seq_count, 2, slot_total)
    )
    senders = selector[:, 0] + selector[:, 1]
    outgoing = lax.dot_general(
        senders, scaled.astype(jnp.bfloat16), (((0,), (0,)), ((), ())), preferred_element_type=jnp.float32
    )
    outgoing = outgoing.astype(jnp.bfloat16).reshape(expert_count, CAP, residual.shape[1])
    slot_squares = jnp.sum(senders.astype(jnp.float32) * squares[:, None], axis=0).reshape(expert_count, CAP)
    counts = jnp.broadcast_to(jnp.sum(onehot, axis=0).astype(jnp.float32), (expert_count, expert_count))
    notes = jnp.concatenate([slot_squares, counts, jnp.zeros((expert_count, 128 - CAP - 8), jnp.float32)], axis=1)
    own_half = jnp.concatenate(
        [raw_logits, squares[:, None], jnp.zeros((seq_count, 128 - expert_count - 1), jnp.float32)], axis=1
    )
    lane = jnp.arange(128, dtype=jnp.int32)[None, :]
    picks = (routes[:, :1] == lane).astype(jnp.float32) - (routes[:, 1:] == lane).astype(jnp.float32)
    landed, at_row, at_column, choice, down_moved, weight_first = dispatch(
        outgoing, notes.reshape(expert_count, 1, 128), own_half, picks, w_down
    )
    weight_second = 1.0 - weight_first
    branches = [
        functools.partial(lambda keep, views, *args: expert_layer(keep, *args, views[: 2 * (keep < ALL_ROWS)]), keep)
        for keep in SIZES
    ]
    returned = lax.switch(
        choice[0, 0], branches, (at_row, at_column), landed, w_gate, w_up, w_down, (*moved, down_moved)
    )
    returned = returned.reshape(slot_total, residual.shape[1])
    pick_first = jnp.dot(selector[:, 0], returned, preferred_element_type=jnp.float32)
    pick_second = jnp.dot(selector[:, 1], returned, preferred_element_type=jnp.float32)
    moe_sum = weight_first * pick_first + weight_second * pick_second
    delta = jnp.where(still_live[:, None], attention_output.astype(jnp.float32) + moe_sum, 0.0)
    return delta.astype(jnp.bfloat16)


def solution(mesh):
    in_specs = (
        P(("grp", "ep"), "tp"),
        P(("grp", "ep"), "tp"),
        P(("grp", "ep"), None, "tp"),
        P(("grp", "ep"), None, None, "tp"),
        P(("grp", "ep")),
        P(("grp", "ep")),
        P(("grp", "ep"), None),
        P("tp"),
        P("tp", None),
        P("ep", ("grp", "tp"), None),
        P("ep", ("grp", "tp"), None),
        P("ep", ("grp", "tp"), None),
    )
    out_specs = P(("grp", "ep"), "tp")
    return jax.shard_map(
        per_device, mesh=mesh, in_specs=in_specs, out_specs=out_specs, check_vma=False
    )
```

```python
import functools

import jax
import jax.numpy as jnp
from jax import lax
from jax.experimental import pallas as pl
from jax.experimental.pallas import tpu as pltpu
from jax.sharding import PartitionSpec as P

MODEL_WIDTH = 4096
QUERY_HEADS = 32
KEY_VALUE_HEADS = 8
HEAD_SIZE = 128


EPSILON = 1e-05

SIDE = 4
DEVICES = 128
CAP = 16
PIECES = 64
ALL_ROWS = PIECES * CAP
CHUNK = 128
SEQS = 4
SIZES = (512, 576, 704, ALL_ROWS)
DBLK = 256
DSET = SIDE * DBLK
FBLK = 2048
FT = 512
WIDE_FT = 1024
MESH_AXES = ("grp", "ep", "tp")
MESH_ID = pl.DeviceIdType.MESH


def line_permutation(step):
    pairs = []
    for grp in range(8):
        for ep in range(8):
            for tp in range(2):
                x, z = grp % 4, (grp // 4) * 2 + tp
                if ep % 2 == 0:
                    x2, z2 = (x + step) % SIDE, z
                else:
                    x2, z2 = x, (z + step) % SIDE
                pairs.append(((grp * 8 + ep) * 2 + tp, (((z2 // 2) * 4 + x2) * 8 + ep) * 2 + z2 % 2))
    return pairs


def coordinates():
    grp, ep, tp = (lax.axis_index(name) for name in MESH_AXES)
    x = lax.rem(grp, 4)
    z = lax.div(grp, 4) * 2 + tp
    core = lax.rem(ep, 2)
    return x + (z - x) * core, z + (x - z) * core, core, ep


def parts_of(keep):
    quarter = keep // SIDE
    upper = (quarter + 31) // 32 * 16
    return quarter, upper, quarter - upper


def peer_of(a, b, core, ep):
    x = a + (b - a) * core
    z = b + (a - b) * core
    return (lax.div(z, 2) * 4 + x, ep, lax.rem(z, 2))


def greet_all():
    itself = own_id()
    barrier = pltpu.get_barrier_semaphore()

    @pl.loop(1, DEVICES)
    def _(step):
        at = lax.rem(itself + step, DEVICES)
        to = (lax.div(at, 16), lax.rem(lax.div(at, 2), 8), lax.rem(at, 2))
        pl.semaphore_signal(barrier, inc=1, device_id=to, device_id_type=MESH_ID)

    return lambda: pl.semaphore_wait(barrier, DEVICES - 1)


def own_id():
    grp, ep, tp = (lax.axis_index(name) for name in MESH_AXES)
    return (grp * 8 + ep) * 2 + tp


def remote(src, dst, ssem, rsem, to):
    return pltpu.make_async_remote_copy(
        src_ref=src, dst_ref=dst, send_sem=ssem, recv_sem=rsem, device_id=to, device_id_type=MESH_ID
    )


def deliver(count, src_of, dst_of, to_of, sends, recvs, spare):
    itself = own_id()

    @pl.loop(0, count)
    def _(step):
        to = to_of(step)
        far = (to[0] * 8 + to[1]) * 2 + to[2] != itself

        @pl.when(far)
        def _():
            remote(src_of(step), dst_of(step), sends.at[0], recvs.at[0], to).start()

        @pl.when(jnp.logical_not(far))
        def _():
            pltpu.make_async_copy(src_of(step), dst_of(step), recvs.at[0]).start()
            pltpu.make_async_copy(src_of(step), spare, sends.at[0]).start()


def dispatch_kernel(
    x_in, notes, halves, picks, w_down, landed, at_row, at_column, choice, moved, weight_first,
    other_half, arrived, table, x_send, x_recv, c_send, c_recv, d_send, d_recv, h_send, h_recv, spare, c_spare,
):
    grp, ep, tp = (lax.axis_index(name) for name in MESH_AXES)
    source = grp * 8 + ep
    own_block = lax.rem(grp, 4) * 2 + tp
    greet_all()()

    half_copy = remote(halves, other_half, h_send.at[0], h_recv.at[0], (grp, ep, 1 - tp))
    half_copy.start()

    def notes_to(step):
        at = lax.rem(own_id() + step, DEVICES)
        return (lax.div(at, 16), lax.rem(lax.div(at, 2), 8), lax.rem(at, 2))

    deliver(
        DEVICES, lambda step: notes.at[notes_to(step)[1]], lambda step: table.at[source * 2 + tp], notes_to,
        c_send, c_recv, c_spare,
    )

    def expert_of(step):
        return lax.rem(ep + lax.div(step, 8), 8)

    def block_of(step):
        return lax.rem(own_block + step, 8)

    deliver(
        PIECES,
        lambda step: x_in.at[expert_of(step), :, pl.ds(pl.multiple_of(block_of(step) * DBLK, DBLK), DBLK)],
        lambda step: arrived.at[source],
        lambda step: (tp * 4 + lax.div(block_of(step), 2), expert_of(step), lax.rem(block_of(step), 2)),
        x_send, x_recv, spare,
    )

    a, b, core, _ = coordinates()
    weights = []
    for index, step in enumerate((1, 3)):
        at = lax.rem(a + step, SIDE)
        copy = remote(
            w_down.at[:, pl.ds(pl.multiple_of(at * FBLK, FBLK), FBLK)], moved.at[index],
            d_send.at[index], d_recv.at[index], peer_of(at, b, core, ep),
        )
        copy.start()
        weights.append(copy)
    pltpu.make_async_copy(table, table, c_send.at[0]).wait()
    pltpu.make_async_copy(table, table, c_recv.at[0]).wait()

    both = table[...].reshape(PIECES, 2, 128)
    both = both[:, 0, :] + both[:, 1, :]
    lane = lax.broadcasted_iota(jnp.int32, (PIECES, 128), 1)
    counts = jnp.where((lane >= CAP) & (lane < CAP + 8), both * 0.5, 0.0)
    largest = jnp.max(jnp.sum(counts, axis=0, keepdims=True), axis=1, keepdims=True)
    choice[...] = sum((largest > keep).astype(jnp.int32) for keep in SIZES[:-1])
    here = jnp.sum(jnp.where(lane == CAP + ep, counts, 0.0), axis=1, keepdims=True)
    up = lax.broadcasted_iota(jnp.int32, (PIECES, PIECES), 0)
    along = lax.broadcasted_iota(jnp.int32, (PIECES, PIECES), 1)
    here_row = jnp.sum(jnp.where(up == along, here, 0.0), axis=0, keepdims=True)
    start = jnp.sum(jnp.where(along < up, here_row, 0.0), axis=1, keepdims=True)
    start_row = jnp.sum(jnp.where(up < along, here, 0.0), axis=0, keepdims=True)

    spot = lax.broadcasted_iota(jnp.int32, (PIECES, ALL_ROWS), 1)
    inside = lax.div(spot, CAP) == lax.broadcasted_iota(jnp.int32, (PIECES, ALL_ROWS), 0)
    place = lax.rem(spot, CAP).astype(jnp.float32)
    value = jnp.where(inside & (place < here), start + place + 1.0, 0.0)
    at_row[...] = jnp.sum(value, axis=0, keepdims=True).astype(jnp.int32) - 1

    spot = lax.broadcasted_iota(jnp.int32, (ALL_ROWS, PIECES), 0)
    inside = lax.div(spot, CAP) == lax.broadcasted_iota(jnp.int32, (ALL_ROWS, PIECES), 1)
    place = lax.rem(spot, CAP).astype(jnp.float32)
    value = jnp.where(inside & (place < here_row), start_row + place + 1.0, 0.0)
    at_column[...] = jnp.sum(value, axis=1, keepdims=True).astype(jnp.int32) - 1

    squares = jnp.dot(
        jnp.where(inside, 1.0, 0.0), both, preferred_element_type=jnp.float32, precision=lax.Precision.HIGHEST
    )
    spot = lax.broadcasted_iota(jnp.int32, (ALL_ROWS, 128), 0)
    chosen = lax.rem(spot, CAP) == lax.broadcasted_iota(jnp.int32, (ALL_ROWS, 128), 1)
    squares = jnp.sum(jnp.where(chosen, squares, 0.0), axis=1, keepdims=True)
    row_scale = jnp.sqrt(squares / MODEL_WIDTH + EPSILON)

    half_copy.wait()
    both = halves[...] + other_half[...]
    lane = lax.broadcasted_iota(jnp.int32, both.shape, 1)
    scale = jnp.sum(jnp.where(lane == 8, both, 0.0), axis=1, keepdims=True)
    scale = jnp.sqrt(scale / MODEL_WIDTH + EPSILON)
    difference = jnp.sum(picks[...] * (both / scale), axis=1, keepdims=True)
    weight_first[...] = 1.0 / (1.0 + jnp.exp(-difference))

    pltpu.make_async_copy(x_in, x_in, x_send.at[0]).wait()
    pltpu.make_async_copy(arrived, arrived, x_recv.at[0]).wait()
    pieces = CHUNK // CAP
    for chunk in range(ALL_ROWS // CHUNK):
        part = arrived[chunk * pieces : (chunk + 1) * pieces].reshape(CHUNK, DBLK).astype(jnp.float32)
        part = part / row_scale[chunk * CHUNK : (chunk + 1) * CHUNK]
        landed[chunk * pieces : (chunk + 1) * pieces] = part.astype(jnp.bfloat16).reshape(pieces, CAP, DBLK)
    for copy in weights:
        copy.wait()


def dispatch(x_in, notes, halves, picks, w_down):
    in_vmem, anywhere = pl.BlockSpec(memory_space=pltpu.VMEM), pl.BlockSpec(memory_space=pl.ANY)
    dma = pltpu.SemaphoreType.DMA
    return pl.pallas_call(
        dispatch_kernel,
        out_shape=(
            jax.ShapeDtypeStruct((PIECES, CAP, DBLK), jnp.bfloat16),
            jax.ShapeDtypeStruct((1, ALL_ROWS), jnp.int32),
            jax.ShapeDtypeStruct((ALL_ROWS, 1), jnp.int32),
            jax.ShapeDtypeStruct((1, 1), jnp.int32),
            jax.ShapeDtypeStruct((2, DBLK, FBLK), jnp.bfloat16),
            jax.ShapeDtypeStruct((halves.shape[0], 1), jnp.float32),
        ),
        in_specs=[anywhere, in_vmem, in_vmem, in_vmem, anywhere],
        out_specs=(in_vmem,) * 4 + (anywhere, in_vmem),
        scratch_shapes=[
            pltpu.VMEM(halves.shape, jnp.float32),
            pltpu.VMEM((PIECES, CAP, DBLK), jnp.bfloat16),
            pltpu.VMEM((2 * PIECES, 1, 128), jnp.float32),
            dma((1,)), dma((1,)), dma((1,)), dma((1,)), dma((2,)), dma((2,)), dma((1,)), dma((1,)),
            pltpu.VMEM((CAP, DBLK), jnp.bfloat16),
            pltpu.VMEM((1, 128), jnp.float32),
        ],
        compiler_params=pltpu.CompilerParams(collective_id=1, has_side_effects=True),
        name="dispatch",
    )(x_in, notes, halves, picks, w_down)


def moe_kernel(
    keep, landed, w_gate, w_up, w_down, g1, g2, g3, u1, u2, u3, d13, *refs
):
    if keep < ALL_ROWS:
        at_row, at_column, *refs = refs
    (
        y_out, rows, wg, wu, wd, send, fwd, got, raw, own, hid, part, part32, part_in, total, y_send,
        w_sem, xa_send, xa_recv, rs_send, rs_recv, ag_send, ag_recv,
        o_send, o_recv, y_ssem, y_rsem, d_send, d_recv, spare,
    ) = refs
    quarter, upper, lower = parts_of(keep)
    a, b, core, ep = coordinates()
    grp, tp = lax.axis_index("grp"), lax.axis_index("tp")
    z_hi = lax.div(grp, 4)
    own_block = lax.rem(grp, 4) * 2 + tp

    def peer(at_a, at_b):
        return peer_of(at_a, at_b, core, ep)

    def shifted(value, by):
        return lax.rem(value + by + SIDE, SIDE)

    right, left, across = shifted(b, 1), shifted(b, -1), shifted(b, 2)

    loads = []
    for which, (full, parts, dst) in enumerate(
        (
            (w_gate, ((1, g1), (2, g2), (3, g3)), wg),
            (w_up, ((1, u1), (2, u2), (3, u3)), wu),
            (w_down, ((1, d13.at[0]), (3, d13.at[1])), wd),
        )
    ):
        own_part = full.at[:, pl.ds(pl.multiple_of(a * FBLK, FBLK), FBLK)]
        for step, src in ((0, own_part), *parts):
            row = pl.ds(pl.multiple_of(shifted(a, -step) * DBLK, DBLK), DBLK)
            copy = pltpu.make_async_copy(src, dst.at[row], w_sem.at[which, step])
            copy.start()
            loads.append(copy)

    wait_for_all = greet_all()

    if keep < ALL_ROWS:
        @pl.loop(0, SIDE)
        def _(chunk):
            first = pl.multiple_of(chunk * quarter, 16)
            place = lax.broadcasted_iota(jnp.int32, (quarter, ALL_ROWS), 0) + first
            pick = jnp.where(place == at_row[...], 1.0, 0.0).astype(jnp.bfloat16)
            packed = jnp.dot(pick, landed[...].reshape(ALL_ROWS, DBLK), preferred_element_type=jnp.float32)
            rows[a, pl.ds(first, quarter), :] = packed.astype(jnp.bfloat16)
    else:
        rows[a] = landed[...].reshape(ALL_ROWS, DBLK)

    wait_for_all()

    turns = (across, right, left, b)
    copies = {}
    for turn, group in enumerate(turns):
        piece = pl.ds(pl.multiple_of(group * quarter, 16), quarter)
        for step in (2, 1, 3):
            copy = remote(
                rows.at[a, piece], rows.at[a, piece],
                xa_send.at[turn, step - 1], xa_recv.at[turn, step - 1], peer(shifted(a, step), b),
            )
            copy.start()
            copies[turn, step] = copy
    at = shifted(a, 2)
    copy = remote(
        w_down.at[:, pl.ds(pl.multiple_of(at * FBLK, FBLK), FBLK)],
        wd.at[pl.ds(pl.multiple_of(a * DBLK, DBLK), DBLK)],
        d_send.at[0], d_recv.at[0], peer(at, b),
    )
    copy.start()
    loads.append(copy)
    for copy in loads[: 2 * SIDE]:
        copy.wait()

    def product(turn, store):
        group = turns[turn]
        for step in range(1, SIDE):
            copies[turn, step].wait()
        first = pl.multiple_of(group * quarter, 16)

        @pl.loop(0, FBLK // WIDE_FT)
        def _(tile):
            lhs = jnp.concatenate([rows[k, pl.ds(first, quarter), :] for k in range(SIDE)], axis=1)
            for part_index, weight in enumerate((wg, wu)):
                cols = pl.ds(pl.multiple_of(tile * WIDE_FT, WIDE_FT), WIDE_FT)
                to = pl.ds(pl.multiple_of(tile * WIDE_FT + part_index * FBLK, WIDE_FT), WIDE_FT)
                value = jnp.dot(lhs, weight[:, cols], preferred_element_type=jnp.float32)
                store(to, value[:upper], value[upper:])

    def store_across(to, top, bottom):
        send[0, :, to] = top.astype(jnp.bfloat16)
        send[1, :lower, to] = bottom.astype(jnp.bfloat16)

    def store_right(to, top, bottom):
        raw[0, :, to] = top
        send[2, :lower, to] = bottom.astype(jnp.bfloat16)

    def store_left(to, top, bottom):
        send[3, :, to] = top.astype(jnp.bfloat16)
        raw[1, :lower, to] = bottom

    def store_own(to, top, bottom):
        own[:upper, to] = top
        own[upper:, to] = bottom

    def add_arrived(slot, which, count):
        @pl.loop(0, 2 * FBLK // FT)
        def _(tile):
            to = pl.ds(pl.multiple_of(tile * FT, FT), FT)
            value = raw[which, :count, to] + fwd[which, :count, to].astype(jnp.float32)
            send[slot, :count, to] = value.astype(jnp.bfloat16)

    def pass_on(slot, count, dst, to):
        copy = remote(send.at[slot, pl.ds(0, count)], dst.at[pl.ds(0, count)], rs_send.at[slot], rs_recv.at[slot], to)
        copy.start()
        return copy

    to_right, to_left = peer(a, right), peer(a, left)
    product(0, store_across)
    over_right = pass_on(0, upper, fwd.at[0], to_right)
    over_left = pass_on(1, lower, fwd.at[1], to_left)
    product(1, store_right)
    plain_right = pass_on(2, lower, got.at[1], to_right)
    product(2, store_left)
    plain_left = pass_on(3, upper, got.at[2], to_left)
    product(3, store_own)
    over_right.wait()
    add_arrived(4, 0, upper)
    sum_right = pass_on(4, upper, got.at[0], to_right)
    over_left.wait()
    add_arrived(5, 1, lower)
    sum_left = pass_on(5, lower, got.at[3], to_left)

    def activate(half, begin, count):
        @pl.loop(0, FBLK // FT)
        def _(tile):
            def whole(which):
                return (
                    own[begin : begin + count, which]
                    + got[half, :count, which].astype(jnp.float32)
                    + got[2 + half, :count, which].astype(jnp.float32)
                )

            cols = pl.ds(pl.multiple_of(tile * FT, FT), FT)
            gate, up = whole(cols), whole(pl.ds(pl.multiple_of(tile * FT + FBLK, FT), FT))
            hid[b, begin : begin + count, cols] = (gate / (1.0 + jnp.exp(-gate)) * up).astype(jnp.bfloat16)

    def spread_half(index, owner, which, to):
        copy = remote(hid.at[owner, which], hid.at[owner, which], ag_send.at[index], ag_recv.at[index], to)
        copy.start()
        return copy

    top, bottom = pl.ds(0, upper), pl.ds(upper, lower)
    plain_right.wait()
    plain_left.wait()
    sum_right.wait()
    activate(0, 0, upper)
    top_right = spread_half(0, b, top, to_right)
    top_left = spread_half(1, b, top, to_left)
    sum_left.wait()
    activate(1, upper, lower)
    bottom_left = spread_half(3, b, bottom, to_left)
    bottom_right = spread_half(2, b, bottom, to_right)
    for copy in loads[2 * SIDE :]:
        copy.wait()

    o_copies = {}

    def down(order, group):
        lhs = hid[group]

        def block(step):
            cols = pl.ds(pl.multiple_of(lax.rem(a + step, SIDE) * DBLK, DBLK), DBLK)
            return lax.dot_general(lhs, wd[cols, :], (((1,), (1,)), ((), ())), preferred_element_type=jnp.float32)

        def send_block(step):
            return remote(
                part.at[order, step - 1], part_in.at[order, step - 1],
                o_send.at[order, step - 1], o_recv.at[order, step - 1], peer(shifted(a, step), b),
            )

        @pl.loop(0, SIDE - 1)
        def _(turn):
            step = lax.rem(turn + 1, SIDE - 1) + 1
            part[order, step - 1] = block(step).astype(jnp.bfloat16)
            send_block(step).start()

        for step in range(1, SIDE):
            o_copies[order, step] = send_block(step)
        part32[order] = block(0)

    def finish(order, group):
        value = part32[order]
        for step in range(1, SIDE):
            o_copies[order, step].wait()
            value = value + part_in[order, step - 1].astype(jnp.float32)
        total[pl.ds(pl.multiple_of(group * quarter, 16), quarter), :] = value.astype(jnp.bfloat16)

    down(0, b)
    top_right.wait()
    on_right = spread_half(4, left, top, to_right)
    bottom_left.wait()
    on_left = spread_half(5, right, bottom, to_left)
    top_left.wait()
    bottom_right.wait()
    down(1, left)
    down(3, right)
    finish(0, b)
    on_right.wait()
    on_left.wait()
    down(2, across)
    finish(1, left)
    finish(3, right)
    finish(2, across)

    if keep < ALL_ROWS:
        @pl.loop(0, ALL_ROWS // CHUNK)
        def _(chunk):
            place = lax.broadcasted_iota(jnp.int32, (CHUNK, keep), 1)
            at = at_column[pl.ds(pl.multiple_of(chunk * CHUNK, CHUNK), CHUNK), :]
            pick = jnp.where(place == at, 1.0, 0.0).astype(jnp.bfloat16)
            spread = jnp.dot(pick, total[...], preferred_element_type=jnp.float32)
            first = pl.multiple_of(chunk * (CHUNK // CAP), CHUNK // CAP)
            y_send[pl.ds(first, CHUNK // CAP)] = spread.astype(jnp.bfloat16).reshape(CHUNK // CAP, CAP, DBLK)
    else:
        y_send[...] = total[...].reshape(PIECES, CAP, DBLK)

    def source_of(step):
        return lax.rem(grp * 8 + ep + step, PIECES)

    deliver(
        PIECES,
        lambda step: y_send.at[source_of(step)],
        lambda step: y_out.at[ep, :, pl.ds(pl.multiple_of(own_block * DBLK, DBLK), DBLK)],
        lambda step: (lax.div(source_of(step), 8), lax.rem(source_of(step), 8), z_hi),
        y_ssem, y_rsem, spare,
    )
    pltpu.make_async_copy(y_send, y_send, y_ssem.at[0]).wait()
    pltpu.make_async_copy(y_out, y_out, y_rsem.at[0]).wait()


def expert_layer(keep, landed, w_gate, w_up, w_down, moved, places=()):
    bf16, f32 = jnp.bfloat16, jnp.float32
    dma = pltpu.SemaphoreType.DMA
    quarter, upper, _ = parts_of(keep)
    scratch = [
        pltpu.VMEM((SIDE, keep, DBLK), bf16),
        pltpu.VMEM((DSET, FBLK), bf16),
        pltpu.VMEM((DSET, FBLK), bf16),
        pltpu.VMEM((DSET, FBLK), bf16),
        pltpu.VMEM((6, upper, 2 * FBLK), bf16),
        pltpu.VMEM((2, upper, 2 * FBLK), bf16),
        pltpu.VMEM((4, upper, 2 * FBLK), bf16),
        pltpu.VMEM((2, upper, 2 * FBLK), f32),
        pltpu.VMEM((quarter, 2 * FBLK), f32),
        pltpu.VMEM((SIDE, quarter, FBLK), bf16),
        pltpu.VMEM((SIDE, SIDE - 1, quarter, DBLK), bf16),
        pltpu.VMEM((SIDE, quarter, DBLK), f32),
        pltpu.VMEM((SIDE, SIDE - 1, quarter, DBLK), bf16),
        pltpu.VMEM((keep, DBLK), bf16),
        pltpu.VMEM((PIECES, CAP, DBLK), bf16),
        dma((3, SIDE)),
        dma((SIDE, 3)), dma((SIDE, 3)),
        dma((6,)), dma((6,)),
        dma((6,)), dma((6,)),
        dma((SIDE, 3)), dma((SIDE, 3)),
        dma((1,)), dma((1,)),
        dma((1,)), dma((1,)),
        pltpu.VMEM((CAP, DBLK), bf16),
    ]
    anywhere, in_vmem = pl.BlockSpec(memory_space=pl.ANY), pl.BlockSpec(memory_space=pltpu.VMEM)
    return pl.pallas_call(
        functools.partial(moe_kernel, keep),
        out_shape=jax.ShapeDtypeStruct((8, CAP, 8 * DBLK), bf16),
        in_specs=[in_vmem] + [anywhere] * 10 + [in_vmem] * len(places),
        out_specs=anywhere,
        scratch_shapes=scratch,
        compiler_params=pltpu.CompilerParams(
            collective_id=keep // 64, has_side_effects=True, vmem_limit_bytes=60 * 1024 * 1024
        ),
        cost_estimate=pl.CostEstimate(
            flops=13 * 10**6 * keep, bytes_accessed=14 * 10**6, transcendentals=10**6
        ),
        name="expert_layer",
    )(landed, w_gate, w_up, w_down, *moved, *places)


def attend_kernel(lengths, queries, token_key_value, cache, attended):
    step = pl.program_id(0)
    share = QUERY_HEADS // KEY_VALUE_HEADS
    heads = queries.shape[1]
    width = cache.shape[3]
    score_scale = HEAD_SIZE ** (-0.5)
    head = lax.broadcasted_iota(jnp.int32, (heads, width), 0)
    column = lax.broadcasted_iota(jnp.int32, (heads, width), 1)
    matches = lax.div(head, share) == lax.div(column, HEAD_SIZE)
    position = lax.broadcasted_iota(jnp.int32, (heads, cache.shape[2]), 1)

    def own_part(wide):
        wide = jnp.where(matches, wide, 0.0)
        return sum(wide[:, k * HEAD_SIZE : (k + 1) * HEAD_SIZE] for k in range(width // HEAD_SIZE))

    for i in range(SEQS):
        query = queries[i].astype(jnp.float32)
        query = jnp.where(matches, jnp.concatenate([query] * (width // HEAD_SIZE), axis=1), 0.0)
        new = token_key_value[i].astype(jnp.float32)
        scores = lax.dot_general(
            query.astype(jnp.bfloat16), cache[i, 0], (((1,), (1,)), ((), ())), preferred_element_type=jnp.float32
        )
        scores = jnp.where(position < lengths[step * SEQS + i], scores * score_scale, -jnp.inf)
        self_score = jnp.sum(query * new[0:1, :], axis=1, keepdims=True) * score_scale
        highest = jnp.maximum(jnp.max(scores, axis=1, keepdims=True), self_score)
        exponent = jnp.exp(scores - highest)
        own_exp = jnp.exp(self_score - highest)
        totals = jnp.sum(exponent, axis=1, keepdims=True) + own_exp
        normalized = (exponent / totals).astype(jnp.bfloat16)
        own_weight = (own_exp / totals).astype(jnp.bfloat16).astype(jnp.float32)
        mixture = jnp.dot(normalized, cache[i, 1], preferred_element_type=jnp.float32)
        mixture = own_part(mixture) + own_weight * own_part(jnp.broadcast_to(new[1:2, :], (heads, width)))
        attended[i] = mixture.astype(jnp.bfloat16)


def attend_local(queries, token_key_value, cache, cache_length):
    seq_count, _, positions, width = cache.shape
    heads = queries.shape[1] // HEAD_SIZE
    attended = pl.pallas_call(
        attend_kernel,
        out_shape=jax.ShapeDtypeStruct((seq_count, heads, HEAD_SIZE), jnp.bfloat16),
        grid_spec=pltpu.PrefetchScalarGridSpec(
            num_scalar_prefetch=1,
            grid=(seq_count // SEQS,),
            in_specs=[
                pl.BlockSpec((SEQS, heads, HEAD_SIZE), lambda i, _: (i, 0, 0)),
                pl.BlockSpec((SEQS, 2, width), lambda i, _: (i, 0, 0)),
                pl.BlockSpec((SEQS, 2, positions, width), lambda i, _: (i, 0, 0, 0)),
            ],
            out_specs=pl.BlockSpec((SEQS, heads, HEAD_SIZE), lambda i, _: (i, 0, 0)),
        ),
        cost_estimate=pl.CostEstimate(
            flops=4 * seq_count * heads * positions * width,
            bytes_accessed=2 * cache.size,
            transcendentals=seq_count * heads * positions,
        ),
        name="attention",
    )(cache_length, queries.reshape(seq_count, heads, HEAD_SIZE), token_key_value, cache)
    return attended.reshape(seq_count, heads * HEAD_SIZE)


def per_device(
    residual,
    queries,
    token_key_value,
    cache,
    cache_length,
    active,
    routes,
    norm_gain,
    router,
    w_gate,
    w_up,
    w_down,
):
    seq_count = residual.shape[0]
    expert_count = router.shape[1]
    slot_total = CAP * expert_count
    still_live = active == 1
    flat_expert = routes.reshape(-1)
    flat_live = jnp.repeat(still_live, 2)
    onehot = (
        (flat_expert[:, None] == jnp.arange(expert_count, dtype=jnp.int32)[None, :])
        & flat_live[:, None]
    ).astype(jnp.int32)
    before = jnp.cumsum(onehot, axis=0) - onehot
    rank_order = jnp.sum(before * onehot, axis=1)
    slot_index = flat_expert * CAP + rank_order
    w_gate, w_up, w_down = w_gate[0], w_up[0], w_down[0]
    line_rank = coordinates()[0]
    moved = []
    for weight in (w_gate, w_up):
        for step in range(1, SIDE):
            column = lax.rem(line_rank + step, SIDE) * FBLK
            piece = lax.dynamic_slice(weight, (0, column), (DBLK, FBLK))
            moved.append(lax.ppermute(piece, MESH_AXES, line_permutation(step)))
    attention_output = attend_local(queries, token_key_value, cache, cache_length)
    state = residual.astype(jnp.float32) + attention_output.astype(jnp.float32)
    scaled = state * norm_gain.astype(jnp.float32)[None, :]
    squares = jnp.sum(state * state, axis=1)
    raw_logits = jnp.dot(scaled, router.astype(jnp.float32), precision=lax.Precision.HIGHEST)
    selector = (
        (
            (slot_index[:, None] == jnp.arange(slot_total, dtype=jnp.int32)[None, :])
            & flat_live[:, None]
        )
        .astype(jnp.bfloat16)
        .reshape(seq_count, 2, slot_total)
    )
    senders = selector[:, 0] + selector[:, 1]
    outgoing = lax.dot_general(
        senders, scaled.astype(jnp.bfloat16), (((0,), (0,)), ((), ())), preferred_element_type=jnp.float32
    )
    outgoing = outgoing.astype(jnp.bfloat16).reshape(expert_count, CAP, residual.shape[1])
    slot_squares = jnp.sum(senders.astype(jnp.float32) * squares[:, None], axis=0).reshape(expert_count, CAP)
    counts = jnp.broadcast_to(jnp.sum(onehot, axis=0).astype(jnp.float32), (expert_count, expert_count))
    notes = jnp.concatenate([slot_squares, counts, jnp.zeros((expert_count, 128 - CAP - 8), jnp.float32)], axis=1)
    own_half = jnp.concatenate(
        [raw_logits, squares[:, None], jnp.zeros((seq_count, 128 - expert_count - 1), jnp.float32)], axis=1
    )
    lane = jnp.arange(128, dtype=jnp.int32)[None, :]
    picks = (routes[:, :1] == lane).astype(jnp.float32) - (routes[:, 1:] == lane).astype(jnp.float32)
    landed, at_row, at_column, choice, down_moved, weight_first = dispatch(
        outgoing, notes.reshape(expert_count, 1, 128), own_half, picks, w_down
    )
    weight_second = 1.0 - weight_first
    branches = [
        functools.partial(lambda keep, views, *args: expert_layer(keep, *args, views[: 2 * (keep < ALL_ROWS)]), keep)
        for keep in SIZES
    ]
    returned = lax.switch(
        choice[0, 0], branches, (at_row, at_column), landed, w_gate, w_up, w_down, (*moved, down_moved)
    )
    returned = returned.reshape(slot_total, residual.shape[1])
    pick_first = jnp.dot(selector[:, 0], returned, preferred_element_type=jnp.float32)
    pick_second = jnp.dot(selector[:, 1], returned, preferred_element_type=jnp.float32)
    moe_sum = weight_first * pick_first + weight_second * pick_second
    delta = jnp.where(still_live[:, None], attention_output.astype(jnp.float32) + moe_sum, 0.0)
    return delta.astype(jnp.bfloat16)


def solution(mesh):
    in_specs = (
        P(("grp", "ep"), "tp"),
        P(("grp", "ep"), "tp"),
        P(("grp", "ep"), None, "tp"),
        P(("grp", "ep"), None, None, "tp"),
        P(("grp", "ep")),
        P(("grp", "ep")),
        P(("grp", "ep"), None),
        P("tp"),
        P("tp", None),
        P("ep", ("grp", "tp"), None),
        P("ep", ("grp", "tp"), None),
        P("ep", ("grp", "tp"), None),
    )
    out_specs = P(("grp", "ep"), "tp")
    return jax.shard_map(
        per_device, mesh=mesh, in_specs=in_specs, out_specs=out_specs, check_vma=False
    )
```
